256 devices in a mesh: seq: 16 (over z, core), section: 4 (over y), tp: 4 (over x).
Axes of the slice: x: 4, y: 4, z: 8, core: 2. Of those that a mesh axis runs over, the one named last changes fastest.
Arguments:
- h_in: bfloat16 [4, 4096, 3072], P('section', 'seq', 'tp'), may hold values from -32 to 32
- memory: bfloat16 [4, 4096, 3072], P('section', 'seq', 'tp'), may hold values from -32 to 32
- cotangent: bfloat16 [4, 4096, 3072], P('section', 'seq', 'tp'), may hold values from -6 to 6
- block_docs: int32 [4, 32], P('section', 'seq'), may hold values from 0 to 3, never falling along the last dimension, each value on 1 to 24 neighbouring positions
- w_query: bfloat16 [4, 3072, 1536], P('section', None, 'tp'), may hold values from -0.109375 to 0.109375
- w_out: bfloat16 [4, 1536, 3072], P('section', 'tp'), may hold values from -0.15625 to 0.15625
- self_key_value_weight: bfloat16 [3072, 2, 512], P(None, None, 'tp'), may hold values from -0.109375 to 0.109375
- cache_key_value_weight: bfloat16 [3072, 2, 512], P(None, None, 'tp'), may hold values from -0.109375 to 0.109375
Outputs:
- passed_forward: bfloat16 [4, 4096, 3072], P('section', 'seq', 'tp')
- grad_input: bfloat16 [4, 4096, 3072], P('section', 'seq', 'tp')
- grad_memory: bfloat16 [4, 4096, 3072], P('section', 'seq', 'tp')
- grad_w_query: float32 [4, 3072, 1536], P('section', 'seq', 'tp')
- grad_w_out: float32 [4, 1536, 3072], P('section', 'tp', 'seq')
- grad_w_self_kv: float32 [3072, 2, 512], P(('seq', 'section'), None, 'tp')
- grad_w_cache: float32 [3072, 2, 512], P(('seq', 'section'), None, 'tp')
The draws below stay inside these ranges and needn't reach their ends.
Inputs may be any that keep to these rules, and one draw needn't show every extreme that they name: block_docs[s, b] is the document of tokens b * 128 to b * 128 + 127 of section s; numbers never fall along a row, and in every row one document spans exactly 24 blocks.
All inputs are finite; a program needn't handle non-finite values.
Results may differ from the reference program's by a relative error of at most 0.02.
Values may be sent and summed in bfloat16 or wider, within the bound.
A program may use at most 128 MiB of HBM per device.

```python
import math
import jax
import jax.numpy as jnp
import numpy as np
from jax import lax

MODEL_DIM = 3072
QUERY_HEAD_COUNT = 12
KEY_VALUE_HEADS = 4
HEAD_DIM = 128
BLK = 128
WIN = 1024
DOCS = 4
SEQ = 4096
NBLK = 32
N_SECTION = 4
N_TP = 4


def draw_hidden_states(key, salt):
    base_key = jax.random.fold_in(key, salt)
    noise_key, row_key = jax.random.split(base_key)
    shape = (N_SECTION, SEQ, MODEL_DIM)
    place = jnp.arange(MODEL_DIM, dtype=jnp.float32) / max(MODEL_DIM - 1, 1)
    noise = jnp.clip(jax.random.normal(noise_key, shape, jnp.float32), -6.0, 6.0)
    feature_scale = jnp.exp(math.log(10.0) * place) / 4.0
    row_scale = jnp.exp(jax.random.uniform(row_key, (N_SECTION, SEQ, 1), jnp.float32, math.log(0.5), math.log(2.0)))
    return (noise * feature_scale[None, None, :] * row_scale).astype(jnp.bfloat16)


def draw_h_in(key, part):
    return draw_hidden_states(key, 11)


def draw_memory(key, part):
    return draw_hidden_states(key, 23)


def level_of(rng, extent, shards, smallest, largest):
    factor_of, own = 1.0, jax.random.fold_in(rng, 6)
    for position, parts in shards:
        heights = jnp.exp(jax.random.uniform(jax.random.fold_in(own, position), (parts,), jnp.float32, smallest / len(shards), largest / len(shards)))
        factor_of = factor_of * jnp.repeat(heights, extent[position] // parts).reshape([-1 if axis == position else 1 for axis in range(len(extent))])
    return factor_of


def length_profile(amount, total, limit, slope):
    loads = [(1 << 20) // math.isqrt(rank ** slope) + 1 for rank in range(2, amount + 1)]
    surplus, counts = total - limit - (amount - 1), [1] * (amount - 1)
    while surplus > 0:
        movable = [i for i in range(amount - 1) if counts[i] < limit]
        mass, remaining = sum([loads[i] for i in movable]), surplus
        for i in movable:
            addition = min(limit - counts[i], max(1, remaining * loads[i] // mass), surplus)
            counts[i] = counts[i] + addition
            surplus = surplus - addition
    return np.array([limit] + counts)


def ragged(own_key, number_of, total, limit, lean):
    if number_of == 2:
        one = jax.random.randint(own_key, (), max(1, total - limit), min(limit, total - 1) + 1)
        return jnp.stack([one, total - one])
    lengths = jnp.asarray(length_profile(number_of, total, limit, lean), jnp.int32)
    pairs = (number_of - 1) // 2
    giver, receiver = lengths[1:1 + 2 * pairs:2], lengths[2:2 + 2 * pairs:2]
    slack = jnp.minimum(giver - 1, limit - receiver)
    moved = jax.random.randint(jax.random.fold_in(own_key, 1), (pairs,), 0, 1 << 20) % (slack + 1)
    lengths = lengths.at[1:1 + 2 * pairs:2].set(giver - moved).at[2:2 + 2 * pairs:2].set(receiver + moved)
    return lengths[jax.random.permutation(jax.random.fold_in(own_key, 2), number_of)]


def centred(own_key, extent, width, limit, pieces=(), kind=jnp.bfloat16):
    values = jax.random.normal(own_key, extent, jnp.float32) * width
    if len(pieces) > 0:
        values = level_of(own_key, extent, pieces, -0.22, 0.18) * values
    return jnp.clip(values, min=-limit, max=limit).astype(kind)


def setup_inputs(seed: int = 0) -> dict:
    streams_of = jax.random.split(jax.random.key(seed), 9)
    return {
        "h_in": draw_h_in(jax.random.fold_in(streams_of[8], 71), 0),
        "memory": draw_memory(jax.random.fold_in(streams_of[8], 71), 0),
        "cotangent": centred(streams_of[2], (N_SECTION, SEQ, MODEL_DIM), 1.0, 6.0, ((0, 4), (1, 16), (2, 4))),
        "block_docs": jax.vmap(lambda own: jnp.searchsorted(jnp.cumsum(ragged(own, DOCS, NBLK, 3 * NBLK // 4, 1)), jnp.arange(NBLK), side="right"))(jax.random.split(streams_of[3], N_SECTION)).reshape((N_SECTION, NBLK)).astype(jnp.int32),
        "w_query": centred(streams_of[4], (N_SECTION, MODEL_DIM, QUERY_HEAD_COUNT * HEAD_DIM), MODEL_DIM ** -0.5, 0.109375, ((0, 4), (2, 4))),
        "w_out": centred(streams_of[5], (N_SECTION, QUERY_HEAD_COUNT * HEAD_DIM, MODEL_DIM), (QUERY_HEAD_COUNT * HEAD_DIM) ** -0.5, 0.15625, ((0, 4), (1, 4))),
        "self_key_value_weight": centred(streams_of[6], (MODEL_DIM, 2, KEY_VALUE_HEADS * HEAD_DIM), MODEL_DIM ** -0.5, 0.109375, ((2, 4),)),
        "cache_key_value_weight": centred(streams_of[7], (MODEL_DIM, 2, KEY_VALUE_HEADS * HEAD_DIM), MODEL_DIM ** -0.5, 0.109375, ((2, 4),)),
    }


score_scale = 40.0
norm_eps = 1e-06

def to_rounded(values):
    return lax.optimization_barrier(values.astype(jnp.bfloat16)).astype(jnp.float32)

def row_norm(values):
    wide_vals = values.astype(jnp.float32)
    factor = lax.rsqrt(lax.optimization_barrier(jnp.mean(wide_vals * wide_vals, axis=-1)) + norm_eps)
    return ((wide_vals * factor[:, None]).astype(jnp.bfloat16), factor)

def unit_rows(values):
    return values * lax.rsqrt(lax.optimization_barrier(jnp.sum(values * values, axis=-1, keepdims=True)) + norm_eps)

def visible(query_pos, query_doc, key_pos, key_doc, self_section):
    upper_bound = jnp.where(self_section, query_pos, query_pos // BLK * BLK + BLK - 1)
    lower_bound = jnp.where(self_section, query_pos - WIN, -1)
    same_doc = query_doc[:, None] == key_doc[None, :]
    return same_doc & (key_pos[None, :] <= upper_bound[:, None]) & (key_pos[None, :] > lower_bound[:, None])

def section_pass(self_section, hidden, source, grad_out, docs, query_projection_weight, out_weight, key_value_matrix):
    sequence_length_total = hidden.shape[0]
    hidden_model_width = hidden.shape[1]
    query_group_width = QUERY_HEAD_COUNT // KEY_VALUE_HEADS
    normalized_input, row_factor = row_norm(hidden)
    normalized_source, source_factor = row_norm(source)
    key_value_flattened = key_value_matrix.reshape(hidden_model_width, 2 * KEY_VALUE_HEADS * HEAD_DIM)
    query_matrix = jnp.dot(normalized_input, query_projection_weight, preferred_element_type=jnp.float32).reshape(sequence_length_total, KEY_VALUE_HEADS, query_group_width, HEAD_DIM)
    key_value_pairs = jnp.dot(normalized_source, key_value_flattened, preferred_element_type=jnp.float32).reshape(sequence_length_total, 2, KEY_VALUE_HEADS, HEAD_DIM)
    query_unit = unit_rows(query_matrix).astype(jnp.bfloat16)
    key_raw = key_value_pairs[:, 0]
    key_unit = unit_rows(key_raw).astype(jnp.bfloat16)
    value_bf = key_value_pairs[:, 1].astype(jnp.bfloat16)
    key_wide = key_unit.astype(jnp.float32)
    value_wide = value_bf.astype(jnp.float32)
    positions = jnp.arange(sequence_length_total, dtype=jnp.int32)
    doc_of = jnp.repeat(docs, BLK)
    span_len = math.gcd(sequence_length_total, 512)
    block_count = sequence_length_total // span_len

    def block_rows(values, block_index):
        return lax.dynamic_slice_in_dim(values, (block_index * span_len).astype(jnp.int32), span_len, 0)

    def block_scores(block_index):
        query_block = block_rows(query_unit, block_index).astype(jnp.float32)
        allowed = visible(block_rows(positions, block_index), block_rows(doc_of, block_index), positions, doc_of, self_section)
        scores = score_scale * jnp.einsum('tgjd,ugd->tgju', query_block, key_wide)
        return (query_block, allowed[:, None, None, :], scores)

    def forward_block(block_index):
        query_block, allowed, scores = block_scores(block_index)
        weights = jnp.where(allowed, jnp.exp(scores), 0.0)
        softmax_denominator = lax.optimization_barrier(jnp.sum(weights, axis=-1))
        numerator = jnp.einsum('tgju,ugd->tgjd', to_rounded(weights), value_wide)
        return (numerator / softmax_denominator[..., None], softmax_denominator)
    block_outputs, denominator_rows = lax.map(forward_block, jnp.arange(block_count, dtype=jnp.int32))
    attention_output = block_outputs.reshape(sequence_length_total, KEY_VALUE_HEADS, query_group_width, HEAD_DIM).astype(jnp.bfloat16)
    softmax_denominator = denominator_rows.reshape(sequence_length_total, KEY_VALUE_HEADS, query_group_width)
    attn_flat = attention_output.reshape(sequence_length_total, QUERY_HEAD_COUNT * HEAD_DIM)
    projected = jnp.dot(attn_flat, out_weight, preferred_element_type=jnp.float32)
    h_out = (hidden.astype(jnp.float32) + projected).astype(jnp.bfloat16)
    attention_gradient = lax.dot_general(grad_out, out_weight, (((1,), (1,)), ((), ())), preferred_element_type=jnp.float32)
    attention_gradient = attention_gradient.astype(jnp.bfloat16).reshape(sequence_length_total, KEY_VALUE_HEADS, query_group_width, HEAD_DIM)
    grad_attn_wide = attention_gradient.astype(jnp.float32)
    delta = lax.optimization_barrier(jnp.sum(grad_attn_wide * attention_output.astype(jnp.float32), axis=-1))

    def backward_block(running, block_index):
        grad_key, value_gradient = running
        query_block, allowed, scores = block_scores(block_index)
        grad_block = block_rows(grad_attn_wide, block_index)
        probs = jnp.where(allowed, jnp.exp(scores) / block_rows(softmax_denominator, block_index)[..., None], 0.0)
        grad_probs = jnp.einsum('tgjd,ugd->tgju', grad_block, value_wide)
        grad_scores = to_rounded(probs * (grad_probs - block_rows(delta, block_index)[..., None]))
        query_gradient = score_scale * jnp.einsum('tgju,ugd->tgjd', grad_scores, key_wide)
        grad_key = grad_key + score_scale * jnp.einsum('tgju,tgjd->ugd', grad_scores, query_block)
        value_gradient = value_gradient + jnp.einsum('tgju,tgjd->ugd', to_rounded(probs), grad_block)
        return ((grad_key, value_gradient), query_gradient)
    empty_gradients = jnp.zeros((sequence_length_total, KEY_VALUE_HEADS, HEAD_DIM), jnp.float32)
    (grad_key, value_gradient), query_gradient = lax.scan(backward_block, (empty_gradients, empty_gradients), jnp.arange(block_count, dtype=jnp.int32))
    query_gradient = query_gradient.reshape(sequence_length_total, KEY_VALUE_HEADS, query_group_width, HEAD_DIM)
    _, query_pull = jax.vjp(unit_rows, query_matrix)
    grad_queries = query_pull(query_gradient)[0].reshape(sequence_length_total, QUERY_HEAD_COUNT * HEAD_DIM).astype(jnp.bfloat16)
    _, key_pull = jax.vjp(unit_rows, key_raw)
    key_gradient_rows = key_pull(grad_key)[0]
    key_value_gradient = jnp.stack([key_gradient_rows, value_gradient], axis=1).reshape(sequence_length_total, 2, KEY_VALUE_HEADS * HEAD_DIM).astype(jnp.bfloat16)
    query_cols = QUERY_HEAD_COUNT * HEAD_DIM // N_TP
    key_value_columns = KEY_VALUE_HEADS * HEAD_DIM // N_TP
    back_rows = jnp.zeros((sequence_length_total, hidden_model_width), jnp.float32)
    back_source = jnp.zeros((sequence_length_total, hidden_model_width), jnp.float32)
    for tp_part in range(N_TP):
        query_first = tp_part * query_cols
        kv_first = tp_part * key_value_columns
        product = lax.dot_general(grad_queries[:, query_first:query_first + query_cols], query_projection_weight[:, query_first:query_first + query_cols], (((1,), (1,)), ((), ())), preferred_element_type=jnp.float32)
        back_rows = back_rows + to_rounded(product)
        grad_part = key_value_gradient[:, :, kv_first:kv_first + key_value_columns].reshape(sequence_length_total, 2 * key_value_columns)
        weight_part = key_value_matrix[:, :, kv_first:kv_first + key_value_columns].reshape(hidden_model_width, 2 * key_value_columns)
        product = lax.dot_general(grad_part, weight_part, (((1,), (1,)), ((), ())), preferred_element_type=jnp.float32)
        back_source = back_source + to_rounded(product)
    hidden_wide = hidden.astype(jnp.float32)
    source_wide = source.astype(jnp.float32)
    row_total = lax.optimization_barrier(jnp.sum(back_rows * hidden_wide, axis=1))
    source_total = lax.optimization_barrier(jnp.sum(back_source * source_wide, axis=1))
    row_cube = row_factor * row_factor * row_factor
    source_cube = source_factor * source_factor * source_factor
    grad_input = grad_out.astype(jnp.float32) + row_factor[:, None] * back_rows - hidden_wide * (row_cube * row_total / hidden_model_width)[:, None]
    grad_memory = source_factor[:, None] * back_source - source_wide * (source_cube * source_total / hidden_model_width)[:, None]
    grad_wq = lax.dot_general(normalized_input, grad_queries, (((0,), (0,)), ((), ())), preferred_element_type=jnp.float32)
    grad_wo = lax.dot_general(attn_flat, grad_out, (((0,), (0,)), ((), ())), preferred_element_type=jnp.float32)
    key_value_weight_gradient = lax.dot_general(normalized_source, key_value_gradient.reshape(sequence_length_total, 2 * KEY_VALUE_HEADS * HEAD_DIM), (((0,), (0,)), ((), ())), preferred_element_type=jnp.float32)
    key_value_weight_gradient = key_value_weight_gradient.reshape(hidden_model_width, 2, KEY_VALUE_HEADS * HEAD_DIM)
    return (h_out, grad_input.astype(jnp.bfloat16), grad_memory.astype(jnp.bfloat16), grad_wq, grad_wo, key_value_weight_gradient)

def reference(h_in, memory, cotangent, block_docs, w_query, w_out, self_key_value_weight, cache_key_value_weight):
    results = []
    for section_id in range(N_SECTION):
        if section_id == 0:
            source = h_in[0]
            key_value_matrix = self_key_value_weight
        else:
            source = memory[section_id]
            key_value_matrix = cache_key_value_weight
        results.append(section_pass(section_id == 0, h_in[section_id], source, cotangent[section_id], block_docs[section_id], w_query[section_id], w_out[section_id], key_value_matrix))
    outputs = jnp.stack([entry[0] for entry in results])
    passed_forward = jnp.roll(outputs, 1, axis=0)
    grad_input = jnp.stack([entry[1] for entry in results])
    grad_memory = jnp.stack([entry[2] for entry in results])
    grad_w_query = jnp.stack([entry[3] for entry in results])
    grad_w_out = jnp.stack([entry[4] for entry in results])
    grad_w_self_kv = results[0][5]
    grad_w_cache = results[1][5]
    for section_id in range(2, N_SECTION):
        grad_w_cache = grad_w_cache + results[section_id][5]
    return (passed_forward, grad_input, grad_memory, grad_w_query, grad_w_out, grad_w_self_kv, grad_w_cache)
```

```python
import functools
import math

import jax
import jax.numpy as jnp
from jax import lax
from jax.experimental import pallas as pl
from jax.experimental.pallas import tpu as pltpu
from jax.sharding import PartitionSpec as P

MESH = pl.DeviceIdType.MESH
HEAD_DIM = 128
BLK = 128
WIN = 1024
SCALE = 40.0
EPS = 1e-06
EXP2_SCALE = SCALE * math.log2(math.e)
F32 = jnp.float32
BF16 = jnp.bfloat16
DOC_ROWS = 16
VMEM_SPEC = pl.BlockSpec(memory_space=pltpu.VMEM)
ANY_SPEC = pl.BlockSpec(memory_space=pl.ANY)
SMEM_SPEC = pl.BlockSpec(memory_space=pltpu.SMEM)
VMEM_LIMIT = 60 * 1024 * 1024


def nt(left, right):
    return lax.dot_general(left, right, (((1,), (1,)), ((), ())), preferred_element_type=F32)


def nn(left, right):
    return lax.dot_general(left, right, (((1,), (0,)), ((), ())), preferred_element_type=F32)


def tn(left, right):
    return lax.dot_general(left, right, (((0,), (0,)), ((), ())), preferred_element_type=F32)


def remote(src, dst, send_sem, recv_sem, device):
    return pltpu.make_async_remote_copy(
        src_ref=src,
        dst_ref=dst,
        send_sem=send_sem,
        recv_sem=recv_sem,
        device_id=device,
        device_id_type=MESH,
    )


def greet(devices):
    barrier = pltpu.get_barrier_semaphore()
    for device in devices:
        pl.semaphore_signal(barrier, inc=1, device_id=device, device_id_type=MESH)
    pl.semaphore_wait(barrier, len(devices))


def run_together(*streams):
    live = list(streams)
    while live:
        for stream in list(live):
            try:
                next(stream)
            except StopIteration:
                live.remove(stream)


class Ring:
    def __init__(self, axis, count):
        self.axis = axis
        self.me = lax.axis_index(axis)
        self.count = count

    def at(self, step):
        return lax.rem(self.me + step + self.count, self.count)

    def device(self, step):
        return {self.axis: self.at(step)}


class Line:
    def __init__(self, count):
        self.me = lax.axis_index("seq")
        self.chips = count // 2
        self.chip = self.me // 2
        self.core = self.me - self.chip * 2
        self.other = 1 - self.core

    def chip_at(self, step):
        return lax.rem(self.chip + step + self.chips, self.chips)

    def index(self, step):
        return self.chip_at(step) * 2 + self.core

    def device(self, step):
        return {"seq": self.index(step)}

    def partner(self):
        return {"seq": self.chip * 2 + self.other}


def gather_four(ring, in_ref, out_ref, send, recv, local_sem):
    rows, width = in_ref.shape
    lo, hi = pl.ds(0, rows // 2), pl.ds(rows // 2, rows // 2)

    def cols(step):
        return pl.ds(pl.multiple_of(ring.at(step) * width, 128), width)

    def own(half, slot, step):
        return remote(
            in_ref.at[half, :], out_ref.at[half, cols(0)], send.at[slot], recv.at[slot], ring.device(step)
        )

    right_lo, left_hi = own(lo, 0, 1), own(hi, 1, -1)
    right_hi, left_lo = own(hi, 2, 1), own(lo, 3, -1)
    for copy in (right_lo, left_hi, right_hi, left_lo):
        copy.start()
    local = pltpu.make_async_copy(in_ref, out_ref.at[:, cols(0)], local_sem)
    local.start()
    yield
    right_lo.wait_recv()
    far_lo = out_ref.at[lo, cols(-1)]
    relay_right = remote(far_lo, far_lo, send.at[4], recv.at[4], ring.device(1))
    relay_right.start()
    left_hi.wait_recv()
    far_hi = out_ref.at[hi, cols(1)]
    relay_left = remote(far_hi, far_hi, send.at[5], recv.at[5], ring.device(-1))
    relay_left.start()
    yield
    for copy in (right_hi, left_lo, relay_right, relay_left):
        copy.wait_recv()
    local.wait()
    yield
    for copy in (right_lo, left_hi, right_hi, left_lo, relay_right, relay_left):
        copy.wait_send()


def gather_rows_kernel(count, src_ref, h_ref, cot_ref, src_out, h_out, cot_out, send, recv, local):
    ring = Ring("tp", count)
    greet([ring.device(1), ring.device(-1)])
    streams = [
        gather_four(ring, i, o, send.at[k], recv.at[k], local.at[k])
        for k, (i, o) in enumerate(((src_ref, src_out), (h_ref, h_out), (cot_ref, cot_out)))
    ]
    next(streams[0])
    for k in range(3):
        next(streams[k])
        if k < 2:
            next(streams[k + 1])
        next(streams[k])
    run_together(*streams)


def gather_rows(count, src, hidden, cot):
    rows, width = hidden.shape
    full = jax.ShapeDtypeStruct((rows, width * count), BF16)
    return pl.pallas_call(
        functools.partial(gather_rows_kernel, count),
        out_shape=(full, full, full),
        in_specs=[VMEM_SPEC] * 3,
        out_specs=[ANY_SPEC] * 3,
        scratch_shapes=[
            pltpu.SemaphoreType.DMA((3, 6)),
            pltpu.SemaphoreType.DMA((3, 6)),
            pltpu.SemaphoreType.DMA((3,)),
        ],
        compiler_params=pltpu.CompilerParams(collective_id=1, has_side_effects=True),
        name="gather_rows",
    )(src, hidden, cot)


def project_kernel(
    docs_ref, h_ref, src_ref, cot_ref, wq_ref, wo_ref, self_ref, cache_ref,
    q_ref, kv_ref, pay_ref, dout_ref, rh_ref, rs_ref,
    acc_q, acc_kv, acc_do, sum_h, sum_s,
):
    step = pl.program_id(0)
    steps = pl.num_programs(0)

    @pl.when(step == 0)
    def _():
        for ref in (acc_q, acc_kv, acc_do, sum_h, sum_s):
            ref[...] = jnp.zeros_like(ref)

    hidden, source = h_ref[...], src_ref[...]
    is_self = lax.axis_index("section") == 0
    weight = jnp.where(is_self, self_ref[...], cache_ref[...])
    acc_q[...] += nn(hidden, wq_ref[...])
    acc_kv[...] += nn(source, weight)
    acc_do[...] += nt(cot_ref[...], wo_ref[...])

    def squares(block):
        wide = block.astype(F32)
        wide = wide * wide
        parts = [wide[:, k : k + 128] for k in range(0, wide.shape[1], 128)]
        return functools.reduce(lambda a, b: a + b, parts)

    sum_h[...] += squares(hidden)
    sum_s[...] += squares(source)

    @pl.when(step == steps - 1)
    def _():
        width = h_ref.shape[1] * steps
        rh = lax.rsqrt(jnp.sum(sum_h[...], axis=1, keepdims=True) / width + EPS)
        rs = lax.rsqrt(jnp.sum(sum_s[...], axis=1, keepdims=True) / width + EPS)
        rh_ref[...] = jnp.broadcast_to(rh, rh_ref.shape)
        rs_ref[...] = jnp.broadcast_to(rs, rs_ref.shape)
        q_ref[...] = acc_q[...] * rh
        kv = acc_kv[...] * rs
        kv_ref[...] = kv
        key, value = kv[:, :HEAD_DIM], kv[:, HEAD_DIM:]
        unit = key * lax.rsqrt(jnp.sum(key * key, axis=1, keepdims=True) + EPS)
        rows = kv.shape[0]
        pay_ref[0:rows, 0:HEAD_DIM] = unit.astype(BF16)
        pay_ref[0:rows, HEAD_DIM:] = value.astype(BF16)
        lane = lax.broadcasted_iota(jnp.int32, (DOC_ROWS, 2 * BLK), 1)
        docs = jnp.where(lane < BLK, docs_ref[0, 0], docs_ref[0, 1])
        pay_ref[rows:, :] = docs.astype(F32).astype(BF16)
        dout_ref[...] = acc_do[...].astype(BF16)


def project(steps, docs, full_h, full_s, full_c, wq, wo, self_w, cache_w):
    rows, width = full_h.shape
    block = width // steps
    heads, kv = wq.shape[1], self_w.shape[1]
    by_col = pl.BlockSpec((rows, block), lambda i: (0, i))
    whole = lambda shape: pl.BlockSpec(shape, lambda i: (0, 0))
    return pl.pallas_call(
        project_kernel,
        grid=(steps,),
        out_shape=(
            jax.ShapeDtypeStruct((rows, heads), F32),
            jax.ShapeDtypeStruct((rows, kv), F32),
            jax.ShapeDtypeStruct((rows + DOC_ROWS, kv), BF16),
            jax.ShapeDtypeStruct((rows, heads), BF16),
            jax.ShapeDtypeStruct((rows, 128), F32),
            jax.ShapeDtypeStruct((rows, 128), F32),
        ),
        in_specs=[
            SMEM_SPEC, by_col, by_col, by_col,
            pl.BlockSpec((block, heads), lambda i: (i, 0)),
            pl.BlockSpec((heads, block), lambda i: (0, i)),
            pl.BlockSpec((block, kv), lambda i: (i, 0)),
            pl.BlockSpec((block, kv), lambda i: (i, 0)),
        ],
        out_specs=[
            whole((rows, heads)), whole((rows, kv)), whole((rows + DOC_ROWS, kv)),
            whole((rows, heads)), whole((rows, 128)), whole((rows, 128)),
        ],
        scratch_shapes=[
            pltpu.VMEM((rows, heads), F32), pltpu.VMEM((rows, kv), F32), pltpu.VMEM((rows, heads), F32),
            pltpu.VMEM((rows, 128), F32), pltpu.VMEM((rows, 128), F32),
        ],
        compiler_params=pltpu.CompilerParams(vmem_limit_bytes=VMEM_LIMIT),
        name="project",
    )(docs, full_h, full_s, full_c, wq, wo, self_w, cache_w)


def gather_keys_kernel(count, in_ref, out_ref, send, recv, to_core, from_core, local_sem):
    line = Line(count)
    rows = in_ref.shape[0]
    cut = (rows // 2 + 15) // 16 * 16
    halves = {1: pl.ds(0, cut), -1: pl.ds(cut, rows - cut)}
    greet([line.device(1), line.device(-1), line.partner()])
    copies = []

    def send_copy(src, dst, s, r, device):
        copy = remote(src, dst, s, r, device)
        copy.start()
        copies.append(copy)
        return copy

    last = line.chips // 2
    hops = {}
    for way, d in ((0, 1), (1, -1)):
        hops[way] = send_copy(
            in_ref, out_ref.at[line.me], send.at[way, 0], recv.at[way, 0], line.device(d)
        )
    passed = [
        send_copy(in_ref, out_ref.at[line.me], to_core.at[0], from_core.at[0], line.partner())
    ]
    local = pltpu.make_async_copy(in_ref, out_ref.at[line.me], local_sem)
    local.start()
    slot = 1
    for hop in range(1, last + 1):
        for way, d in ((0, 1), (1, -1)):
            hops[way].wait_recv()
            block = line.index(-d * hop)
            if hop < last:
                ahead = out_ref.at[block]
                if hop == last - 1:
                    ahead = out_ref.at[block, halves[d], :]
                hops[way] = send_copy(
                    ahead, ahead, send.at[way, hop], recv.at[way, hop], line.device(d)
                )
                piece = out_ref.at[block]
            else:
                piece = out_ref.at[block, halves[d], :]
            passed.append(
                send_copy(piece, piece, to_core.at[slot], from_core.at[slot], line.partner())
            )
            slot += 1
    for copy in passed:
        copy.wait_recv()
    local.wait()
    for copy in copies:
        copy.wait_send()


def gather_keys(count, payload):
    last = count // 4
    return pl.pallas_call(
        functools.partial(gather_keys_kernel, count),
        out_shape=jax.ShapeDtypeStruct((count,) + payload.shape, BF16),
        in_specs=[VMEM_SPEC],
        out_specs=ANY_SPEC,
        scratch_shapes=[
            pltpu.SemaphoreType.DMA((2, last)),
            pltpu.SemaphoreType.DMA((2, last)),
            pltpu.SemaphoreType.DMA((2 * last + 1,)),
            pltpu.SemaphoreType.DMA((2 * last + 1,)),
            pltpu.SemaphoreType.DMA,
        ],
        compiler_params=pltpu.CompilerParams(collective_id=2, has_side_effects=True),
        name="gather_keys",
    )(payload)


def attend_kernel(
    docs_ref, q_ref, dout_ref, kv_ref, wo_ref,
    attn_ref, proj_ref, gq_ref, dot_ref, dkv_ref,
    q_unit, dout, weights, acc, dq,
):
    seq = lax.axis_index("seq")
    is_self = lax.axis_index("section") == 0
    rows = q_ref.shape[0]
    heads = q_ref.shape[1] // HEAD_DIM
    chunks = kv_ref.shape[0]
    low = jnp.where(is_self, jnp.maximum(seq - WIN // rows, 0), 0)

    def head_rows(head):
        return pl.ds(head * rows, rows)

    def head_cols(head):
        return pl.ds(head * HEAD_DIM, HEAD_DIM)

    for head in range(heads):
        q = q_ref[:, head_cols(head)]
        unit = q * lax.rsqrt(jnp.sum(q * q, axis=1, keepdims=True) + EPS)
        q_unit[head_rows(head), :] = unit.astype(BF16)
    acc[...] = jnp.zeros_like(acc)
    dq[...] = jnp.zeros_like(dq)
    zero_chunk = jnp.zeros((rows, 2 * HEAD_DIM), BF16)

    @pl.loop(0, low)
    def _(j):
        dkv_ref[j] = zero_chunk

    @pl.loop(seq + 1, chunks)
    def _(j):
        dkv_ref[j] = zero_chunk

    row = lax.broadcasted_iota(jnp.int32, (rows, 1), 0)
    lane = lax.broadcasted_iota(jnp.int32, (1, rows), 1)
    query_doc = jnp.where(row < BLK, docs_ref[0, 0], docs_ref[0, 1]).astype(F32)
    query_pos = seq * rows + row
    upper = jnp.where(is_self, query_pos, query_pos // BLK * BLK + BLK - 1)
    lower = jnp.where(is_self, query_pos - WIN, -1)
    ones = jnp.ones((rows, HEAD_DIM), BF16)

    @pl.loop(low, seq + 1)
    def _(j):
        key = kv_ref[j, 0:rows, 0:HEAD_DIM]
        value = jnp.concatenate([kv_ref[j, 0:rows, HEAD_DIM:], ones], axis=1)
        key_doc = kv_ref[j, rows:, :].astype(F32)[0:1, :]
        key_pos = j * rows + lane
        seen = (key_doc == query_doc) & (key_pos <= upper) & (key_pos > lower)
        for head in range(heads):
            score = nt(q_unit[head_rows(head), :], key)
            weight = jnp.where(seen, jnp.exp2(score * EXP2_SCALE), 0.0).astype(BF16)
            weights[j, head_rows(head), :] = weight
            acc[head_rows(head), :] += nn(weight, value)

    deltas = []
    for head in range(heads):
        total = acc[head_rows(head), :]
        inverse = 1.0 / total[:, HEAD_DIM:]
        out = (total[:, :HEAD_DIM] * inverse).astype(BF16)
        attn_ref[:, head_cols(head)] = out
        grad = dout_ref[:, head_cols(head)].astype(F32)
        delta = jnp.sum(grad * out.astype(F32), axis=1, keepdims=True)
        dout[head_rows(head), :] = (grad * inverse).astype(BF16)
        deltas.append(delta * inverse[:, 0:1])

    @pl.loop(low, seq + 1)
    def _(j):
        key = kv_ref[j, 0:rows, 0:HEAD_DIM]
        value = kv_ref[j, 0:rows, HEAD_DIM:]
        grad_key = jnp.zeros((rows, HEAD_DIM), F32)
        grad_value = jnp.zeros((rows, HEAD_DIM), F32)
        for head in range(heads):
            weight = weights[j, head_rows(head), :]
            grad = dout[head_rows(head), :]
            grad_prob = nt(grad, value)
            grad_score = (weight.astype(F32) * (grad_prob - deltas[head])).astype(BF16)
            dq[head_rows(head), :] += nn(grad_score, key)
            grad_key += tn(grad_score, q_unit[head_rows(head), :])
            grad_value += tn(weight, grad)
        dkv_ref[j, :, 0:HEAD_DIM] = (SCALE * grad_key).astype(BF16)
        dkv_ref[j, :, HEAD_DIM:] = grad_value.astype(BF16)

    total = jnp.zeros((rows, 1), F32)
    for head in range(heads):
        q = q_ref[:, head_cols(head)]
        grad = SCALE * dq[head_rows(head), :]
        inverse = lax.rsqrt(jnp.sum(q * q, axis=1, keepdims=True) + EPS)
        along = jnp.sum(q * grad, axis=1, keepdims=True)
        back = (inverse * grad - q * (inverse * inverse * inverse * along)).astype(BF16)
        gq_ref[:, head_cols(head)] = back
        total += jnp.sum(back.astype(F32) * q, axis=1, keepdims=True)
    dot_ref[...] = jnp.broadcast_to(total, dot_ref.shape)
    attn = attn_ref[...]
    width = wo_ref.shape[1]
    piece = 768 if width % 768 == 0 else width
    for first in range(0, width, piece):
        span = pl.ds(first, piece)
        proj_ref[:, span] = nn(attn, wo_ref[:, span]).astype(BF16)


def attend(docs, q, dout, all_kv, wo):
    rows, cols = q.shape
    heads = cols // HEAD_DIM
    chunks = all_kv.shape[0]
    return pl.pallas_call(
        attend_kernel,
        out_shape=(
            jax.ShapeDtypeStruct((rows, cols), BF16),
            jax.ShapeDtypeStruct((rows, wo.shape[1]), BF16),
            jax.ShapeDtypeStruct((rows, cols), BF16),
            jax.ShapeDtypeStruct((rows, 128), F32),
            jax.ShapeDtypeStruct((chunks, rows, 2 * HEAD_DIM), BF16),
        ),
        in_specs=[SMEM_SPEC] + [VMEM_SPEC] * 4,
        out_specs=[VMEM_SPEC] * 5,
        scratch_shapes=[
            pltpu.VMEM((heads * rows, HEAD_DIM), BF16),
            pltpu.VMEM((heads * rows, HEAD_DIM), BF16),
            pltpu.VMEM((chunks, heads * rows, rows), BF16),
            pltpu.VMEM((heads * rows, 2 * HEAD_DIM), F32),
            pltpu.VMEM((heads * rows, HEAD_DIM), F32),
        ],
        compiler_params=pltpu.CompilerParams(vmem_limit_bytes=VMEM_LIMIT),
        name="attend",
    )(docs, q, dout, all_kv, wo)


def scatter_four(ring, in_ref, buf, stage, send, recv, finish):
    rows = in_ref.shape[0]
    width = in_ref.shape[1] // ring.count
    lo, hi = pl.ds(0, rows // 2), pl.ds(rows // 2, rows // 2)

    def block(half, step):
        return in_ref.at[half, pl.ds(pl.multiple_of(ring.at(step) * width, 128), width)]

    def move(src, slot, step):
        copy = remote(src, buf.at[slot], send.at[slot], recv.at[slot], ring.device(step))
        copy.start()
        return copy

    copies = [
        move(block(lo, 2), 0, 1),
        move(block(hi, 2), 1, -1),
        move(block(hi, 1), 2, 1),
        move(block(lo, -1), 3, -1),
    ]
    yield
    copies[0].wait_recv()
    stage[0] = (buf[0].astype(F32) + block(lo, 1)[...].astype(F32)).astype(BF16)
    copies.append(move(stage.at[0], 4, 1))
    yield
    copies[1].wait_recv()
    stage[1] = (buf[1].astype(F32) + block(hi, -1)[...].astype(F32)).astype(BF16)
    copies.append(move(stage.at[1], 5, -1))
    yield
    copies[2].wait_recv()
    copies[5].wait_recv()
    finish(hi, block(hi, 0)[...].astype(F32) + buf[2].astype(F32) + buf[5].astype(F32))
    yield
    copies[3].wait_recv()
    copies[4].wait_recv()
    finish(lo, block(lo, 0)[...].astype(F32) + buf[3].astype(F32) + buf[4].astype(F32))
    yield
    for copy in copies:
        copy.wait_send()


def scatter_four_scratch(rows, width):
    return [
        pltpu.VMEM((6, rows // 2, width), BF16),
        pltpu.VMEM((2, rows // 2, width), BF16),
        pltpu.SemaphoreType.DMA((6,)),
        pltpu.SemaphoreType.DMA((6,)),
    ]


def scatter_line(line, in_ref, other, buf, stage, send, recv, to_core, from_core, finish):
    rows = in_ref.shape[2]
    last = line.chips // 2
    halves = (pl.ds(0, rows // 2), pl.ds(rows // 2, rows // 2))
    order = [last]
    for k in range(last - 1, 0, -1):
        order += [k, -k]
    order.append(0)
    pieces = {}
    copies = []
    for slot, step in enumerate(order):
        chip = line.chip_at(step)
        copy = remote(
            in_ref.at[chip, line.other], other.at[chip], to_core.at[slot], from_core.at[slot], line.partner()
        )
        copy.start()
        copies.append(copy)
        pieces[step] = copy
    yield
    ready = set()

    def own(step, half):
        if abs(step) == last:
            step = last
        if step not in ready:
            pieces[step].wait_recv()
            ready.add(step)
        chip = line.chip_at(step)
        return in_ref[chip, line.core, half, :].astype(F32) + other[chip, half, :].astype(F32)

    sent = {}
    plan = [(last, 0)]
    for k in range(last - 1, 0, -1):
        plan += [(k, 1), (k, 0)]
    for k, which in plan:
        for way, d in ((0, 1), (1, -1)):
            part = which if way == 0 else 1 - which
            half = halves[part]
            value = own(d * k, half)
            if (way, k + 1, part) in sent:
                sent[way, k + 1, part].wait_recv()
                value = value + buf[way, k, half, :].astype(F32)
            stage[way, k - 1, half, :] = value.astype(BF16)
            copy = remote(
                stage.at[way, k - 1, half, :],
                buf.at[way, k - 1, half, :],
                send.at[way, k - 1, part],
                recv.at[way, k - 1, part],
                line.device(d),
            )
            copy.start()
            sent[way, k, part] = copy
            copies.append(copy)
            yield
    for part in (1, 0):
        half = halves[part]
        value = own(0, half)
        for way in (0, 1):
            sent[way, 1, part].wait_recv()
            value = value + buf[way, 0, half, :].astype(F32)
        finish(half, value)
        yield
    for copy in copies:
        copy.wait_send()


def scatter_line_scratch(chips, rows, width):
    last = chips // 2
    return [
        pltpu.VMEM((chips, rows, width), BF16),
        pltpu.VMEM((2, last, rows, width), BF16),
        pltpu.VMEM((2, last, rows, width), BF16),
        pltpu.SemaphoreType.DMA((2, last, 2)),
        pltpu.SemaphoreType.DMA((2, last, 2)),
        pltpu.SemaphoreType.DMA((chips,)),
        pltpu.SemaphoreType.DMA((chips,)),
    ]


def reduce_first_kernel(tp, seq, proj_ref, h_ref, dkv_ref, hout_ref, sum_ref, *scratch):
    four, rest = scratch[:4], scratch[4:]
    ring, line = Ring("tp", tp), Line(seq)
    greet([ring.device(1), ring.device(-1), line.device(1), line.device(-1), line.partner()])

    def finish_rows(half, value):
        hout_ref[half, :] = (h_ref[half, :].astype(F32) + value).astype(BF16)

    def finish_keys(half, value):
        sum_ref[half, :] = value

    run_together(
        scatter_line(line, dkv_ref, *rest, finish_keys),
        scatter_four(ring, proj_ref, *four, finish_rows),
    )


def reduce_first(tp, seq, proj, hidden, dkv):
    rows, width = hidden.shape
    chips = seq // 2
    dkv = dkv.reshape((chips, 2) + dkv.shape[1:])
    return pl.pallas_call(
        functools.partial(reduce_first_kernel, tp, seq),
        out_shape=(
            jax.ShapeDtypeStruct((rows, width), BF16),
            jax.ShapeDtypeStruct(dkv.shape[2:], F32),
        ),
        in_specs=[VMEM_SPEC] * 3,
        out_specs=[VMEM_SPEC] * 2,
        scratch_shapes=scatter_four_scratch(rows, width) + scatter_line_scratch(chips, *dkv.shape[2:]),
        compiler_params=pltpu.CompilerParams(
            collective_id=3, has_side_effects=True, vmem_limit_bytes=VMEM_LIMIT
        ),
        name="reduce_first",
    )(proj, hidden, dkv)


def backward_kernel(
    h_ref, src_ref, cot_ref, wq_ref, self_ref, cache_ref, gq_ref, dot_ref, attn_ref, kv_ref, sum_ref, rh_ref, rs_ref,
    rows_ref, source_ref, weight_ref,
    gkv, scaled_q, scaled_kv, fix_h, fix_s,
):
    step = pl.program_id(0)
    width = h_ref.shape[1] * pl.num_programs(0)

    @pl.when(step == 0)
    def _():
        kv, sums = kv_ref[...], sum_ref[...]
        key, grad = kv[:, :HEAD_DIM], sums[:, :HEAD_DIM]
        inverse = lax.rsqrt(jnp.sum(key * key, axis=1, keepdims=True) + EPS)
        along = jnp.sum(key * grad, axis=1, keepdims=True)
        back = inverse * grad - key * (inverse * inverse * inverse * along)
        both = jnp.concatenate([back, sums[:, HEAD_DIM:]], axis=1).astype(BF16)
        gkv[...] = both
        total = jnp.sum(both.astype(F32) * kv, axis=1, keepdims=True)
        rh, rs = rh_ref[:, 0:1], rs_ref[:, 0:1]
        fix_h[...] = rh_ref[...] * rh_ref[...] * dot_ref[...] / width
        fix_s[...] = rs_ref[...] * rs_ref[...] * total / width
        scaled_q[...] = (gq_ref[...].astype(F32) * rh).astype(BF16)
        scaled_kv[...] = (both.astype(F32) * rs).astype(BF16)

    hidden, source = h_ref[...], src_ref[...]
    is_self = lax.axis_index("section") == 0
    weight = jnp.where(is_self, self_ref[...], cache_ref[...])
    rh, rs = rh_ref[:, 0:1], rs_ref[:, 0:1]
    rows_ref[...] = (nt(gq_ref[...], wq_ref[...]) * rh - hidden.astype(F32) * fix_h[:, 0:1]).astype(BF16)
    source_ref[...] = (nt(gkv[...], weight) * rs - source.astype(F32) * fix_s[:, 0:1]).astype(BF16)
    cols = gq_ref.shape[1]
    weight_ref[:, 0:cols] = tn(hidden, scaled_q[...]).astype(BF16)
    weight_ref[:, cols : 2 * cols] = tn(cot_ref[...], attn_ref[...]).astype(BF16)
    weight_ref[:, 2 * cols :] = tn(source, scaled_kv[...]).astype(BF16)


def backward(steps, full_h, full_s, full_c, wq, self_w, cache_w, gq, dot, attn, kv, sums, rh, rs):
    rows, width = full_h.shape
    block = width // steps
    heads, kvw = wq.shape[1], self_w.shape[1]
    by_col = pl.BlockSpec((rows, block), lambda i: (0, i))
    by_row = lambda n: pl.BlockSpec((block, n), lambda i: (i, 0))
    whole = lambda n: pl.BlockSpec((rows, n), lambda i: (0, 0))
    return pl.pallas_call(
        backward_kernel,
        grid=(steps,),
        out_shape=(
            jax.ShapeDtypeStruct((rows, width), BF16),
            jax.ShapeDtypeStruct((rows, width), BF16),
            jax.ShapeDtypeStruct((width, 2 * heads + kvw), BF16),
        ),
        in_specs=[
            by_col, by_col, by_col, by_row(heads), by_row(kvw), by_row(kvw),
            whole(heads), whole(128), whole(heads), whole(kvw), whole(kvw), whole(128), whole(128),
        ],
        out_specs=[by_col, by_col, by_row(2 * heads + kvw)],
        scratch_shapes=[
            pltpu.VMEM((rows, kvw), BF16),
            pltpu.VMEM((rows, heads), BF16),
            pltpu.VMEM((rows, kvw), BF16),
            pltpu.VMEM((rows, 128), F32),
            pltpu.VMEM((rows, 128), F32),
        ],
        compiler_params=pltpu.CompilerParams(vmem_limit_bytes=VMEM_LIMIT),
        name="backward",
    )(full_h, full_s, full_c, wq, self_w, cache_w, gq, dot, attn, kv, sums, rh, rs)


def pass_along(ring, in_ref, out_ref, send, recv):
    copy = remote(in_ref, out_ref, send, recv, ring.device(1))
    copy.start()
    yield
    yield
    copy.wait()


def reduce_last_kernel(
    tp, seq, section, rows_ref, source_ref, weight_ref, hout_ref, cot_ref,
    passed_ref, gin_ref, gmem_ref, wq_ref, wo_ref, wself_ref, wcache_ref, *scratch
):
    four_a, four_b, rest = scratch[:4], scratch[4:8], scratch[8:15]
    pass_send, pass_recv, mine, got, ex_send, ex_recv, ex_local = scratch[15:]
    ring, line, sections = Ring("tp", tp), Line(seq), Ring("section", section)
    others = [sections.device(k) for k in range(1, section)]
    greet(
        [ring.device(1), ring.device(-1), line.device(1), line.device(-1), line.partner()] + others
    )
    heads = wq_ref.shape[1]

    def finish_input(half, value):
        gin_ref[half, :] = (cot_ref[half, :].astype(F32) + value).astype(BF16)

    def finish_memory(half, value):
        gmem_ref[half, :] = value.astype(BF16)

    def finish_weights(half, value):
        wq_ref[half, :] = value[:, 0:heads]
        wo_ref[half, :] = value[:, heads : 2 * heads]
        mine[half, :] = value[:, 2 * heads :]

    run_together(
        pass_along(sections, hout_ref, passed_ref, pass_send, pass_recv),
        scatter_line(line, weight_ref, *rest, finish_weights),
        scatter_four(ring, rows_ref, *four_a, finish_input),
        scatter_four(ring, source_ref, *four_b, finish_memory),
    )
    share = wself_ref.shape[0]
    copies = []
    for k in range(1, section):
        first = pl.multiple_of(sections.at(k) * share, 8)
        copy = remote(
            mine.at[pl.ds(first, share), :],
            got.at[sections.me],
            ex_send.at[k],
            ex_recv.at[k],
            sections.device(k),
        )
        copy.start()
        copies.append(copy)
    first = pl.multiple_of(sections.me * share, 8)
    local = pltpu.make_async_copy(mine.at[pl.ds(first, share), :], got.at[sections.me], ex_local)
    local.start()
    for copy in copies:
        copy.wait_recv()
    local.wait()
    wself_ref[...] = got[0]
    total = got[1]
    for k in range(2, section):
        total = total + got[k]
    wcache_ref[...] = total
    for copy in copies:
        copy.wait_send()


def reduce_last(tp, seq, section, rows_part, source_part, weight_part, hout, cot, heads, kvw):
    rows, width = hout.shape
    chips = seq // 2
    share = weight_part.shape[0] // seq
    weight_part = weight_part.reshape(chips, 2, share, weight_part.shape[1])
    piece = share // section
    return pl.pallas_call(
        functools.partial(reduce_last_kernel, tp, seq, section),
        out_shape=(
            jax.ShapeDtypeStruct((rows, width), BF16),
            jax.ShapeDtypeStruct((rows, width), BF16),
            jax.ShapeDtypeStruct((rows, width), BF16),
            jax.ShapeDtypeStruct((share, heads), F32),
            jax.ShapeDtypeStruct((share, heads), F32),
            jax.ShapeDtypeStruct((piece, kvw), F32),
            jax.ShapeDtypeStruct((piece, kvw), F32),
        ),
        in_specs=[VMEM_SPEC] * 5,
        out_specs=[VMEM_SPEC] * 7,
        scratch_shapes=scatter_four_scratch(rows, width)
        + scatter_four_scratch(rows, width)
        + scatter_line_scratch(chips, *weight_part.shape[2:])
        + [
            pltpu.SemaphoreType.DMA,
            pltpu.SemaphoreType.DMA,
            pltpu.VMEM((share, kvw), F32),
            pltpu.VMEM((section, piece, kvw), F32),
            pltpu.SemaphoreType.DMA((section,)),
            pltpu.SemaphoreType.DMA((section,)),
            pltpu.SemaphoreType.DMA,
        ],
        compiler_params=pltpu.CompilerParams(
            collective_id=4, has_side_effects=True, vmem_limit_bytes=VMEM_LIMIT
        ),
        name="reduce_last",
    )(rows_part, source_part, weight_part, hout, cot)


def on_device(
    tp, seq, section, h_in, memory, cotangent, block_docs, w_query, w_out, self_weight, cache_weight
):
    is_self = lax.axis_index("section") == 0
    hidden, cot = h_in[0], cotangent[0]
    source = jnp.where(is_self, hidden, memory[0])
    wq, wo = w_query[0], w_out[0]
    width = wq.shape[0]
    self_w = self_weight.reshape(width, -1)
    cache_w = cache_weight.reshape(width, -1)
    full_s, full_h, full_c = gather_rows(tp, source, hidden, cot)
    q, kv, payload, dout, rh, rs = project(
        tp, block_docs, full_h, full_s, full_c, wq, wo, self_w, cache_w
    )
    all_kv = gather_keys(seq, payload)
    attn, proj, gq, dot, dkv = attend(block_docs, q, dout, all_kv, wo)
    hout, sums = reduce_first(tp, seq, proj, hidden, dkv)
    rows_part, source_part, weight_part = backward(
        tp, full_h, full_s, full_c, wq, self_w, cache_w, gq, dot, attn, kv, sums, rh, rs
    )
    passed, gin, gmem, gwq, gwo, gself, gcache = reduce_last(
        tp, seq, section, rows_part, source_part, weight_part, hout, cot, wq.shape[1], self_w.shape[1]
    )
    kv_shape = (gself.shape[0],) + self_weight.shape[1:]
    return (
        passed[None], gin[None], gmem[None], gwq[None], gwo.T[None],
        gself.reshape(kv_shape), gcache.reshape(kv_shape),
    )


def solution(mesh):
    sizes = mesh.shape
    return jax.shard_map(
        functools.partial(on_device, sizes["tp"], sizes["seq"], sizes["section"]),
        mesh=mesh,
        in_specs=(
            P("section", "seq", "tp"),
            P("section", "seq", "tp"),
            P("section", "seq", "tp"),
            P("section", "seq"),
            P("section", None, "tp"),
            P("section", "tp", None),
            P(None, None, "tp"),
            P(None, None, "tp"),
        ),
        out_specs=(
            P("section", "seq", "tp"),
            P("section", "seq", "tp"),
            P("section", "seq", "tp"),
            P("section", "seq", "tp"),
            P("section", "tp", "seq"),
            P(("seq", "section"), None, "tp"),
            P(("seq", "section"), None, "tp"),
        ),
        check_vma=False,
    )
```

```python
import functools
import math

import jax
import jax.numpy as jnp
from jax import lax
from jax.experimental import pallas as pl
from jax.experimental.pallas import tpu as pltpu
from jax.sharding import PartitionSpec as P

MESH = pl.DeviceIdType.MESH
HEAD_DIM = 128
BLK = 128
WIN = 1024
SCALE = 40.0
EPS = 1e-06
EXP2_SCALE = SCALE * math.log2(math.e)
F32 = jnp.float32
BF16 = jnp.bfloat16
DOC_ROWS = 16
VMEM_SPEC = pl.BlockSpec(memory_space=pltpu.VMEM)
ANY_SPEC = pl.BlockSpec(memory_space=pl.ANY)
SMEM_SPEC = pl.BlockSpec(memory_space=pltpu.SMEM)
VMEM_LIMIT = 60 * 1024 * 1024


def nt(left, right):
    return lax.dot_general(left, right, (((1,), (1,)), ((), ())), preferred_element_type=F32)


def nn(left, right):
    return lax.dot_general(left, right, (((1,), (0,)), ((), ())), preferred_element_type=F32)


def tn(left, right):
    return lax.dot_general(left, right, (((0,), (0,)), ((), ())), preferred_element_type=F32)


def remote(src, dst, send_sem, recv_sem, device):
    return pltpu.make_async_remote_copy(
        src_ref=src,
        dst_ref=dst,
        send_sem=send_sem,
        recv_sem=recv_sem,
        device_id=device,
        device_id_type=MESH,
    )


def greet(devices):
    barrier = pltpu.get_barrier_semaphore()
    for device in devices:
        pl.semaphore_signal(barrier, inc=1, device_id=device, device_id_type=MESH)
    pl.semaphore_wait(barrier, len(devices))


def run_together(*streams):
    live = list(streams)
    while live:
        for stream in list(live):
            try:
                next(stream)
            except StopIteration:
                live.remove(stream)


class Ring:
    def __init__(self, axis, count):
        self.axis = axis
        self.me = lax.axis_index(axis)
        self.count = count

    def at(self, step):
        return lax.rem(self.me + step + self.count, self.count)

    def device(self, step):
        return {self.axis: self.at(step)}


class Line:
    def __init__(self, count):
        self.me = lax.axis_index("seq")
        self.chips = count // 2
        self.chip = self.me // 2
        self.core = self.me - self.chip * 2
        self.other = 1 - self.core

    def chip_at(self, step):
        return lax.rem(self.chip + step + self.chips, self.chips)

    def index(self, step):
        return self.chip_at(step) * 2 + self.core

    def device(self, step):
        return {"seq": self.index(step)}

    def partner(self):
        return {"seq": self.chip * 2 + self.other}


def gather_four(ring, full, send, recv):
    rows = full.shape[0]
    width = full.shape[1] // ring.count
    lo, hi = pl.ds(0, rows // 2), pl.ds(rows // 2, rows // 2)

    def block(half, step):
        return full.at[half, pl.ds(pl.multiple_of(ring.at(step) * width, 128), width)]

    def move(piece, slot, step):
        copy = remote(piece, piece, send.at[slot], recv.at[slot], ring.device(step))
        copy.start()
        return copy

    right_lo, left_hi = move(block(lo, 0), 0, 1), move(block(hi, 0), 1, -1)
    right_hi, left_lo = move(block(hi, 0), 2, 1), move(block(lo, 0), 3, -1)
    yield
    right_lo.wait_recv()
    relay_right = move(block(lo, -1), 4, 1)
    left_hi.wait_recv()
    relay_left = move(block(hi, 1), 5, -1)
    yield
    for copy in (right_hi, left_lo, relay_right, relay_left):
        copy.wait_recv()
    yield
    for copy in (right_lo, left_hi, right_hi, left_lo, relay_right, relay_left):
        copy.wait_send()


def gather_line(line, full, send, recv, to_core, from_core):
    rows = full.shape[1]
    cut = (rows // 2 + 15) // 16 * 16
    halves = {1: pl.ds(0, cut), -1: pl.ds(cut, rows - cut)}
    copies, hops, passed = [], {}, []

    def move(piece, s, r, device):
        copy = remote(piece, piece, s, r, device)
        copy.start()
        copies.append(copy)
        return copy

    last = line.chips // 2
    own = full.at[line.me]
    for way, d in ((0, 1), (1, -1)):
        hops[way] = move(own, send.at[way, 0], recv.at[way, 0], line.device(d))
    passed.append(move(own, to_core.at[0], from_core.at[0], line.partner()))
    yield
    slot = 1
    for hop in range(1, last + 1):
        for way, d in ((0, 1), (1, -1)):
            hops[way].wait_recv()
            block = line.index(-d * hop)
            piece = full.at[block]
            if hop < last:
                ahead = piece if hop < last - 1 else full.at[block, halves[d], :]
                hops[way] = move(ahead, send.at[way, hop], recv.at[way, hop], line.device(d))
            else:
                piece = full.at[block, halves[d], :]
            passed.append(move(piece, to_core.at[slot], from_core.at[slot], line.partner()))
            slot += 1
        yield
    for copy in passed:
        copy.wait_recv()
    yield
    for copy in copies:
        copy.wait_send()


def gather_line_scratch(chips):
    last = chips // 2
    return [
        pltpu.SemaphoreType.DMA((2, last)),
        pltpu.SemaphoreType.DMA((2, last)),
        pltpu.SemaphoreType.DMA((2 * last + 1,)),
        pltpu.SemaphoreType.DMA((2 * last + 1,)),
    ]


def scatter_four(ring, in_ref, buf, stage, send, recv, finish):
    rows = in_ref.shape[0]
    width = in_ref.shape[1] // ring.count
    lo, hi = pl.ds(0, rows // 2), pl.ds(rows // 2, rows // 2)

    def block(half, step):
        return in_ref.at[half, pl.ds(pl.multiple_of(ring.at(step) * width, 128), width)]

    def move(src, slot, step):
        copy = remote(src, buf.at[slot], send.at[slot], recv.at[slot], ring.device(step))
        copy.start()
        return copy

    copies = [
        move(block(lo, 2), 0, 1),
        move(block(hi, 2), 1, -1),
        move(block(hi, 1), 2, 1),
        move(block(lo, -1), 3, -1),
    ]
    yield
    copies[0].wait_recv()
    stage[0] = (buf[0].astype(F32) + block(lo, 1)[...].astype(F32)).astype(BF16)
    copies.append(move(stage.at[0], 4, 1))
    yield
    copies[1].wait_recv()
    stage[1] = (buf[1].astype(F32) + block(hi, -1)[...].astype(F32)).astype(BF16)
    copies.append(move(stage.at[1], 5, -1))
    yield
    copies[2].wait_recv()
    copies[5].wait_recv()
    finish(hi, block(hi, 0)[...].astype(F32) + buf[2].astype(F32) + buf[5].astype(F32))
    yield
    copies[3].wait_recv()
    copies[4].wait_recv()
    finish(lo, block(lo, 0)[...].astype(F32) + buf[3].astype(F32) + buf[4].astype(F32))
    yield
    for copy in copies:
        copy.wait_send()


def scatter_four_scratch(rows, width):
    return [
        pltpu.VMEM((6, rows // 2, width), BF16),
        pltpu.VMEM((2, rows // 2, width), BF16),
        pltpu.SemaphoreType.DMA((6,)),
        pltpu.SemaphoreType.DMA((6,)),
    ]


def scatter_line(line, in_ref, other, buf, stage, send, recv, to_core, from_core, finish):
    rows = in_ref.shape[1]
    last = line.chips // 2
    halves = (pl.ds(0, rows // 2), pl.ds(rows // 2, rows // 2))
    order = [last]
    for k in range(last - 1, 0, -1):
        order += [k, -k]
    order.append(0)
    pieces = {}
    copies = []
    for slot, step in enumerate(order):
        chip = line.chip_at(step)
        copy = remote(
            in_ref.at[chip * 2 + line.other], other.at[chip], to_core.at[slot], from_core.at[slot], line.partner()
        )
        copy.start()
        copies.append(copy)
        pieces[step] = copy
    yield
    ready = set()

    def own(step, half):
        if abs(step) == last:
            step = last
        if step not in ready:
            pieces[step].wait_recv()
            ready.add(step)
        chip = line.chip_at(step)
        return in_ref[chip * 2 + line.core, half, :].astype(F32) + other[chip, half, :].astype(F32)

    sent = {}
    plan = [(last, 0)]
    for k in range(last - 1, 0, -1):
        plan += [(k, 1), (k, 0)]
    for k, which in plan:
        for way, d in ((0, 1), (1, -1)):
            part = which if way == 0 else 1 - which
            half = halves[part]
            value = own(d * k, half)
            if (way, k + 1, part) in sent:
                sent[way, k + 1, part].wait_recv()
                value = value + buf[way, k, half, :].astype(F32)
            stage[way, k - 1, half, :] = value.astype(BF16)
            copy = remote(
                stage.at[way, k - 1, half, :],
                buf.at[way, k - 1, half, :],
                send.at[way, k - 1, part],
                recv.at[way, k - 1, part],
                line.device(d),
            )
            copy.start()
            sent[way, k, part] = copy
            copies.append(copy)
            yield
    for part in (1, 0):
        half = halves[part]
        value = own(0, half)
        for way in (0, 1):
            sent[way, 1, part].wait_recv()
            value = value + buf[way, 0, half, :].astype(F32)
        finish(half, value)
        yield
    for copy in copies:
        copy.wait_send()


def scatter_line_scratch(chips, rows, width):
    last = chips // 2
    return [
        pltpu.VMEM((chips, rows, width), BF16),
        pltpu.VMEM((2, last, rows, width), BF16),
        pltpu.VMEM((2, last, rows, width), BF16),
        pltpu.SemaphoreType.DMA((2, last, 2)),
        pltpu.SemaphoreType.DMA((2, last, 2)),
        pltpu.SemaphoreType.DMA((chips,)),
        pltpu.SemaphoreType.DMA((chips,)),
    ]


def step_kernel(
    tp, seq, section,
    docs_ref, h_ref, mem_ref, cot_ref, wq_any, wo_any, kvw_any,
    passed_ref, gin_ref, gmem_ref, gwq_ref, gwo_ref, gself_ref, gcache_ref,
    full_h, full_s, full_c, wq, wo, kvw,
    q_raw, kv_raw, all_kv, q_unit, dout, weights, acc, dq, attn, gq, gkv, hout,
    proj, rows_part, source_part, dkv, part_q, part_o, part_kv, sums, mine, got,
    load, gather_send, gather_recv, pass_send, pass_recv, ex_send, ex_recv, ex_local,
    *scratch,
):
    line_gather, scratch = scratch[:4], scratch[4:]
    four = [scratch[4 * k : 4 * k + 4] for k in range(3)]
    scratch = scratch[12:]
    lines = [scratch[7 * k : 7 * k + 7] for k in range(4)]
    ring, line, sections = Ring("tp", tp), Line(seq), Ring("section", section)
    me = line.me
    is_self = sections.me == 0
    rows, width = h_ref.shape
    model = width * tp
    heads = wq.shape[1] // HEAD_DIM
    chunks = seq

    def cols(step):
        return pl.ds(pl.multiple_of(ring.at(step) * width, 128), width)

    own_h = pltpu.make_async_copy(h_ref, full_h.at[:, cols(0)], load.at[0])
    own_c = pltpu.make_async_copy(cot_ref, full_c.at[:, cols(0)], load.at[1])
    source_self = pltpu.make_async_copy(h_ref, full_s.at[:, cols(0)], load.at[2])
    source_cross = pltpu.make_async_copy(mem_ref, full_s.at[:, cols(0)], load.at[2])

    @pl.when(is_self)
    def _():
        source_self.start()

    @pl.when(jnp.logical_not(is_self))
    def _():
        source_cross.start()

    own_h.start()
    own_c.start()
    load_kvw = pltpu.make_async_copy(kvw_any, kvw, load.at[3])
    load_wq = pltpu.make_async_copy(wq_any, wq, load.at[4])
    load_wo = pltpu.make_async_copy(wo_any, wo, load.at[5])
    load_kvw.start()
    load_wq.start()
    load_wo.start()
    greet(
        [ring.device(1), ring.device(-1), line.device(1), line.device(-1), line.partner()]
        + [sections.device(k) for k in range(1, section)]
    )
    gather_s, gather_h, gather_c = [
        gather_four(ring, full, gather_send.at[k], gather_recv.at[k])
        for k, full in enumerate((full_s, full_h, full_c))
    ]
    keys = gather_line(line, all_kv, *line_gather)
    blocks = [pl.ds(k * width, width) for k in range(tp)]

    def factor(full):
        total = jnp.zeros((rows, 128), F32)
        for span in blocks:
            wide = full[:, span].astype(F32)
            wide = wide * wide
            for first in range(0, width, 128):
                total += wide[:, first : first + 128]
        return lax.rsqrt(jnp.sum(total, axis=1, keepdims=True) / model + EPS)

    def head_rows(head):
        return pl.ds(head * rows, rows)

    def head_cols(head):
        return pl.ds(head * HEAD_DIM, HEAD_DIM)

    source_self.wait()
    next(gather_s)
    own_h.wait()
    own_c.wait()
    acc[...] = jnp.zeros_like(acc)
    dq[...] = jnp.zeros_like(dq)
    low = jnp.where(is_self, jnp.maximum(me - WIN // rows, 0), 0)
    zero_chunk = jnp.zeros((rows, 2 * HEAD_DIM), BF16)

    @pl.loop(0, low)
    def _(j):
        dkv[j] = zero_chunk

    @pl.loop(me + 1, chunks)
    def _(j):
        dkv[j] = zero_chunk

    load_kvw.wait()
    next(gather_s)
    next(gather_h)
    next(gather_s)
    rs = factor(full_s)
    kv = nn(full_s[:, blocks[0]], kvw[blocks[0], :])
    for span in blocks[1:]:
        kv += nn(full_s[:, span], kvw[span, :])
    kv = kv * rs
    kv_raw[...] = kv
    key, value = kv[:, :HEAD_DIM], kv[:, HEAD_DIM:]
    unit = key * lax.rsqrt(jnp.sum(key * key, axis=1, keepdims=True) + EPS)
    all_kv[me, 0:rows, 0:HEAD_DIM] = unit.astype(BF16)
    all_kv[me, 0:rows, HEAD_DIM:] = value.astype(BF16)
    doc_lane = lax.broadcasted_iota(jnp.int32, (DOC_ROWS, 2 * BLK), 1)
    docs = jnp.where(doc_lane < BLK, docs_ref[0, 0], docs_ref[0, 1])
    all_kv[me, rows:, :] = docs.astype(F32).astype(BF16)
    next(keys)
    next(gather_h)
    next(gather_c)
    load_wq.wait()
    next(keys)
    next(keys)
    next(gather_h)
    rh = factor(full_h)
    q = nn(full_h[:, blocks[0]], wq[blocks[0], :])
    for span in blocks[1:]:
        q += nn(full_h[:, span], wq[span, :])
    q_raw[...] = q * rh
    for head in range(heads):
        part = q_raw[:, head_cols(head)]
        unit = part * lax.rsqrt(jnp.sum(part * part, axis=1, keepdims=True) + EPS)
        q_unit[head_rows(head), :] = unit.astype(BF16)
    next(keys)
    next(gather_c)
    next(keys)
    next(keys)

    row = lax.broadcasted_iota(jnp.int32, (rows, 1), 0)
    lane = lax.broadcasted_iota(jnp.int32, (1, rows), 1)
    query_doc = jnp.where(row < BLK, docs_ref[0, 0], docs_ref[0, 1]).astype(F32)
    query_pos = me * rows + row
    upper = jnp.where(is_self, query_pos, query_pos // BLK * BLK + BLK - 1)
    lower = jnp.where(is_self, query_pos - WIN, -1)
    ones = jnp.ones((rows, HEAD_DIM), BF16)

    @pl.loop(low, me + 1)
    def _(j):
        key = all_kv[j, 0:rows, 0:HEAD_DIM]
        value = jnp.concatenate([all_kv[j, 0:rows, HEAD_DIM:], ones], axis=1)
        key_doc = all_kv[j, rows:, :].astype(F32)[0:1, :]
        key_pos = j * rows + lane
        seen = (key_doc == query_doc) & (key_pos <= upper) & (key_pos > lower)
        for head in range(heads):
            score = nt(q_unit[head_rows(head), :], key)
            weight = jnp.where(seen, jnp.exp2(score * EXP2_SCALE), 0.0).astype(BF16)
            weights[j, head_rows(head), :] = weight
            acc[head_rows(head), :] += nn(weight, value)

    for head in range(heads):
        total = acc[head_rows(head), :]
        attn[:, head_cols(head)] = (total[:, :HEAD_DIM] * (1.0 / total[:, HEAD_DIM:])).astype(BF16)
    load_wo.wait()
    attn_now = attn[...]
    for span in blocks:
        proj[:, span] = nn(attn_now, wo[:, span]).astype(BF16)

    def finish_rows(half, value):
        hout[half, :] = (full_h[half, cols(0)].astype(F32) + value).astype(BF16)

    def finish_input(half, value):
        gin_ref[half, :] = (full_c[half, cols(0)].astype(F32) + value).astype(BF16)

    def finish_memory(half, value):
        gmem_ref[half, :] = value.astype(BF16)

    def finish_keys(half, value):
        sums[half, :] = value

    def finish_wq(half, value):
        gwq_ref[half, :] = value

    def finish_wo(half, value):
        gwo_ref[half, :] = value

    def finish_kv(half, value):
        mine[half, :] = value

    red_hout = scatter_four(ring, proj, *four[0], finish_rows)
    next(red_hout)
    next(gather_c)
    grad = nt(full_c[:, blocks[0]], wo[:, blocks[0]])
    for span in blocks[1:]:
        grad += nt(full_c[:, span], wo[:, span])
    share = part_o.shape[1]
    per_block = width // share
    for k, span in enumerate(blocks):
        value = tn(full_c[:, span], attn_now).astype(BF16)
        part_o[k * per_block : (k + 1) * per_block] = value.reshape(per_block, share, value.shape[1])
    red_wo = scatter_line(line, part_o, *lines[0], finish_wo)
    next(red_wo)
    deltas = []
    for head in range(heads):
        inverse = 1.0 / acc[head_rows(head), HEAD_DIM:]
        part = grad[:, head * HEAD_DIM : (head + 1) * HEAD_DIM].astype(BF16).astype(F32)
        delta = jnp.sum(part * attn[:, head_cols(head)].astype(F32), axis=1, keepdims=True)
        dout[head_rows(head), :] = (part * inverse).astype(BF16)
        deltas.append(delta * inverse[:, 0:1])

    def advance(stream, times):
        for _ in range(times):
            next(stream, None)

    def back(start, stop):
        @pl.loop(jnp.maximum(low, start), jnp.minimum(me + 1, stop))
        def _(j):
            key = all_kv[j, 0:rows, 0:HEAD_DIM]
            value = all_kv[j, 0:rows, HEAD_DIM:]
            grad_key = jnp.zeros((rows, HEAD_DIM), F32)
            grad_value = jnp.zeros((rows, HEAD_DIM), F32)
            for head in range(heads):
                weight = weights[j, head_rows(head), :]
                part = dout[head_rows(head), :]
                grad_prob = nt(part, value)
                grad_score = (weight.astype(F32) * (grad_prob - deltas[head])).astype(BF16)
                dq[head_rows(head), :] += nn(grad_score, key)
                grad_key += tn(grad_score, q_unit[head_rows(head), :])
                grad_value += tn(weight, part)
            dkv[j, :, 0:HEAD_DIM] = (SCALE * grad_key).astype(BF16)
            dkv[j, :, HEAD_DIM:] = grad_value.astype(BF16)

    quarter = chunks // 4
    for k in range(4):
        back(k * quarter, (k + 1) * quarter)
        if k < 3:
            advance(red_hout, 2)
            advance(red_wo, 4)
    red_keys = scatter_line(line, dkv, *lines[1], finish_keys)
    next(red_keys)
    pass_on = pass_along(sections, hout, passed_ref, pass_send, pass_recv)
    next(pass_on)

    total = jnp.zeros((rows, 1), F32)
    scaled = []
    for head in range(heads):
        part = q_raw[:, head_cols(head)]
        slope = SCALE * dq[head_rows(head), :]
        inverse = lax.rsqrt(jnp.sum(part * part, axis=1, keepdims=True) + EPS)
        along = jnp.sum(part * slope, axis=1, keepdims=True)
        value = (inverse * slope - part * (inverse * inverse * inverse * along)).astype(BF16)
        gq[:, head_cols(head)] = value
        total += jnp.sum(value.astype(F32) * part, axis=1, keepdims=True)
        scaled.append((value.astype(F32) * rh).astype(BF16))
    scaled_q = jnp.concatenate(scaled, axis=1)
    fix = rh * rh * total / model
    for span in blocks:
        value = nt(gq[...], wq[span, :]) * rh - full_h[:, span].astype(F32) * fix
        rows_part[:, span] = value.astype(BF16)
    red_rows = scatter_four(ring, rows_part, *four[1], finish_input)
    next(red_rows)
    advance(red_keys, 4)
    for k, span in enumerate(blocks):
        value = tn(full_h[:, span], scaled_q).astype(BF16)
        part_q[k * per_block : (k + 1) * per_block] = value.reshape(per_block, share, value.shape[1])
        advance(red_keys, 1)
    red_wq = scatter_line(line, part_q, *lines[2], finish_wq)
    while next(red_keys, 1) is None:
        next(red_rows, None)
        next(red_wo, None)
    next(red_wq)
    summed = sums[...]
    kv = kv_raw[...]
    key, slope = kv[:, :HEAD_DIM], summed[:, :HEAD_DIM]
    inverse = lax.rsqrt(jnp.sum(key * key, axis=1, keepdims=True) + EPS)
    along = jnp.sum(key * slope, axis=1, keepdims=True)
    slope = inverse * slope - key * (inverse * inverse * inverse * along)
    both = jnp.concatenate([slope, summed[:, HEAD_DIM:]], axis=1).astype(BF16)
    total = jnp.sum(both.astype(F32) * kv, axis=1, keepdims=True)
    fix = rs * rs * total / model
    for span in blocks:
        value = nt(both, kvw[span, :]) * rs - full_s[:, span].astype(F32) * fix
        source_part[:, span] = value.astype(BF16)
    red_source = scatter_four(ring, source_part, *four[2], finish_memory)
    next(red_source)
    scaled_kv = (both.astype(F32) * rs).astype(BF16)
    for k, span in enumerate(blocks):
        value = tn(full_s[:, span], scaled_kv).astype(BF16)
        part_kv[k * per_block : (k + 1) * per_block] = value.reshape(per_block, share, value.shape[1])
        next(red_wo, None)
        next(red_wq, None)
    red_kv = scatter_line(line, part_kv, *lines[3], finish_kv)
    run_together(red_kv, red_wq, red_source, red_rows, red_wo)

    piece = gself_ref.shape[0]
    copies = []
    for k in range(1, section):
        first = pl.multiple_of(sections.at(k) * piece, 8)
        copy = remote(
            mine.at[pl.ds(first, piece), :], got.at[sections.me], ex_send.at[k], ex_recv.at[k], sections.device(k)
        )
        copy.start()
        copies.append(copy)
    first = pl.multiple_of(sections.me * piece, 8)
    local = pltpu.make_async_copy(mine.at[pl.ds(first, piece), :], got.at[sections.me], ex_local)
    local.start()
    run_together(pass_on, red_hout, gather_s, gather_h, gather_c, keys)
    for copy in copies:
        copy.wait_recv()
    local.wait()
    gself_ref[...] = got[0]
    total = got[1]
    for k in range(2, section):
        total = total + got[k]
    gcache_ref[...] = total
    for copy in copies:
        copy.wait_send()


def pass_along(ring, in_ref, out_ref, send, recv):
    copy = remote(in_ref, out_ref, send, recv, ring.device(1))
    copy.start()
    yield
    copy.wait()


def whole_step(tp, seq, section, docs, hidden, memory, cot, wq, wo, kvw):
    rows, width = hidden.shape
    model, cols = wq.shape
    heads = cols // HEAD_DIM
    kv = kvw.shape[1]
    chips = seq // 2
    share = model // seq
    piece = share // section
    small = jax.ShapeDtypeStruct((rows, width), BF16)
    vmem = pltpu.VMEM
    dma = pltpu.SemaphoreType.DMA
    scratch = [
        vmem((rows, model), BF16), vmem((rows, model), BF16), vmem((rows, model), BF16),
        vmem((model, cols), BF16), vmem((cols, model), BF16), vmem((model, kv), BF16),
        vmem((rows, cols), F32), vmem((rows, kv), F32),
        vmem((seq, rows + DOC_ROWS, kv), BF16),
        vmem((heads * rows, HEAD_DIM), BF16), vmem((heads * rows, HEAD_DIM), BF16),
        vmem((seq, heads * rows, rows), BF16),
        vmem((heads * rows, 2 * HEAD_DIM), F32), vmem((heads * rows, HEAD_DIM), F32),
        vmem((rows, cols), BF16), vmem((rows, cols), BF16), vmem((rows, kv), BF16), vmem((rows, width), BF16),
        vmem((rows, model), BF16), vmem((rows, model), BF16), vmem((rows, model), BF16),
        vmem((seq, rows, kv), BF16),
        vmem((seq, share, cols), BF16), vmem((seq, share, cols), BF16), vmem((seq, share, kv), BF16),
        vmem((rows, kv), F32), vmem((share, kv), F32), vmem((section, piece, kv), F32),
        dma((6,)), dma((3, 6)), dma((3, 6)), dma, dma, dma((section,)), dma((section,)), dma,
    ]
    scratch += gather_line_scratch(chips)
    for _ in range(3):
        scratch += scatter_four_scratch(rows, width)
    for shape in ((share, cols), (rows, kv), (share, cols), (share, kv)):
        scratch += scatter_line_scratch(chips, *shape)
    return pl.pallas_call(
        functools.partial(step_kernel, tp, seq, section),
        out_shape=(
            small, small, small,
            jax.ShapeDtypeStruct((share, cols), F32), jax.ShapeDtypeStruct((share, cols), F32),
            jax.ShapeDtypeStruct((piece, kv), F32), jax.ShapeDtypeStruct((piece, kv), F32),
        ),
        in_specs=[SMEM_SPEC] + [ANY_SPEC] * 6,
        out_specs=[VMEM_SPEC] * 7,
        scratch_shapes=scratch,
        compiler_params=pltpu.CompilerParams(
            collective_id=1, has_side_effects=True, vmem_limit_bytes=VMEM_LIMIT
        ),
        name="step",
    )(docs, hidden, memory, cot, wq, wo, kvw)


def finish_kernel(passed, gin, gmem, gwq, gwo, gself, gcache, *outs):
    for source, target in zip((passed, gin, gmem, gwq), outs[:4]):
        target[...] = source[...]
    outs[4][...] = gwo[...].T
    for source, target in ((gself, outs[5]), (gcache, outs[6])):
        half = source.shape[1] // 2
        target[:, 0, :] = source[:, :half]
        target[:, 1, :] = source[:, half:]


def finish(results):
    shapes = [jax.ShapeDtypeStruct(x.shape, x.dtype) for x in results[:4]]
    shapes.append(jax.ShapeDtypeStruct(results[4].shape[::-1], F32))
    for x in results[5:]:
        shapes.append(jax.ShapeDtypeStruct((x.shape[0], 2, x.shape[1] // 2), F32))
    return pl.pallas_call(
        finish_kernel,
        out_shape=tuple(shapes),
        in_specs=[VMEM_SPEC] * 7,
        out_specs=[VMEM_SPEC] * 7,
        name="finish",
    )(*results)


def on_device(
    tp, seq, section, h_in, memory, cotangent, block_docs, w_query, w_out, self_weight, cache_weight
):
    is_self = lax.axis_index("section") == 0
    width = w_query.shape[1]
    kvw = jnp.where(is_self, self_weight, cache_weight).reshape(width, -1)
    results = whole_step(
        tp, seq, section, block_docs, h_in[0], memory[0], cotangent[0], w_query[0], w_out[0], kvw
    )
    passed, gin, gmem, gwq, gwo, gself, gcache = finish(results)
    return (passed[None], gin[None], gmem[None], gwq[None], gwo[None], gself, gcache)


def solution(mesh):
    sizes = mesh.shape
    return jax.shard_map(
        functools.partial(on_device, sizes["tp"], sizes["seq"], sizes["section"]),
        mesh=mesh,
        in_specs=(
            P("section", "seq", "tp"),
            P("section", "seq", "tp"),
            P("section", "seq", "tp"),
            P("section", "seq"),
            P("section", None, "tp"),
            P("section", "tp", None),
            P(None, None, "tp"),
            P(None, None, "tp"),
        ),
        out_specs=(
            P("section", "seq", "tp"),
            P("section", "seq", "tp"),
            P("section", "seq", "tp"),
            P("section", "seq", "tp"),
            P("section", "tp", "seq"),
            P(("seq", "section"), None, "tp"),
            P(("seq", "section"), None, "tp"),
        ),
        check_vma=False,
    )
```

```python
import functools
import math

import jax
import jax.numpy as jnp
from jax import lax
from jax.experimental import pallas as pl
from jax.experimental.pallas import tpu as pltpu
from jax.sharding import PartitionSpec as P

MESH = pl.DeviceIdType.MESH
HEAD_DIM = 128
BLK = 128
WIN = 1024
SCALE = 40.0
EPS = 1e-06
EXP2_SCALE = SCALE * math.log2(math.e)
F32 = jnp.float32
BF16 = jnp.bfloat16
DOC_ROWS = 16
VMEM_SPEC = pl.BlockSpec(memory_space=pltpu.VMEM)
ANY_SPEC = pl.BlockSpec(memory_space=pl.ANY)
SMEM_SPEC = pl.BlockSpec(memory_space=pltpu.SMEM)
VMEM_LIMIT = 60 * 1024 * 1024


def nt(left, right):
    return lax.dot_general(left, right, (((1,), (1,)), ((), ())), preferred_element_type=F32)


def nn(left, right):
    return lax.dot_general(left, right, (((1,), (0,)), ((), ())), preferred_element_type=F32)


def tn(left, right):
    return lax.dot_general(left, right, (((0,), (0,)), ((), ())), preferred_element_type=F32)


def remote(src, dst, send_sem, recv_sem, device):
    return pltpu.make_async_remote_copy(
        src_ref=src,
        dst_ref=dst,
        send_sem=send_sem,
        recv_sem=recv_sem,
        device_id=device,
        device_id_type=MESH,
    )


def greet(devices):
    barrier = pltpu.get_barrier_semaphore()
    for device in devices:
        pl.semaphore_signal(barrier, inc=1, device_id=device, device_id_type=MESH)
    pl.semaphore_wait(barrier, len(devices))


def run_together(*streams):
    live = list(streams)
    while live:
        for stream in list(live):
            try:
                next(stream)
            except StopIteration:
                live.remove(stream)


class Ring:
    def __init__(self, axis, count):
        self.axis = axis
        self.me = lax.axis_index(axis)
        self.count = count

    def at(self, step):
        return lax.rem(self.me + step + self.count, self.count)

    def device(self, step):
        return {self.axis: self.at(step)}


class Line:
    def __init__(self, count):
        self.me = lax.axis_index("seq")
        self.chips = count // 2
        self.chip = self.me // 2
        self.core = self.me - self.chip * 2
        self.other = 1 - self.core

    def chip_at(self, step):
        return lax.rem(self.chip + step + self.chips, self.chips)

    def index(self, step):
        return self.chip_at(step) * 2 + self.core

    def device(self, step):
        return {"seq": self.index(step)}

    def partner(self):
        return {"seq": self.chip * 2 + self.other}


def gather_four(ring, full, send, recv):
    rows = full.shape[0]
    width = full.shape[1] // ring.count
    lo, hi = pl.ds(0, rows // 2), pl.ds(rows // 2, rows // 2)

    def block(half, step):
        return full.at[half, pl.ds(pl.multiple_of(ring.at(step) * width, 128), width)]

    def move(piece, slot, step):
        copy = remote(piece, piece, send.at[slot], recv.at[slot], ring.device(step))
        copy.start()
        return copy

    right_lo, left_hi = move(block(lo, 0), 0, 1), move(block(hi, 0), 1, -1)
    right_hi, left_lo = move(block(hi, 0), 2, 1), move(block(lo, 0), 3, -1)
    yield
    right_lo.wait_recv()
    relay_right = move(block(lo, -1), 4, 1)
    left_hi.wait_recv()
    relay_left = move(block(hi, 1), 5, -1)
    yield
    for copy in (right_hi, left_lo, relay_right, relay_left):
        copy.wait_recv()
    yield
    for copy in (right_lo, left_hi, right_hi, left_lo, relay_right, relay_left):
        copy.wait_send()


def gather_line(line, full, send, recv, to_core, from_core):
    rows = full.shape[1]
    cut = (rows // 2 + 15) // 16 * 16
    halves = {1: pl.ds(0, cut), -1: pl.ds(cut, rows - cut)}
    copies, hops, passed = [], {}, []

    def move(piece, s, r, device):
        copy = remote(piece, piece, s, r, device)
        copy.start()
        copies.append(copy)
        return copy

    last = line.chips // 2
    own = full.at[line.me]
    for way, d in ((0, 1), (1, -1)):
        hops[way] = move(own, send.at[way, 0], recv.at[way, 0], line.device(d))
    passed.append(move(own, to_core.at[0], from_core.at[0], line.partner()))
    yield
    slot = 1
    for hop in range(1, last + 1):
        earlier, passed = passed, []
        for way, d in ((0, 1), (1, -1)):
            hops[way].wait_recv()
            block = line.index(-d * hop)
            piece = full.at[block]
            if hop < last:
                ahead = piece if hop < last - 1 else full.at[block, halves[d], :]
                hops[way] = move(ahead, send.at[way, hop], recv.at[way, hop], line.device(d))
            else:
                piece = full.at[block, halves[d], :]
            passed.append(move(piece, to_core.at[slot], from_core.at[slot], line.partner()))
            slot += 1
        for copy in earlier:
            copy.wait_recv()
        yield
    for copy in passed:
        copy.wait_recv()
    yield
    for copy in copies:
        copy.wait_send()


def gather_line_scratch(chips):
    last = chips // 2
    return [
        pltpu.SemaphoreType.DMA((2, last)),
        pltpu.SemaphoreType.DMA((2, last)),
        pltpu.SemaphoreType.DMA((2 * last + 1,)),
        pltpu.SemaphoreType.DMA((2 * last + 1,)),
    ]


def scatter_four(ring, in_ref, buf, stage, send, recv, finish):
    rows = in_ref.shape[0]
    width = in_ref.shape[1] // ring.count
    lo, hi = pl.ds(0, rows // 2), pl.ds(rows // 2, rows // 2)

    def block(half, step):
        return in_ref.at[half, pl.ds(pl.multiple_of(ring.at(step) * width, 128), width)]

    def move(src, slot, step):
        copy = remote(src, buf.at[slot], send.at[slot], recv.at[slot], ring.device(step))
        copy.start()
        return copy

    copies = [
        move(block(lo, 2), 0, 1),
        move(block(hi, 2), 1, -1),
        move(block(hi, 1), 2, 1),
        move(block(lo, -1), 3, -1),
    ]
    yield
    copies[0].wait_recv()
    stage[0] = (buf[0].astype(F32) + block(lo, 1)[...].astype(F32)).astype(BF16)
    copies.append(move(stage.at[0], 4, 1))
    yield
    copies[1].wait_recv()
    stage[1] = (buf[1].astype(F32) + block(hi, -1)[...].astype(F32)).astype(BF16)
    copies.append(move(stage.at[1], 5, -1))
    yield
    copies[2].wait_recv()
    copies[5].wait_recv()
    finish(hi, block(hi, 0)[...].astype(F32) + buf[2].astype(F32) + buf[5].astype(F32))
    yield
    copies[3].wait_recv()
    copies[4].wait_recv()
    finish(lo, block(lo, 0)[...].astype(F32) + buf[3].astype(F32) + buf[4].astype(F32))
    yield
    for copy in copies:
        copy.wait_send()


def scatter_four_scratch(rows, width):
    return [
        pltpu.VMEM((6, rows // 2, width), BF16),
        pltpu.VMEM((2, rows // 2, width), BF16),
        pltpu.SemaphoreType.DMA((6,)),
        pltpu.SemaphoreType.DMA((6,)),
    ]


def scatter_line(line, in_ref, other, buf, stage, send, recv, to_core, from_core, finish, paced=False):
    rows = in_ref.shape[1]
    last = line.chips // 2
    halves = (pl.ds(0, rows // 2), pl.ds(rows // 2, rows // 2))
    groups = [[last]] + [[k, -k] for k in range(last - 1, 0, -1)] + [[0]]
    pieces, copies, ready, sent = {}, [], set(), {}

    def offer(group):
        for step in group:
            slot = len(pieces)
            chip = line.chip_at(step)
            copy = remote(
                in_ref.at[chip * 2 + line.other], other.at[chip], to_core.at[slot], from_core.at[slot], line.partner()
            )
            copy.start()
            copies.append(copy)
            pieces[step] = copy

    def own(step, half):
        if abs(step) == last:
            step = last
        if step not in ready:
            pieces[step].wait_recv()
            ready.add(step)
        chip = line.chip_at(step)
        return in_ref[chip * 2 + line.core, half, :].astype(F32) + other[chip, half, :].astype(F32)

    def ahead(k, which):
        for way, d in ((0, 1), (1, -1)):
            part = which if way == 0 else 1 - which
            half = halves[part]
            value = own(d * k, half)
            if (way, k + 1, part) in sent:
                sent[way, k + 1, part].wait_recv()
                value = value + buf[way, k, half, :].astype(F32)
            stage[way, k - 1, half, :] = value.astype(BF16)
            copy = remote(
                stage.at[way, k - 1, half, :],
                buf.at[way, k - 1, half, :],
                send.at[way, k - 1, part],
                recv.at[way, k - 1, part],
                line.device(d),
            )
            copy.start()
            sent[way, k, part] = copy
            copies.append(copy)
            yield

    plan = [[(last, 0)]] + [[(k, 1), (k, 0)] for k in range(last - 1, 0, -1)]
    if paced:
        offer(groups[0])
        yield
        for group, steps in zip(groups[1:], plan):
            offer(group)
            for step in steps:
                for _ in ahead(*step):
                    pass
            yield
    else:
        for group in groups:
            offer(group)
        yield
        for steps in plan:
            for step in steps:
                yield from ahead(*step)
    for part in (1, 0):
        half = halves[part]
        value = own(0, half)
        for way in (0, 1):
            sent[way, 1, part].wait_recv()
            value = value + buf[way, 0, half, :].astype(F32)
        finish(half, value)
        yield
    for copy in copies:
        copy.wait_send()


def scatter_line_scratch(chips, rows, width):
    last = chips // 2
    return [
        pltpu.VMEM((chips, rows, width), BF16),
        pltpu.VMEM((2, last, rows, width), BF16),
        pltpu.VMEM((2, last, rows, width), BF16),
        pltpu.SemaphoreType.DMA((2, last, 2)),
        pltpu.SemaphoreType.DMA((2, last, 2)),
        pltpu.SemaphoreType.DMA((chips,)),
        pltpu.SemaphoreType.DMA((chips,)),
    ]


def step_kernel(
    tp, seq, section,
    docs_ref, h_ref, mem_ref, cot_ref, wq_any, wo_any, kvw_any,
    passed_ref, gin_ref, gmem_ref, gwq_ref, gwo_ref, gself_ref, gcache_ref,
    full_h, full_s, full_c, wq, wo, kvw,
    q_raw, kv_raw, all_kv, q_unit, dout, weights, scores, delta_all, acc, dq, attn, gq, hout,
    proj, rows_part, source_part, dkv, part_q, part_o, part_kv, sums, mine, got,
    load, gather_send, gather_recv, pass_send, pass_recv, ex_send, ex_recv, ex_local,
    *scratch,
):
    line_gather, scratch = scratch[:4], scratch[4:]
    four = [scratch[4 * k : 4 * k + 4] for k in range(3)]
    scratch = scratch[12:]
    lines = [scratch[7 * k : 7 * k + 7] for k in range(4)]
    ring, line, sections = Ring("tp", tp), Line(seq), Ring("section", section)
    me = line.me
    is_self = sections.me == 0
    rows, width = h_ref.shape
    model = width * tp
    heads = wq.shape[1] // HEAD_DIM

    def cols(step):
        return pl.ds(pl.multiple_of(ring.at(step) * width, 128), width)

    own_h = pltpu.make_async_copy(h_ref, full_h.at[:, cols(0)], load.at[0])
    own_c = pltpu.make_async_copy(cot_ref, full_c.at[:, cols(0)], load.at[1])
    source_self = pltpu.make_async_copy(h_ref, full_s.at[:, cols(0)], load.at[2])
    source_cross = pltpu.make_async_copy(mem_ref, full_s.at[:, cols(0)], load.at[2])

    @pl.when(is_self)
    def _():
        source_self.start()

    @pl.when(jnp.logical_not(is_self))
    def _():
        source_cross.start()

    own_h.start()
    own_c.start()
    load_kvw = pltpu.make_async_copy(kvw_any, kvw, load.at[3])
    load_wq = pltpu.make_async_copy(wq_any, wq, load.at[4])
    load_wo = pltpu.make_async_copy(wo_any, wo, load.at[5])
    load_kvw.start()
    load_wq.start()
    load_wo.start()
    greet(
        [ring.device(1), ring.device(-1), line.device(1), line.device(-1), line.partner()]
        + [sections.device(k) for k in range(1, section)]
    )
    gather_s, gather_h, gather_c = [
        gather_four(ring, full, gather_send.at[k], gather_recv.at[k])
        for k, full in enumerate((full_s, full_h, full_c))
    ]
    keys = gather_line(line, all_kv, *line_gather)
    blocks = [pl.ds(k * width, width) for k in range(tp)]

    def factor(full):
        total = jnp.zeros((rows, 128), F32)
        for span in blocks:
            wide = full[:, span].astype(F32)
            wide = wide * wide
            for first in range(0, width, 128):
                total += wide[:, first : first + 128]
        return lax.rsqrt(jnp.sum(total, axis=1, keepdims=True) / model + EPS)

    def head_rows(head):
        return pl.ds(head * rows, rows)

    def head_cols(head):
        return pl.ds(head * HEAD_DIM, HEAD_DIM)

    source_self.wait()
    next(gather_s)
    own_h.wait()
    own_c.wait()
    acc[...] = jnp.zeros_like(acc)
    dq[...] = jnp.zeros_like(dq)
    low_chip = jnp.where(is_self, jnp.maximum(line.chip - WIN // (2 * rows), 0), 0)
    zero_chunk = jnp.zeros((2 * rows, 2 * HEAD_DIM), BF16).reshape(2, rows, 2 * HEAD_DIM)

    @pl.loop(0, low_chip)
    def _(j):
        dkv[pl.ds(2 * j, 2)] = zero_chunk

    @pl.loop(line.chip + 1, line.chips)
    def _(j):
        dkv[pl.ds(2 * j, 2)] = zero_chunk

    load_kvw.wait()
    next(gather_s)
    next(gather_h)
    next(gather_s)
    rs = factor(full_s)
    kv = nn(full_s[:, blocks[0]], kvw[blocks[0], :])
    for span in blocks[1:]:
        kv += nn(full_s[:, span], kvw[span, :])
    kv = kv * rs
    kv_raw[...] = kv
    key, value = kv[:, :HEAD_DIM], kv[:, HEAD_DIM:]
    unit = key * lax.rsqrt(jnp.sum(key * key, axis=1, keepdims=True) + EPS)
    all_kv[me, 0:rows, 0:HEAD_DIM] = unit.astype(BF16)
    all_kv[me, 0:rows, HEAD_DIM:] = value.astype(BF16)
    doc_lane = lax.broadcasted_iota(jnp.int32, (DOC_ROWS, 2 * BLK), 1)
    docs = jnp.where(doc_lane < BLK, docs_ref[0, 0], docs_ref[0, 1])
    all_kv[me, rows:, :] = docs.astype(F32).astype(BF16)
    next(keys)
    next(gather_h)
    next(gather_c)
    load_wq.wait()
    next(keys)
    next(keys)
    next(gather_h)
    rh = factor(full_h)
    q = nn(full_h[:, blocks[0]], wq[blocks[0], :])
    for span in blocks[1:]:
        q += nn(full_h[:, span], wq[span, :])
    q_raw[...] = q * rh
    for head in range(heads):
        part = q_raw[:, head_cols(head)]
        unit = part * lax.rsqrt(jnp.sum(part * part, axis=1, keepdims=True) + EPS)
        q_unit[head_rows(head), :] = unit.astype(BF16)
    row = lax.broadcasted_iota(jnp.int32, (rows, 1), 0)
    lane = lax.broadcasted_iota(jnp.int32, (1, rows), 1)
    query_doc = jnp.where(row < BLK, docs_ref[0, 0], docs_ref[0, 1]).astype(F32)
    query_pos = me * rows + row
    upper = jnp.where(is_self, query_pos, query_pos // BLK * BLK + BLK - 1)
    lower = jnp.where(is_self, query_pos - WIN, -1)
    ones = jnp.ones((2 * rows, HEAD_DIM), BF16)

    def for_chips(hop, body):
        count = 1 if hop % (line.chips // 2) == 0 else 2

        @pl.loop(0, count)
        def _(turn):
            chip = line.chip_at(hop * (1 - 2 * turn))

            @pl.when((chip >= low_chip) & (chip <= line.chip))
            def _():
                body(chip)

    def forward(chip):
        sides = [2 * chip, 2 * chip + 1]
        value = jnp.concatenate([all_kv[j, 0:rows, HEAD_DIM:] for j in sides], axis=0)
        value = jnp.concatenate([value, ones], axis=1)
        seen = []
        for j in sides:
            key_doc = all_kv[j, rows:, :].astype(F32)[0:1, :]
            key_pos = j * rows + lane
            seen.append((key_doc == query_doc) & (key_pos <= upper) & (key_pos > lower))
        for head in range(heads):
            parts = []
            for side, j in enumerate(sides):
                score = nt(q_unit[head_rows(head), :], all_kv[j, 0:rows, 0:HEAD_DIM])
                weight = jnp.where(seen[side], jnp.exp2(score * EXP2_SCALE), 0.0).astype(BF16)
                weights[chip, head_rows(head), side * rows : (side + 1) * rows] = weight
                parts.append(weight)
            acc[head_rows(head), :] += nn(jnp.concatenate(parts, axis=1), value)

    next(keys)
    for_chips(0, forward)
    next(gather_c)
    next(keys)
    for_chips(1, forward)
    for_chips(2, forward)
    next(keys)
    for_chips(3, forward)
    for_chips(4, forward)
    for head in range(heads):
        total = acc[head_rows(head), :]
        attn[:, head_cols(head)] = (total[:, :HEAD_DIM] * (1.0 / total[:, HEAD_DIM:])).astype(BF16)
    load_wo.wait()
    attn_now = attn[...]
    for span in blocks:
        proj[:, span] = nn(attn_now, wo[:, span]).astype(BF16)

    def finish_rows(half, value):
        hout[half, :] = (full_h[half, cols(0)].astype(F32) + value).astype(BF16)

    def finish_input(half, value):
        gin_ref[half, :] = (full_c[half, cols(0)].astype(F32) + value).astype(BF16)

    def finish_memory(half, value):
        gmem_ref[half, :] = value.astype(BF16)

    def finish_keys(half, value):
        sums[half, :] = value

    def finish_wq(half, value):
        gwq_ref[half, :] = value

    def finish_wo(half, value):
        gwo_ref[half, :] = value

    def finish_kv(half, value):
        mine[half, :] = value

    red_hout = scatter_four(ring, proj, *four[0], finish_rows)
    next(red_hout)
    next(gather_c)
    grad = nt(full_c[:, blocks[0]], wo[:, blocks[0]])
    for span in blocks[1:]:
        grad += nt(full_c[:, span], wo[:, span])
    share = part_o.shape[1]
    per_block = width // share
    for k, span in enumerate(blocks):
        value = tn(full_c[:, span], attn_now).astype(BF16)
        part_o[k * per_block : (k + 1) * per_block] = value.reshape(per_block, share, value.shape[1])
    red_wo = scatter_line(line, part_o, *lines[0], finish_wo)
    next(red_wo)
    deltas = []
    for head in range(heads):
        inverse = 1.0 / acc[head_rows(head), HEAD_DIM:]
        part = grad[:, head * HEAD_DIM : (head + 1) * HEAD_DIM].astype(BF16).astype(F32)
        delta = jnp.sum(part * attn[:, head_cols(head)].astype(F32), axis=1, keepdims=True)
        dout[head_rows(head), :] = (part * inverse).astype(BF16)
        deltas.append(delta * inverse[:, 0:1])

    def advance(stream, times):
        for _ in range(times):
            next(stream, None)

    delta_all[...] = jnp.concatenate([jnp.broadcast_to(d, (rows, 128)) for d in deltas], axis=0)

    def backward(chip):
        sides = [2 * chip, 2 * chip + 1]
        key = jnp.concatenate([all_kv[j, 0:rows, 0:HEAD_DIM] for j in sides], axis=0)
        for head in range(heads):
            part = dout[head_rows(head), :]
            delta = delta_all[head_rows(head), 0:1]
            for side, j in enumerate(sides):
                span = pl.ds(side * rows, rows)
                grad_prob = nt(part, all_kv[j, 0:rows, HEAD_DIM:])
                weight = weights[chip, head_rows(head), span].astype(F32)
                scores[head_rows(head), span] = (weight * (grad_prob - delta)).astype(BF16)
        dq[...] += nn(scores[...], key)
        grad_key = (SCALE * tn(q_unit[...], scores[...])).T
        grad_value = tn(dout[...], weights[chip]).T
        for side, j in enumerate(sides):
            part = slice(side * rows, (side + 1) * rows)
            dkv[j, :, 0:HEAD_DIM] = grad_key[part].astype(BF16)
            dkv[j, :, HEAD_DIM:] = grad_value[part].astype(BF16)

    red_keys = scatter_line(line, dkv, *lines[1], finish_keys, paced=True)
    for hop in range(line.chips // 2, -1, -1):
        for_chips(hop, backward)
        next(red_keys)
        if hop:
            advance(red_hout, 2)
            advance(red_wo, 3)
    pass_on = pass_along(sections, hout, passed_ref, pass_send, pass_recv)
    next(pass_on)

    total = jnp.zeros((rows, 1), F32)
    scaled = []
    for head in range(heads):
        part = q_raw[:, head_cols(head)]
        slope = SCALE * dq[head_rows(head), :]
        inverse = lax.rsqrt(jnp.sum(part * part, axis=1, keepdims=True) + EPS)
        along = jnp.sum(part * slope, axis=1, keepdims=True)
        value = (inverse * slope - part * (inverse * inverse * inverse * along)).astype(BF16)
        gq[:, head_cols(head)] = value
        total += jnp.sum(value.astype(F32) * part, axis=1, keepdims=True)
        scaled.append((value.astype(F32) * rh).astype(BF16))
    scaled_q = jnp.concatenate(scaled, axis=1)
    fix = rh * rh * total / model
    for span in blocks:
        value = nt(gq[...], wq[span, :]) * rh - full_h[:, span].astype(F32) * fix
        rows_part[:, span] = value.astype(BF16)
    red_rows = scatter_four(ring, rows_part, *four[1], finish_input)
    next(red_rows)
    for k, span in enumerate(blocks):
        value = tn(full_h[:, span], scaled_q).astype(BF16)
        part_q[k * per_block : (k + 1) * per_block] = value.reshape(per_block, share, value.shape[1])
        advance(red_wo, 1)
    red_wq = scatter_line(line, part_q, *lines[2], finish_wq)
    advance(red_keys, 2)
    next(red_wq)
    summed = sums[...]
    kv = kv_raw[...]
    key, slope = kv[:, :HEAD_DIM], summed[:, :HEAD_DIM]
    inverse = lax.rsqrt(jnp.sum(key * key, axis=1, keepdims=True) + EPS)
    along = jnp.sum(key * slope, axis=1, keepdims=True)
    slope = inverse * slope - key * (inverse * inverse * inverse * along)
    both = jnp.concatenate([slope, summed[:, HEAD_DIM:]], axis=1).astype(BF16)
    total = jnp.sum(both.astype(F32) * kv, axis=1, keepdims=True)
    fix = rs * rs * total / model
    for span in blocks:
        value = nt(both, kvw[span, :]) * rs - full_s[:, span].astype(F32) * fix
        source_part[:, span] = value.astype(BF16)
    red_source = scatter_four(ring, source_part, *four[2], finish_memory)
    next(red_source)
    scaled_kv = (both.astype(F32) * rs).astype(BF16)
    for k, span in enumerate(blocks):
        value = tn(full_s[:, span], scaled_kv).astype(BF16)
        part_kv[k * per_block : (k + 1) * per_block] = value.reshape(per_block, share, value.shape[1])
        next(red_wo, None)
        next(red_wq, None)
    red_kv = scatter_line(line, part_kv, *lines[3], finish_kv)
    run_together(red_kv, red_wq, red_source, red_rows, red_wo, red_keys)

    piece = gself_ref.shape[0]
    copies = []
    for k in range(1, section):
        first = pl.multiple_of(sections.at(k) * piece, 8)
        copy = remote(
            mine.at[pl.ds(first, piece), :], got.at[sections.me], ex_send.at[k], ex_recv.at[k], sections.device(k)
        )
        copy.start()
        copies.append(copy)
    first = pl.multiple_of(sections.me * piece, 8)
    local = pltpu.make_async_copy(mine.at[pl.ds(first, piece), :], got.at[sections.me], ex_local)
    local.start()
    run_together(pass_on, red_hout, gather_s, gather_h, gather_c, keys)
    for copy in copies:
        copy.wait_recv()
    local.wait()
    gself_ref[...] = got[0]
    total = got[1]
    for k in range(2, section):
        total = total + got[k]
    gcache_ref[...] = total
    for copy in copies:
        copy.wait_send()


def pass_along(ring, in_ref, out_ref, send, recv):
    copy = remote(in_ref, out_ref, send, recv, ring.device(1))
    copy.start()
    yield
    copy.wait()


def whole_step(tp, seq, section, docs, hidden, memory, cot, wq, wo, kvw):
    rows, width = hidden.shape
    model, cols = wq.shape
    heads = cols // HEAD_DIM
    kv = kvw.shape[1]
    chips = seq // 2
    share = model // seq
    piece = share // section
    small = jax.ShapeDtypeStruct((rows, width), BF16)
    vmem = pltpu.VMEM
    dma = pltpu.SemaphoreType.DMA
    scratch = [
        vmem((rows, model), BF16), vmem((rows, model), BF16), vmem((rows, model), BF16),
        vmem((model, cols), BF16), vmem((cols, model), BF16), vmem((model, kv), BF16),
        vmem((rows, cols), F32), vmem((rows, kv), F32),
        vmem((seq, rows + DOC_ROWS, kv), BF16),
        vmem((heads * rows, HEAD_DIM), BF16), vmem((heads * rows, HEAD_DIM), BF16),
        vmem((chips, heads * rows, 2 * rows), BF16),
        vmem((heads * rows, 2 * rows), BF16), vmem((heads * rows, 128), F32),
        vmem((heads * rows, 2 * HEAD_DIM), F32), vmem((heads * rows, HEAD_DIM), F32),
        vmem((rows, cols), BF16), vmem((rows, cols), BF16), vmem((rows, width), BF16),
        vmem((rows, model), BF16), vmem((rows, model), BF16), vmem((rows, model), BF16),
        vmem((seq, rows, kv), BF16),
        vmem((seq, share, cols), BF16), vmem((seq, share, cols), BF16), vmem((seq, share, kv), BF16),
        vmem((rows, kv), F32), vmem((share, kv), F32), vmem((section, piece, kv), F32),
        dma((6,)), dma((3, 6)), dma((3, 6)), dma, dma, dma((section,)), dma((section,)), dma,
    ]
    scratch += gather_line_scratch(chips)
    for _ in range(3):
        scratch += scatter_four_scratch(rows, width)
    for shape in ((share, cols), (rows, kv), (share, cols), (share, kv)):
        scratch += scatter_line_scratch(chips, *shape)
    return pl.pallas_call(
        functools.partial(step_kernel, tp, seq, section),
        out_shape=(
            small, small, small,
            jax.ShapeDtypeStruct((share, cols), F32), jax.ShapeDtypeStruct((share, cols), F32),
            jax.ShapeDtypeStruct((piece, kv), F32), jax.ShapeDtypeStruct((piece, kv), F32),
        ),
        in_specs=[SMEM_SPEC] + [ANY_SPEC] * 6,
        out_specs=[VMEM_SPEC] * 7,
        scratch_shapes=scratch,
        compiler_params=pltpu.CompilerParams(
            collective_id=1, has_side_effects=True, vmem_limit_bytes=VMEM_LIMIT
        ),
        name="step",
    )(docs, hidden, memory, cot, wq, wo, kvw)


def finish_kernel(passed, gin, gmem, gwq, gwo, gself, gcache, *outs):
    for source, target in zip((passed, gin, gmem, gwq, gwo), outs[:5]):
        target[...] = source[...]
    for source, target in ((gself, outs[5]), (gcache, outs[6])):
        half = source.shape[1] // 2
        target[:, 0, :] = source[:, :half]
        target[:, 1, :] = source[:, half:]


def finish(results):
    shapes = [jax.ShapeDtypeStruct(x.shape, x.dtype) for x in results[:5]]
    for x in results[5:]:
        shapes.append(jax.ShapeDtypeStruct((x.shape[0], 2, x.shape[1] // 2), F32))
    return pl.pallas_call(
        finish_kernel,
        out_shape=tuple(shapes),
        in_specs=[VMEM_SPEC] * 7,
        out_specs=[VMEM_SPEC] * 7,
        name="finish",
    )(*results)


def on_device(
    tp, seq, section, h_in, memory, cotangent, block_docs, w_query, w_out, self_weight, cache_weight
):
    is_self = lax.axis_index("section") == 0
    width = w_query.shape[1]
    kvw = jnp.where(is_self, self_weight, cache_weight).reshape(width, -1)
    results = whole_step(
        tp, seq, section, block_docs, h_in[0], memory[0], cotangent[0], w_query[0], w_out[0], kvw
    )
    passed, gin, gmem, gwq, gwo, gself, gcache = finish(results)
    return (passed[None], gin[None], gmem[None], gwq[None], gwo.T[None], gself, gcache)


def solution(mesh):
    sizes = mesh.shape
    return jax.shard_map(
        functools.partial(on_device, sizes["tp"], sizes["seq"], sizes["section"]),
        mesh=mesh,
        in_specs=(
            P("section", "seq", "tp"),
            P("section", "seq", "tp"),
            P("section", "seq", "tp"),
            P("section", "seq"),
            P("section", None, "tp"),
            P("section", "tp", None),
            P(None, None, "tp"),
            P(None, None, "tp"),
        ),
        out_specs=(
            P("section", "seq", "tp"),
            P("section", "seq", "tp"),
            P("section", "seq", "tp"),
            P("section", "seq", "tp"),
            P("section", "tp", "seq"),
            P(("seq", "section"), None, "tp"),
            P(("seq", "section"), None, "tp"),
        ),
        check_vma=False,
    )
```

```python
import functools
import math

import jax
import jax.numpy as jnp
from jax import lax
from jax.experimental import pallas as pl
from jax.experimental.pallas import tpu as pltpu
from jax.sharding import PartitionSpec as P

MESH = pl.DeviceIdType.MESH
HEAD_DIM = 128
BLK = 128
WIN = 1024
SCALE = 40.0
EPS = 1e-06
EXP2_SCALE = SCALE * math.log2(math.e)
F32 = jnp.float32
BF16 = jnp.bfloat16
DOC_ROWS = 16
VMEM_SPEC = pl.BlockSpec(memory_space=pltpu.VMEM)
ANY_SPEC = pl.BlockSpec(memory_space=pl.ANY)
SMEM_SPEC = pl.BlockSpec(memory_space=pltpu.SMEM)
VMEM_LIMIT = 60 * 1024 * 1024


def nt(left, right):
    return lax.dot_general(left, right, (((1,), (1,)), ((), ())), preferred_element_type=F32)


def nn(left, right):
    return lax.dot_general(left, right, (((1,), (0,)), ((), ())), preferred_element_type=F32)


def tn(left, right):
    return lax.dot_general(left, right, (((0,), (0,)), ((), ())), preferred_element_type=F32)


def remote(src, dst, send_sem, recv_sem, device):
    return pltpu.make_async_remote_copy(
        src_ref=src,
        dst_ref=dst,
        send_sem=send_sem,
        recv_sem=recv_sem,
        device_id=device,
        device_id_type=MESH,
    )


def greet(devices):
    barrier = pltpu.get_barrier_semaphore()
    for device in devices:
        pl.semaphore_signal(barrier, inc=1, device_id=device, device_id_type=MESH)
    pl.semaphore_wait(barrier, len(devices))


def run_together(*streams):
    live = list(streams)
    while live:
        for stream in list(live):
            try:
                next(stream)
            except StopIteration:
                live.remove(stream)


class Ring:
    def __init__(self, axis, count):
        self.axis = axis
        self.me = lax.axis_index(axis)
        self.count = count

    def at(self, step):
        return lax.rem(self.me + step + self.count, self.count)

    def device(self, step):
        return {self.axis: self.at(step)}


class Line:
    def __init__(self, count):
        self.me = lax.axis_index("seq")
        self.chips = count // 2
        self.chip = self.me // 2
        self.core = self.me - self.chip * 2
        self.other = 1 - self.core

    def chip_at(self, step):
        return lax.rem(self.chip + step + self.chips, self.chips)

    def index(self, step):
        return self.chip_at(step) * 2 + self.core

    def device(self, step):
        return {"seq": self.index(step)}

    def partner(self):
        return {"seq": self.chip * 2 + self.other}


def gather_four(ring, full, send, recv):
    rows = full.shape[0]
    width = full.shape[1] // ring.count
    lo, hi = pl.ds(0, rows // 2), pl.ds(rows // 2, rows // 2)

    def block(half, step):
        return full.at[half, pl.ds(pl.multiple_of(ring.at(step) * width, 128), width)]

    def move(piece, slot, step):
        copy = remote(piece, piece, send.at[slot], recv.at[slot], ring.device(step))
        copy.start()
        return copy

    right_lo, left_hi = move(block(lo, 0), 0, 1), move(block(hi, 0), 1, -1)
    right_hi, left_lo = move(block(hi, 0), 2, 1), move(block(lo, 0), 3, -1)
    yield
    right_lo.wait_recv()
    relay_right = move(block(lo, -1), 4, 1)
    left_hi.wait_recv()
    relay_left = move(block(hi, 1), 5, -1)
    yield
    for copy in (right_hi, left_lo, relay_right, relay_left):
        copy.wait_recv()
    yield
    for copy in (right_lo, left_hi, right_hi, left_lo, relay_right, relay_left):
        copy.wait_send()


def gather_line(line, full, send, recv, to_core, from_core):
    rows = full.shape[1]
    cut = (rows // 2 + 15) // 16 * 16
    halves = {1: pl.ds(0, cut), -1: pl.ds(cut, rows - cut)}
    copies, hops, passed = [], {}, []

    def move(piece, s, r, device):
        copy = remote(piece, piece, s, r, device)
        copy.start()
        copies.append(copy)
        return copy

    last = line.chips // 2
    own = full.at[line.me]
    for way, d in ((0, 1), (1, -1)):
        hops[way] = move(own, send.at[way, 0], recv.at[way, 0], line.device(d))
    passed.append(move(own, to_core.at[0], from_core.at[0], line.partner()))
    yield
    slot = 1
    for hop in range(1, last + 1):
        earlier, passed = passed, []
        for way, d in ((0, 1), (1, -1)):
            hops[way].wait_recv()
            block = line.index(-d * hop)
            piece = full.at[block]
            if hop < last:
                ahead = piece if hop < last - 1 else full.at[block, halves[d], :]
                hops[way] = move(ahead, send.at[way, hop], recv.at[way, hop], line.device(d))
            else:
                piece = full.at[block, halves[d], :]
            passed.append(move(piece, to_core.at[slot], from_core.at[slot], line.partner()))
            slot += 1
        for copy in earlier:
            copy.wait_recv()
        yield
    for copy in passed:
        copy.wait_recv()
    yield
    for copy in copies:
        copy.wait_send()


def gather_line_scratch(chips):
    last = chips // 2
    return [
        pltpu.SemaphoreType.DMA((2, last)),
        pltpu.SemaphoreType.DMA((2, last)),
        pltpu.SemaphoreType.DMA((2 * last + 1,)),
        pltpu.SemaphoreType.DMA((2 * last + 1,)),
    ]


def scatter_four(ring, in_ref, buf, stage, send, recv, finish):
    rows = in_ref.shape[0]
    width = in_ref.shape[1] // ring.count
    lo, hi = pl.ds(0, rows // 2), pl.ds(rows // 2, rows // 2)

    def block(half, step):
        return in_ref.at[half, pl.ds(pl.multiple_of(ring.at(step) * width, 128), width)]

    def move(src, slot, step):
        copy = remote(src, buf.at[slot], send.at[slot], recv.at[slot], ring.device(step))
        copy.start()
        return copy

    copies = [
        move(block(lo, 2), 0, 1),
        move(block(hi, 2), 1, -1),
        move(block(hi, 1), 2, 1),
        move(block(lo, -1), 3, -1),
    ]
    yield
    copies[0].wait_recv()
    stage[0] = (buf[0].astype(F32) + block(lo, 1)[...].astype(F32)).astype(BF16)
    copies.append(move(stage.at[0], 4, 1))
    yield
    copies[1].wait_recv()
    stage[1] = (buf[1].astype(F32) + block(hi, -1)[...].astype(F32)).astype(BF16)
    copies.append(move(stage.at[1], 5, -1))
    yield
    copies[2].wait_recv()
    copies[5].wait_recv()
    finish(hi, block(hi, 0)[...].astype(F32) + buf[2].astype(F32) + buf[5].astype(F32))
    yield
    copies[3].wait_recv()
    copies[4].wait_recv()
    finish(lo, block(lo, 0)[...].astype(F32) + buf[3].astype(F32) + buf[4].astype(F32))
    yield
    for copy in copies:
        copy.wait_send()


def scatter_four_scratch(rows, width):
    return [
        pltpu.VMEM((6, rows // 2, width), BF16),
        pltpu.VMEM((2, rows // 2, width), BF16),
        pltpu.SemaphoreType.DMA((6,)),
        pltpu.SemaphoreType.DMA((6,)),
    ]


def scatter_line(line, in_ref, other, buf, stage, send, recv, to_core, from_core, finish, paced=False):
    rows = in_ref.shape[1]
    last = line.chips // 2
    halves = (pl.ds(0, rows // 2), pl.ds(rows // 2, rows // 2))
    groups = [[last]] + [[k, -k] for k in range(last - 1, 0, -1)] + [[0]]
    pieces, copies, ready, sent = {}, [], set(), {}

    def offer(group):
        for step in group:
            slot = len(pieces)
            chip = line.chip_at(step)
            copy = remote(
                in_ref.at[chip * 2 + line.other], other.at[chip], to_core.at[slot], from_core.at[slot], line.partner()
            )
            copy.start()
            copies.append(copy)
            pieces[step] = copy

    def own(step, half):
        if abs(step) == last:
            step = last
        if step not in ready:
            pieces[step].wait_recv()
            ready.add(step)
        chip = line.chip_at(step)
        return in_ref[chip * 2 + line.core, half, :].astype(F32) + other[chip, half, :].astype(F32)

    def ahead(k, which):
        for way, d in ((0, 1), (1, -1)):
            part = which if way == 0 else 1 - which
            half = halves[part]
            value = own(d * k, half)
            if (way, k + 1, part) in sent:
                sent[way, k + 1, part].wait_recv()
                value = value + buf[way, k, half, :].astype(F32)
            stage[way, k - 1, half, :] = value.astype(BF16)
            copy = remote(
                stage.at[way, k - 1, half, :],
                buf.at[way, k - 1, half, :],
                send.at[way, k - 1, part],
                recv.at[way, k - 1, part],
                line.device(d),
            )
            copy.start()
            sent[way, k, part] = copy
            copies.append(copy)
            yield

    plan = [[(last, 0)]] + [[(k, 1), (k, 0)] for k in range(last - 1, 0, -1)]
    if paced:
        offer(groups[0])
        yield
        for group, steps in zip(groups[1:], plan):
            offer(group)
            for step in steps:
                for _ in ahead(*step):
                    pass
            yield
    else:
        for group in groups:
            offer(group)
        yield
        for steps in plan:
            for step in steps:
                yield from ahead(*step)
    for part in (1, 0):
        half = halves[part]
        value = own(0, half)
        for way in (0, 1):
            sent[way, 1, part].wait_recv()
            value = value + buf[way, 0, half, :].astype(F32)
        finish(half, value)
        yield
    for copy in copies:
        copy.wait_send()


def scatter_line_scratch(chips, rows, width):
    last = chips // 2
    return [
        pltpu.VMEM((chips, rows, width), BF16),
        pltpu.VMEM((2, last, rows, width), BF16),
        pltpu.VMEM((2, last, rows, width), BF16),
        pltpu.SemaphoreType.DMA((2, last, 2)),
        pltpu.SemaphoreType.DMA((2, last, 2)),
        pltpu.SemaphoreType.DMA((chips,)),
        pltpu.SemaphoreType.DMA((chips,)),
    ]


def step_kernel(
    tp, seq, section,
    docs_ref, h_ref, mem_ref, cot_ref, wq_any, wo_any, kvw_any,
    passed_ref, gin_ref, gmem_ref, gwq_ref, gwo_ref, gself_ref, gcache_ref,
    full_h, full_s, full_c, wq, wo, kvw,
    q_raw, kv_raw, all_kv, q_unit, dout, weights, scores, delta_all, acc, dq, attn, gq, hout,
    proj, rows_part, source_part, dkv, part_q, part_o, part_kv, sums, mine, got,
    load, gather_send, gather_recv, pass_send, pass_recv, ex_send, ex_recv, ex_local,
    *scratch,
):
    line_gather, scratch = scratch[:4], scratch[4:]
    four = [scratch[4 * k : 4 * k + 4] for k in range(3)]
    scratch = scratch[12:]
    lines = [scratch[7 * k : 7 * k + 7] for k in range(4)]
    ring, line, sections = Ring("tp", tp), Line(seq), Ring("section", section)
    me = line.me
    is_self = sections.me == 0
    rows, width = h_ref.shape
    model = width * tp
    heads = wq.shape[1] // HEAD_DIM

    def cols(step):
        return pl.ds(pl.multiple_of(ring.at(step) * width, 128), width)

    own_h = pltpu.make_async_copy(h_ref, full_h.at[:, cols(0)], load.at[0])
    own_c = pltpu.make_async_copy(cot_ref, full_c.at[:, cols(0)], load.at[1])
    source_self = pltpu.make_async_copy(h_ref, full_s.at[:, cols(0)], load.at[2])
    source_cross = pltpu.make_async_copy(mem_ref, full_s.at[:, cols(0)], load.at[2])

    @pl.when(is_self)
    def _():
        source_self.start()

    @pl.when(jnp.logical_not(is_self))
    def _():
        source_cross.start()

    own_h.start()
    own_c.start()
    load_kvw = pltpu.make_async_copy(kvw_any, kvw, load.at[3])
    load_wq = pltpu.make_async_copy(wq_any, wq, load.at[4])
    load_wo = pltpu.make_async_copy(wo_any, wo, load.at[5])
    load_kvw.start()
    load_wq.start()
    load_wo.start()
    greet(
        [ring.device(1), ring.device(-1), line.device(1), line.device(-1), line.partner()]
        + [sections.device(k) for k in range(1, section)]
    )
    gather_s, gather_h, gather_c = [
        gather_four(ring, full, gather_send.at[k], gather_recv.at[k])
        for k, full in enumerate((full_s, full_h, full_c))
    ]
    keys = gather_line(line, all_kv, *line_gather)
    blocks = [pl.ds(k * width, width) for k in range(tp)]

    def factor(full):
        total = jnp.zeros((rows, 128), F32)
        for span in blocks:
            wide = full[:, span].astype(F32)
            wide = wide * wide
            for first in range(0, width, 128):
                total += wide[:, first : first + 128]
        return lax.rsqrt(jnp.sum(total, axis=1, keepdims=True) / model + EPS)

    def head_rows(head):
        return pl.ds(head * rows, rows)

    def head_cols(head):
        return pl.ds(head * HEAD_DIM, HEAD_DIM)

    source_self.wait()
    next(gather_s)
    own_h.wait()
    own_c.wait()
    acc[...] = jnp.zeros_like(acc)
    dq[...] = jnp.zeros_like(dq)
    low_chip = jnp.where(is_self, jnp.maximum(line.chip - WIN // (2 * rows), 0), 0)
    zero_chunk = jnp.zeros((2 * rows, 2 * HEAD_DIM), BF16).reshape(2, rows, 2 * HEAD_DIM)

    @pl.loop(0, low_chip)
    def _(j):
        dkv[pl.ds(2 * j, 2)] = zero_chunk

    @pl.loop(line.chip + 1, line.chips)
    def _(j):
        dkv[pl.ds(2 * j, 2)] = zero_chunk

    load_kvw.wait()
    next(gather_s)
    next(gather_h)
    next(gather_s)
    rs = factor(full_s)
    kv = nn(full_s[:, blocks[0]], kvw[blocks[0], :])
    for span in blocks[1:]:
        kv += nn(full_s[:, span], kvw[span, :])
    kv = kv * rs
    kv_raw[...] = kv
    key, value = kv[:, :HEAD_DIM], kv[:, HEAD_DIM:]
    unit = key * lax.rsqrt(jnp.sum(key * key, axis=1, keepdims=True) + EPS)
    all_kv[me, 0:rows, 0:HEAD_DIM] = unit.astype(BF16)
    all_kv[me, 0:rows, HEAD_DIM:] = value.astype(BF16)
    doc_lane = lax.broadcasted_iota(jnp.int32, (DOC_ROWS, 2 * BLK), 1)
    docs = jnp.where(doc_lane < BLK, docs_ref[0, 0], docs_ref[0, 1])
    all_kv[me, rows:, :] = docs.astype(F32).astype(BF16)
    next(keys)
    next(gather_h)
    next(gather_c)
    load_wq.wait()
    next(keys)
    next(keys)
    next(gather_h)
    rh = factor(full_h)
    q = nn(full_h[:, blocks[0]], wq[blocks[0], :])
    for span in blocks[1:]:
        q += nn(full_h[:, span], wq[span, :])
    q_raw[...] = q * rh
    for head in range(heads):
        part = q_raw[:, head_cols(head)]
        unit = part * lax.rsqrt(jnp.sum(part * part, axis=1, keepdims=True) + EPS)
        q_unit[head_rows(head), :] = unit.astype(BF16)
    row = lax.broadcasted_iota(jnp.int32, (rows, 1), 0)
    lane = lax.broadcasted_iota(jnp.int32, (1, rows), 1)
    query_doc = jnp.where(row < BLK, docs_ref[0, 0], docs_ref[0, 1]).astype(F32)
    query_pos = me * rows + row
    upper = jnp.where(is_self, query_pos, query_pos // BLK * BLK + BLK - 1)
    lower = jnp.where(is_self, query_pos - WIN, -1)
    ones = jnp.ones((2 * rows, HEAD_DIM), BF16)

    def for_chips(hop, body):
        count = 1 if hop % (line.chips // 2) == 0 else 2

        @pl.loop(0, count)
        def _(turn):
            chip = line.chip_at(hop * (1 - 2 * turn))

            @pl.when((chip >= low_chip) & (chip <= line.chip))
            def _():
                body(chip)

    def forward(chip):
        sides = [2 * chip, 2 * chip + 1]
        value = jnp.concatenate([all_kv[j, 0:rows, HEAD_DIM:] for j in sides], axis=0)
        value = jnp.concatenate([value, ones], axis=1)
        seen = []
        for j in sides:
            key_doc = all_kv[j, rows:, :].astype(F32)[0:1, :]
            key_pos = j * rows + lane
            seen.append((key_doc == query_doc) & (key_pos <= upper) & (key_pos > lower))
        for head in range(heads):
            parts = []
            for side, j in enumerate(sides):
                score = nt(q_unit[head_rows(head), :], all_kv[j, 0:rows, 0:HEAD_DIM])
                weight = jnp.where(seen[side], jnp.exp2(score * EXP2_SCALE), 0.0).astype(BF16)
                weights[chip, head_rows(head), side * rows : (side + 1) * rows] = weight
                parts.append(weight)
            acc[head_rows(head), :] += nn(jnp.concatenate(parts, axis=1), value)

    next(keys)
    for_chips(0, forward)
    next(gather_c)
    next(keys)
    for_chips(1, forward)
    for_chips(2, forward)
    next(keys)
    for_chips(3, forward)
    for_chips(4, forward)
    for head in range(heads):
        total = acc[head_rows(head), :]
        attn[:, head_cols(head)] = (total[:, :HEAD_DIM] * (1.0 / total[:, HEAD_DIM:])).astype(BF16)
    load_wo.wait()
    attn_now = attn[...]
    for span in blocks:
        proj[:, span] = nn(attn_now, wo[:, span]).astype(BF16)

    def finish_rows(half, value):
        hout[half, :] = (full_h[half, cols(0)].astype(F32) + value).astype(BF16)

    def finish_input(half, value):
        gin_ref[half, :] = (full_c[half, cols(0)].astype(F32) + value).astype(BF16)

    def finish_memory(half, value):
        gmem_ref[half, :] = value.astype(BF16)

    def finish_keys(half, value):
        sums[half, :] = value

    def finish_wq(half, value):
        gwq_ref[half, :] = value

    def finish_wo(half, value):
        gwo_ref[half, :] = value

    def finish_kv(half, value):
        mine[half, :] = value

    red_hout = scatter_four(ring, proj, *four[0], finish_rows)
    next(red_hout)
    next(gather_c)
    grad = nt(full_c[:, blocks[0]], wo[:, blocks[0]])
    for span in blocks[1:]:
        grad += nt(full_c[:, span], wo[:, span])
    share = part_o.shape[1]
    per_block = width // share
    for k, span in enumerate(blocks):
        value = tn(full_c[:, span], attn_now).astype(BF16)
        part_o[k * per_block : (k + 1) * per_block] = value.reshape(per_block, share, value.shape[1])
    red_wo = scatter_line(line, part_o, *lines[0], finish_wo)
    deltas = []
    for head in range(heads):
        inverse = 1.0 / acc[head_rows(head), HEAD_DIM:]
        part = grad[:, head * HEAD_DIM : (head + 1) * HEAD_DIM].astype(BF16).astype(F32)
        delta = jnp.sum(part * attn[:, head_cols(head)].astype(F32), axis=1, keepdims=True)
        dout[head_rows(head), :] = (part * inverse).astype(BF16)
        deltas.append(delta * inverse[:, 0:1])

    def advance(stream, times):
        for _ in range(times):
            next(stream, None)

    delta_all[...] = jnp.concatenate([jnp.broadcast_to(d, (rows, 128)) for d in deltas], axis=0)

    def backward(chip):
        sides = [2 * chip, 2 * chip + 1]
        key = jnp.concatenate([all_kv[j, 0:rows, 0:HEAD_DIM] for j in sides], axis=0)
        for head in range(heads):
            part = dout[head_rows(head), :]
            delta = delta_all[head_rows(head), 0:1]
            for side, j in enumerate(sides):
                span = pl.ds(side * rows, rows)
                grad_prob = nt(part, all_kv[j, 0:rows, HEAD_DIM:])
                weight = weights[chip, head_rows(head), span].astype(F32)
                scores[head_rows(head), span] = (weight * (grad_prob - delta)).astype(BF16)
        dq[...] += nn(scores[...], key)
        grad_key = (SCALE * tn(q_unit[...], scores[...])).T
        grad_value = tn(dout[...], weights[chip]).T
        for side, j in enumerate(sides):
            part = slice(side * rows, (side + 1) * rows)
            dkv[j, :, 0:HEAD_DIM] = grad_key[part].astype(BF16)
            dkv[j, :, HEAD_DIM:] = grad_value[part].astype(BF16)

    red_keys = scatter_line(line, dkv, *lines[1], finish_keys, paced=True)
    for hop in range(line.chips // 2, -1, -1):
        for_chips(hop, backward)
        next(red_keys)
        if hop == 2:
            advance(red_hout, 2)
    next(red_wo)

    total = jnp.zeros((rows, 1), F32)
    scaled = []
    for head in range(heads):
        part = q_raw[:, head_cols(head)]
        slope = SCALE * dq[head_rows(head), :]
        inverse = lax.rsqrt(jnp.sum(part * part, axis=1, keepdims=True) + EPS)
        along = jnp.sum(part * slope, axis=1, keepdims=True)
        value = (inverse * slope - part * (inverse * inverse * inverse * along)).astype(BF16)
        gq[:, head_cols(head)] = value
        total += jnp.sum(value.astype(F32) * part, axis=1, keepdims=True)
        scaled.append((value.astype(F32) * rh).astype(BF16))
    scaled_q = jnp.concatenate(scaled, axis=1)
    fix = rh * rh * total / model
    for span in blocks:
        value = nt(gq[...], wq[span, :]) * rh - full_h[:, span].astype(F32) * fix
        rows_part[:, span] = value.astype(BF16)
    red_rows = scatter_four(ring, rows_part, *four[1], finish_input)
    next(red_rows)
    advance(red_wo, 2)
    advance(red_hout, 2)
    pass_on = pass_along(sections, hout, passed_ref, pass_send, pass_recv)
    next(pass_on)
    for k, span in enumerate(blocks):
        value = tn(full_h[:, span], scaled_q).astype(BF16)
        part_q[k * per_block : (k + 1) * per_block] = value.reshape(per_block, share, value.shape[1])
    red_wq = scatter_line(line, part_q, *lines[2], finish_wq)
    next(red_wq)
    advance(red_keys, 2)
    summed = sums[...]
    kv = kv_raw[...]
    key, slope = kv[:, :HEAD_DIM], summed[:, :HEAD_DIM]
    inverse = lax.rsqrt(jnp.sum(key * key, axis=1, keepdims=True) + EPS)
    along = jnp.sum(key * slope, axis=1, keepdims=True)
    slope = inverse * slope - key * (inverse * inverse * inverse * along)
    both = jnp.concatenate([slope, summed[:, HEAD_DIM:]], axis=1).astype(BF16)
    total = jnp.sum(both.astype(F32) * kv, axis=1, keepdims=True)
    fix = rs * rs * total / model
    for span in blocks:
        value = nt(both, kvw[span, :]) * rs - full_s[:, span].astype(F32) * fix
        source_part[:, span] = value.astype(BF16)
    red_source = scatter_four(ring, source_part, *four[2], finish_memory)
    next(red_source)
    advance(red_wo, 4)
    advance(red_wq, 2)
    advance(red_rows, 2)
    scaled_kv = (both.astype(F32) * rs).astype(BF16)
    for k, span in enumerate(blocks):
        value = tn(full_s[:, span], scaled_kv).astype(BF16)
        part_kv[k * per_block : (k + 1) * per_block] = value.reshape(per_block, share, value.shape[1])
    red_kv = scatter_line(line, part_kv, *lines[3], finish_kv)
    next(red_kv)
    advance(red_wo, 4)
    advance(red_kv, 2)
    advance(red_wq, 4)
    advance(red_kv, 4)
    advance(red_wo, 4)
    advance(red_rows, 2)
    advance(red_wq, 4)
    advance(red_kv, 4)
    advance(red_source, 2)
    advance(red_wq, 4)
    advance(red_kv, 4)
    advance(red_wo, 2)
    advance(red_kv, 2)
    piece = gself_ref.shape[0]
    copies = []
    for k in range(1, section):
        first = pl.multiple_of(sections.at(k) * piece, 8)
        copy = remote(
            mine.at[pl.ds(first, piece), :], got.at[sections.me], ex_send.at[k], ex_recv.at[k], sections.device(k)
        )
        copy.start()
        copies.append(copy)
    first = pl.multiple_of(sections.me * piece, 8)
    local = pltpu.make_async_copy(mine.at[pl.ds(first, piece), :], got.at[sections.me], ex_local)
    local.start()
    advance(red_wq, 2)
    run_together(red_source, pass_on, red_rows, red_hout, gather_s, gather_h, gather_c, keys)
    run_together(red_keys, red_wo, red_wq, red_kv)
    for copy in copies:
        copy.wait_recv()
    local.wait()
    gself_ref[...] = got[0]
    total = got[1]
    for k in range(2, section):
        total = total + got[k]
    gcache_ref[...] = total
    for copy in copies:
        copy.wait_send()


def pass_along(ring, in_ref, out_ref, send, recv):
    copy = remote(in_ref, out_ref, send, recv, ring.device(1))
    copy.start()
    yield
    copy.wait()


def whole_step(tp, seq, section, docs, hidden, memory, cot, wq, wo, kvw):
    rows, width = hidden.shape
    model, cols = wq.shape
    heads = cols // HEAD_DIM
    kv = kvw.shape[1]
    chips = seq // 2
    share = model // seq
    piece = share // section
    small = jax.ShapeDtypeStruct((rows, width), BF16)
    vmem = pltpu.VMEM
    dma = pltpu.SemaphoreType.DMA
    scratch = [
        vmem((rows, model), BF16), vmem((rows, model), BF16), vmem((rows, model), BF16),
        vmem((model, cols), BF16), vmem((cols, model), BF16), vmem((model, kv), BF16),
        vmem((rows, cols), F32), vmem((rows, kv), F32),
        vmem((seq, rows + DOC_ROWS, kv), BF16),
        vmem((heads * rows, HEAD_DIM), BF16), vmem((heads * rows, HEAD_DIM), BF16),
        vmem((chips, heads * rows, 2 * rows), BF16),
        vmem((heads * rows, 2 * rows), BF16), vmem((heads * rows, 128), F32),
        vmem((heads * rows, 2 * HEAD_DIM), F32), vmem((heads * rows, HEAD_DIM), F32),
        vmem((rows, cols), BF16), vmem((rows, cols), BF16), vmem((rows, width), BF16),
        vmem((rows, model), BF16), vmem((rows, model), BF16), vmem((rows, model), BF16),
        vmem((seq, rows, kv), BF16),
        vmem((seq, share, cols), BF16), vmem((seq, share, cols), BF16), vmem((seq, share, kv), BF16),
        vmem((rows, kv), F32), vmem((share, kv), F32), vmem((section, piece, kv), F32),
        dma((6,)), dma((3, 6)), dma((3, 6)), dma, dma, dma((section,)), dma((section,)), dma,
    ]
    scratch += gather_line_scratch(chips)
    for _ in range(3):
        scratch += scatter_four_scratch(rows, width)
    for shape in ((share, cols), (rows, kv), (share, cols), (share, kv)):
        scratch += scatter_line_scratch(chips, *shape)
    return pl.pallas_call(
        functools.partial(step_kernel, tp, seq, section),
        out_shape=(
            small, small, small,
            jax.ShapeDtypeStruct((share, cols), F32), jax.ShapeDtypeStruct((share, cols), F32),
            jax.ShapeDtypeStruct((piece, kv), F32), jax.ShapeDtypeStruct((piece, kv), F32),
        ),
        in_specs=[SMEM_SPEC] + [ANY_SPEC] * 6,
        out_specs=[VMEM_SPEC] * 7,
        scratch_shapes=scratch,
        compiler_params=pltpu.CompilerParams(
            collective_id=1, has_side_effects=True, vmem_limit_bytes=VMEM_LIMIT
        ),
        name="step",
    )(docs, hidden, memory, cot, wq, wo, kvw)


def finish_kernel(passed, gin, gmem, gwq, gwo, gself, gcache, *outs):
    for source, target in zip((passed, gin, gmem, gwq, gwo), outs[:5]):
        target[...] = source[...]
    for source, target in ((gself, outs[5]), (gcache, outs[6])):
        half = source.shape[1] // 2
        target[:, 0, :] = source[:, :half]
        target[:, 1, :] = source[:, half:]


def finish(results):
    shapes = [jax.ShapeDtypeStruct(x.shape, x.dtype) for x in results[:5]]
    for x in results[5:]:
        shapes.append(jax.ShapeDtypeStruct((x.shape[0], 2, x.shape[1] // 2), F32))
    return pl.pallas_call(
        finish_kernel,
        out_shape=tuple(shapes),
        in_specs=[VMEM_SPEC] * 7,
        out_specs=[VMEM_SPEC] * 7,
        name="finish",
    )(*results)


def on_device(
    tp, seq, section, h_in, memory, cotangent, block_docs, w_query, w_out, self_weight, cache_weight
):
    is_self = lax.axis_index("section") == 0
    width = w_query.shape[1]
    kvw = jnp.where(is_self, self_weight, cache_weight).reshape(width, -1)
    results = whole_step(
        tp, seq, section, block_docs, h_in[0], memory[0], cotangent[0], w_query[0], w_out[0], kvw
    )
    passed, gin, gmem, gwq, gwo, gself, gcache = finish(results)
    return (passed[None], gin[None], gmem[None], gwq[None], gwo.T[None], gself, gcache)


def solution(mesh):
    sizes = mesh.shape
    return jax.shard_map(
        functools.partial(on_device, sizes["tp"], sizes["seq"], sizes["section"]),
        mesh=mesh,
        in_specs=(
            P("section", "seq", "tp"),
            P("section", "seq", "tp"),
            P("section", "seq", "tp"),
            P("section", "seq"),
            P("section", None, "tp"),
            P("section", "tp", None),
            P(None, None, "tp"),
            P(None, None, "tp"),
        ),
        out_specs=(
            P("section", "seq", "tp"),
            P("section", "seq", "tp"),
            P("section", "seq", "tp"),
            P("section", "seq", "tp"),
            P("section", "tp", "seq"),
            P(("seq", "section"), None, "tp"),
            P(("seq", "section"), None, "tp"),
        ),
        check_vma=False,
    )
```

```python
import functools
import math

import jax
import jax.numpy as jnp
from jax import lax
from jax.experimental import pallas as pl
from jax.experimental.pallas import tpu as pltpu
from jax.sharding import PartitionSpec as P

MESH = pl.DeviceIdType.MESH
HEAD_DIM = 128
BLK = 128
WIN = 1024
SCALE = 40.0
EPS = 1e-06
EXP2_SCALE = SCALE * math.log2(math.e)
F32 = jnp.float32
BF16 = jnp.bfloat16
DOC_ROWS = 16
VMEM_SPEC = pl.BlockSpec(memory_space=pltpu.VMEM)
ANY_SPEC = pl.BlockSpec(memory_space=pl.ANY)
SMEM_SPEC = pl.BlockSpec(memory_space=pltpu.SMEM)
VMEM_LIMIT = 60 * 1024 * 1024


def nt(left, right):
    return lax.dot_general(left, right, (((1,), (1,)), ((), ())), preferred_element_type=F32)


def nn(left, right):
    return lax.dot_general(left, right, (((1,), (0,)), ((), ())), preferred_element_type=F32)


def tn(left, right):
    return lax.dot_general(left, right, (((0,), (0,)), ((), ())), preferred_element_type=F32)


def remote(src, dst, send_sem, recv_sem, device):
    return pltpu.make_async_remote_copy(
        src_ref=src,
        dst_ref=dst,
        send_sem=send_sem,
        recv_sem=recv_sem,
        device_id=device,
        device_id_type=MESH,
    )


def greet(devices):
    barrier = pltpu.get_barrier_semaphore()
    for device in devices:
        pl.semaphore_signal(barrier, inc=1, device_id=device, device_id_type=MESH)
    pl.semaphore_wait(barrier, len(devices))


def run_together(*streams):
    live = list(streams)
    while live:
        for stream in list(live):
            try:
                next(stream)
            except StopIteration:
                live.remove(stream)


class Ring:
    def __init__(self, axis, count):
        self.axis = axis
        self.me = lax.axis_index(axis)
        self.count = count

    def at(self, step):
        return lax.rem(self.me + step + self.count, self.count)

    def device(self, step):
        return {self.axis: self.at(step)}


class Line:
    def __init__(self, count):
        self.me = lax.axis_index("seq")
        self.chips = count // 2
        self.chip = self.me // 2
        self.core = self.me - self.chip * 2
        self.other = 1 - self.core

    def chip_at(self, step):
        return lax.rem(self.chip + step + self.chips, self.chips)

    def index(self, step):
        return self.chip_at(step) * 2 + self.core

    def device(self, step):
        return {"seq": self.index(step)}

    def partner(self):
        return {"seq": self.chip * 2 + self.other}


def gather_four(ring, full, send, recv):
    rows = full.shape[0]
    width = full.shape[1] // ring.count
    lo, hi = pl.ds(0, rows // 2), pl.ds(rows // 2, rows // 2)

    def block(half, step):
        return full.at[half, pl.ds(pl.multiple_of(ring.at(step) * width, 128), width)]

    def move(piece, slot, step):
        copy = remote(piece, piece, send.at[slot], recv.at[slot], ring.device(step))
        copy.start()
        return copy

    right_lo, left_hi = move(block(lo, 0), 0, 1), move(block(hi, 0), 1, -1)
    right_hi, left_lo = move(block(hi, 0), 2, 1), move(block(lo, 0), 3, -1)
    yield
    right_lo.wait_recv()
    relay_right = move(block(lo, -1), 4, 1)
    left_hi.wait_recv()
    relay_left = move(block(hi, 1), 5, -1)
    yield
    for copy in (right_hi, left_lo, relay_right, relay_left):
        copy.wait_recv()
    yield
    for copy in (right_lo, left_hi, right_hi, left_lo, relay_right, relay_left):
        copy.wait_send()


def gather_line(line, full, send, recv, to_core, from_core):
    rows = full.shape[1]
    cut = (rows // 2 + 15) // 16 * 16
    halves = {1: pl.ds(0, cut), -1: pl.ds(cut, rows - cut)}
    copies, hops, passed = [], {}, []

    def move(piece, s, r, device):
        copy = remote(piece, piece, s, r, device)
        copy.start()
        copies.append(copy)
        return copy

    last = line.chips // 2
    own = full.at[line.me]
    for way, d in ((0, 1), (1, -1)):
        hops[way] = move(own, send.at[way, 0], recv.at[way, 0], line.device(d))
    passed.append(move(own, to_core.at[0], from_core.at[0], line.partner()))
    yield
    slot = 1
    for hop in range(1, last + 1):
        earlier, passed = passed, []
        for way, d in ((0, 1), (1, -1)):
            hops[way].wait_recv()
            block = line.index(-d * hop)
            piece = full.at[block]
            if hop < last:
                ahead = piece if hop < last - 1 else full.at[block, halves[d], :]
                hops[way] = move(ahead, send.at[way, hop], recv.at[way, hop], line.device(d))
            else:
                piece = full.at[block, halves[d], :]
            passed.append(move(piece, to_core.at[slot], from_core.at[slot], line.partner()))
            slot += 1
        for copy in earlier:
            copy.wait_recv()
        yield
    for copy in passed:
        copy.wait_recv()
    yield
    for copy in copies:
        copy.wait_send()


def gather_line_scratch(chips):
    last = chips // 2
    return [
        pltpu.SemaphoreType.DMA((2, last)),
        pltpu.SemaphoreType.DMA((2, last)),
        pltpu.SemaphoreType.DMA((2 * last + 1,)),
        pltpu.SemaphoreType.DMA((2 * last + 1,)),
    ]


def scatter_four(ring, in_ref, buf, stage, send, recv, finish):
    rows = in_ref.shape[0]
    width = in_ref.shape[1] // ring.count
    lo, hi = pl.ds(0, rows // 2), pl.ds(rows // 2, rows // 2)

    def block(half, step):
        return in_ref.at[half, pl.ds(pl.multiple_of(ring.at(step) * width, 128), width)]

    def move(src, slot, step):
        copy = remote(src, buf.at[slot], send.at[slot], recv.at[slot], ring.device(step))
        copy.start()
        return copy

    copies = [
        move(block(lo, 2), 0, 1),
        move(block(hi, 2), 1, -1),
        move(block(hi, 1), 2, 1),
        move(block(lo, -1), 3, -1),
    ]
    yield
    copies[0].wait_recv()
    stage[0] = (buf[0].astype(F32) + block(lo, 1)[...].astype(F32)).astype(BF16)
    copies.append(move(stage.at[0], 4, 1))
    yield
    copies[1].wait_recv()
    stage[1] = (buf[1].astype(F32) + block(hi, -1)[...].astype(F32)).astype(BF16)
    copies.append(move(stage.at[1], 5, -1))
    yield
    copies[2].wait_recv()
    copies[5].wait_recv()
    finish(hi, block(hi, 0)[...].astype(F32) + buf[2].astype(F32) + buf[5].astype(F32))
    yield
    copies[3].wait_recv()
    copies[4].wait_recv()
    finish(lo, block(lo, 0)[...].astype(F32) + buf[3].astype(F32) + buf[4].astype(F32))
    yield
    for copy in copies:
        copy.wait_send()


def scatter_four_scratch(rows, width):
    return [
        pltpu.VMEM((6, rows // 2, width), BF16),
        pltpu.VMEM((2, rows // 2, width), BF16),
        pltpu.SemaphoreType.DMA((6,)),
        pltpu.SemaphoreType.DMA((6,)),
    ]


def scatter_line(line, in_ref, other, buf, stage, send, recv, to_core, from_core, finish, paced=False):
    rows = in_ref.shape[1]
    last = line.chips // 2
    halves = (pl.ds(0, rows // 2), pl.ds(rows // 2, rows // 2))
    groups = [[last]] + [[k, -k] for k in range(last - 1, 0, -1)] + [[0]]
    pieces, copies, ready, sent = {}, [], set(), {}

    def offer(group):
        for step in group:
            slot = len(pieces)
            chip = line.chip_at(step)
            copy = remote(
                in_ref.at[chip * 2 + line.other], other.at[chip], to_core.at[slot], from_core.at[slot], line.partner()
            )
            copy.start()
            copies.append(copy)
            pieces[step] = copy

    def own(step, half):
        if abs(step) == last:
            step = last
        if step not in ready:
            pieces[step].wait_recv()
            ready.add(step)
        chip = line.chip_at(step)
        return in_ref[chip * 2 + line.core, half, :].astype(F32) + other[chip, half, :].astype(F32)

    def ahead(k, which):
        for way, d in ((0, 1), (1, -1)):
            part = which if way == 0 else 1 - which
            half = halves[part]
            value = own(d * k, half)
            if (way, k + 1, part) in sent:
                sent[way, k + 1, part].wait_recv()
                value = value + buf[way, k, half, :].astype(F32)
            stage[way, k - 1, half, :] = value.astype(BF16)
            copy = remote(
                stage.at[way, k - 1, half, :],
                buf.at[way, k - 1, half, :],
                send.at[way, k - 1, part],
                recv.at[way, k - 1, part],
                line.device(d),
            )
            copy.start()
            sent[way, k, part] = copy
            copies.append(copy)
            yield

    plan = [[(last, 0)]] + [[(k, 1), (k, 0)] for k in range(last - 1, 0, -1)]
    if paced:
        offer(groups[0])
        yield
        for group, steps in zip(groups[1:], plan):
            offer(group)
            for step in steps:
                for _ in ahead(*step):
                    pass
            yield
    else:
        for group in groups:
            offer(group)
        yield
        for steps in plan:
            for step in steps:
                yield from ahead(*step)
    for part in (1, 0):
        half = halves[part]
        value = own(0, half)
        for way in (0, 1):
            sent[way, 1, part].wait_recv()
            value = value + buf[way, 0, half, :].astype(F32)
        finish(half, value)
        yield
    for copy in copies:
        copy.wait_send()


def scatter_line_scratch(chips, rows, width):
    last = chips // 2
    return [
        pltpu.VMEM((chips, rows, width), BF16),
        pltpu.VMEM((2, last, rows, width), BF16),
        pltpu.VMEM((2, last, rows, width), BF16),
        pltpu.SemaphoreType.DMA((2, last, 2)),
        pltpu.SemaphoreType.DMA((2, last, 2)),
        pltpu.SemaphoreType.DMA((chips,)),
        pltpu.SemaphoreType.DMA((chips,)),
    ]


def step_kernel(
    tp, seq, section,
    docs_ref, h_ref, mem_ref, cot_ref, wq_any, wo_any, self_any, cache_any,
    passed_out, gin_out, gmem_out, gwq_out, gwo_out, gself_out, gcache_out,
    passed_ref, gin_ref, gmem_ref, gwq_ref, gwo_ref, gself_ref, gcache_ref, store,
    kv_pair, full_h, full_s, full_c, wq, wo, kvw,
    q_raw, kv_raw, all_kv, q_unit, dout, weights, scores, delta_all, acc, dq, attn, gq, hout,
    proj, rows_part, source_part, dkv, part_q, part_o, part_kv, sums, mine, got,
    load, gather_send, gather_recv, pass_send, pass_recv, ex_send, ex_recv, ex_local,
    *scratch,
):
    line_gather, scratch = scratch[:4], scratch[4:]
    four = [scratch[4 * k : 4 * k + 4] for k in range(3)]
    scratch = scratch[12:]
    lines = [scratch[7 * k : 7 * k + 7] for k in range(4)]
    ring, line, sections = Ring("tp", tp), Line(seq), Ring("section", section)
    me = line.me
    is_self = sections.me == 0
    rows, width = h_ref.shape
    model = width * tp
    heads = wq.shape[1] // HEAD_DIM

    def cols(step):
        return pl.ds(pl.multiple_of(ring.at(step) * width, 128), width)

    own_h = pltpu.make_async_copy(h_ref, full_h.at[:, cols(0)], load.at[0])
    own_c = pltpu.make_async_copy(cot_ref, full_c.at[:, cols(0)], load.at[1])
    source_self = pltpu.make_async_copy(h_ref, full_s.at[:, cols(0)], load.at[2])
    source_cross = pltpu.make_async_copy(mem_ref, full_s.at[:, cols(0)], load.at[2])

    kvw_self = pltpu.make_async_copy(self_any, kv_pair, load.at[3])
    kvw_cross = pltpu.make_async_copy(cache_any, kv_pair, load.at[3])

    @pl.when(is_self)
    def _():
        source_self.start()
        kvw_self.start()

    @pl.when(jnp.logical_not(is_self))
    def _():
        source_cross.start()
        kvw_cross.start()

    own_h.start()
    own_c.start()
    load_wq = pltpu.make_async_copy(wq_any, wq, load.at[4])
    load_wo = pltpu.make_async_copy(wo_any, wo, load.at[5])
    load_wq.start()
    load_wo.start()
    greet(
        [ring.device(1), ring.device(-1), line.device(1), line.device(-1), line.partner()]
        + [sections.device(k) for k in range(1, section)]
    )
    gather_s, gather_h, gather_c = [
        gather_four(ring, full, gather_send.at[k], gather_recv.at[k])
        for k, full in enumerate((full_s, full_h, full_c))
    ]
    keys = gather_line(line, all_kv, *line_gather)
    blocks = [pl.ds(k * width, width) for k in range(tp)]

    def factor(full):
        total = jnp.zeros((rows, 128), F32)
        for span in blocks:
            wide = full[:, span].astype(F32)
            wide = wide * wide
            for first in range(0, width, 128):
                total += wide[:, first : first + 128]
        return lax.rsqrt(jnp.sum(total, axis=1, keepdims=True) / model + EPS)

    def head_rows(head):
        return pl.ds(head * rows, rows)

    def head_cols(head):
        return pl.ds(head * HEAD_DIM, HEAD_DIM)

    source_self.wait()
    next(gather_s)
    own_h.wait()
    own_c.wait()
    acc[...] = jnp.zeros_like(acc)
    dq[...] = jnp.zeros_like(dq)
    low_chip = jnp.where(is_self, jnp.maximum(line.chip - WIN // (2 * rows), 0), 0)
    zero_chunk = jnp.zeros((2 * rows, 2 * HEAD_DIM), BF16).reshape(2, rows, 2 * HEAD_DIM)

    @pl.loop(0, low_chip)
    def _(j):
        dkv[pl.ds(2 * j, 2)] = zero_chunk

    @pl.loop(line.chip + 1, line.chips)
    def _(j):
        dkv[pl.ds(2 * j, 2)] = zero_chunk

    kvw_self.wait()
    pairs = 256

    @pl.loop(0, model // pairs)
    def _(k):
        span = pl.ds(k * pairs, pairs)
        kvw[span, :] = kv_pair[span].reshape(pairs, kvw.shape[1])

    next(gather_s)
    next(gather_h)
    next(gather_s)
    rs = factor(full_s)
    kv = nn(full_s[:, blocks[0]], kvw[blocks[0], :])
    for span in blocks[1:]:
        kv += nn(full_s[:, span], kvw[span, :])
    kv = kv * rs
    kv_raw[...] = kv
    key, value = kv[:, :HEAD_DIM], kv[:, HEAD_DIM:]
    unit = key * lax.rsqrt(jnp.sum(key * key, axis=1, keepdims=True) + EPS)
    all_kv[me, 0:rows, 0:HEAD_DIM] = unit.astype(BF16)
    all_kv[me, 0:rows, HEAD_DIM:] = value.astype(BF16)
    doc_lane = lax.broadcasted_iota(jnp.int32, (DOC_ROWS, 2 * BLK), 1)
    docs = jnp.where(doc_lane < BLK, docs_ref[0, 0], docs_ref[0, 1])
    all_kv[me, rows:, :] = docs.astype(F32).astype(BF16)
    next(keys)
    next(gather_h)
    next(gather_c)
    load_wq.wait()
    next(keys)
    next(keys)
    next(gather_h)
    rh = factor(full_h)
    q = nn(full_h[:, blocks[0]], wq[blocks[0], :])
    for span in blocks[1:]:
        q += nn(full_h[:, span], wq[span, :])
    q_raw[...] = q * rh
    for head in range(heads):
        part = q_raw[:, head_cols(head)]
        unit = part * lax.rsqrt(jnp.sum(part * part, axis=1, keepdims=True) + EPS)
        q_unit[head_rows(head), :] = unit.astype(BF16)
    row = lax.broadcasted_iota(jnp.int32, (rows, 1), 0)
    lane = lax.broadcasted_iota(jnp.int32, (1, rows), 1)
    query_doc = jnp.where(row < BLK, docs_ref[0, 0], docs_ref[0, 1]).astype(F32)
    query_pos = me * rows + row
    upper = jnp.where(is_self, query_pos, query_pos // BLK * BLK + BLK - 1)
    lower = jnp.where(is_self, query_pos - WIN, -1)
    ones = jnp.ones((2 * rows, HEAD_DIM), BF16)

    def for_chips(hop, body):
        count = 1 if hop % (line.chips // 2) == 0 else 2

        @pl.loop(0, count)
        def _(turn):
            chip = line.chip_at(hop * (1 - 2 * turn))

            @pl.when((chip >= low_chip) & (chip <= line.chip))
            def _():
                body(chip)

    def forward(chip):
        sides = [2 * chip, 2 * chip + 1]
        value = jnp.concatenate([all_kv[j, 0:rows, HEAD_DIM:] for j in sides], axis=0)
        value = jnp.concatenate([value, ones], axis=1)
        seen = []
        for j in sides:
            key_doc = all_kv[j, rows:, :].astype(F32)[0:1, :]
            key_pos = j * rows + lane
            seen.append((key_doc == query_doc) & (key_pos <= upper) & (key_pos > lower))
        for head in range(heads):
            parts = []
            for side, j in enumerate(sides):
                score = nt(q_unit[head_rows(head), :], all_kv[j, 0:rows, 0:HEAD_DIM])
                weight = jnp.where(seen[side], jnp.exp2(score * EXP2_SCALE), 0.0).astype(BF16)
                weights[chip, head_rows(head), side * rows : (side + 1) * rows] = weight
                parts.append(weight)
            acc[head_rows(head), :] += nn(jnp.concatenate(parts, axis=1), value)

    next(keys)
    for_chips(0, forward)
    next(gather_c)
    next(keys)
    for_chips(1, forward)
    for_chips(2, forward)
    next(keys)
    for_chips(3, forward)
    for_chips(4, forward)
    for head in range(heads):
        total = acc[head_rows(head), :]
        attn[:, head_cols(head)] = (total[:, :HEAD_DIM] * (1.0 / total[:, HEAD_DIM:])).astype(BF16)
    load_wo.wait()
    attn_now = attn[...]
    for span in blocks:
        proj[:, span] = nn(attn_now, wo[:, span]).astype(BF16)

    def finish_rows(half, value):
        hout[half, :] = (full_h[half, cols(0)].astype(F32) + value).astype(BF16)

    def finish_input(half, value):
        gin_ref[half, :] = (full_c[half, cols(0)].astype(F32) + value).astype(BF16)

    def finish_memory(half, value):
        gmem_ref[half, :] = value.astype(BF16)

    def finish_keys(half, value):
        sums[half, :] = value

    def finish_wq(half, value):
        gwq_ref[half, :] = value

    def finish_wo(half, value):
        gwo_ref[half, :] = value

    def finish_kv(half, value):
        mine[half, :] = value

    red_hout = scatter_four(ring, proj, *four[0], finish_rows)
    next(red_hout)
    next(gather_c)
    grad = nt(full_c[:, blocks[0]], wo[:, blocks[0]])
    for span in blocks[1:]:
        grad += nt(full_c[:, span], wo[:, span])
    share = part_o.shape[1]
    per_block = width // share
    for k, span in enumerate(blocks):
        value = tn(full_c[:, span], attn_now).astype(BF16)
        part_o[k * per_block : (k + 1) * per_block] = value.reshape(per_block, share, value.shape[1])
    red_wo = scatter_line(line, part_o, *lines[0], finish_wo)
    deltas = []
    for head in range(heads):
        inverse = 1.0 / acc[head_rows(head), HEAD_DIM:]
        part = grad[:, head * HEAD_DIM : (head + 1) * HEAD_DIM].astype(BF16).astype(F32)
        delta = jnp.sum(part * attn[:, head_cols(head)].astype(F32), axis=1, keepdims=True)
        dout[head_rows(head), :] = (part * inverse).astype(BF16)
        deltas.append(delta * inverse[:, 0:1])

    def advance(stream, times):
        for _ in range(times):
            next(stream, None)

    delta_all[...] = jnp.concatenate([jnp.broadcast_to(d, (rows, 128)) for d in deltas], axis=0)

    def backward(chip):
        sides = [2 * chip, 2 * chip + 1]
        key = jnp.concatenate([all_kv[j, 0:rows, 0:HEAD_DIM] for j in sides], axis=0)
        for head in range(heads):
            part = dout[head_rows(head), :]
            delta = delta_all[head_rows(head), 0:1]
            for side, j in enumerate(sides):
                span = pl.ds(side * rows, rows)
                grad_prob = nt(part, all_kv[j, 0:rows, HEAD_DIM:])
                weight = weights[chip, head_rows(head), span].astype(F32)
                scores[head_rows(head), span] = (weight * (grad_prob - delta)).astype(BF16)
        dq[...] += nn(scores[...], key)
        grad_key = (SCALE * tn(q_unit[...], scores[...])).T
        grad_value = tn(dout[...], weights[chip]).T
        for side, j in enumerate(sides):
            part = slice(side * rows, (side + 1) * rows)
            dkv[j, :, 0:HEAD_DIM] = grad_key[part].astype(BF16)
            dkv[j, :, HEAD_DIM:] = grad_value[part].astype(BF16)

    red_keys = scatter_line(line, dkv, *lines[1], finish_keys, paced=True)
    for hop in range(line.chips // 2, -1, -1):
        for_chips(hop, backward)
        next(red_keys)
        if hop == 2:
            advance(red_hout, 2)
    next(red_wo)

    total = jnp.zeros((rows, 1), F32)
    scaled = []
    for head in range(heads):
        part = q_raw[:, head_cols(head)]
        slope = SCALE * dq[head_rows(head), :]
        inverse = lax.rsqrt(jnp.sum(part * part, axis=1, keepdims=True) + EPS)
        along = jnp.sum(part * slope, axis=1, keepdims=True)
        value = (inverse * slope - part * (inverse * inverse * inverse * along)).astype(BF16)
        gq[:, head_cols(head)] = value
        total += jnp.sum(value.astype(F32) * part, axis=1, keepdims=True)
        scaled.append((value.astype(F32) * rh).astype(BF16))
    scaled_q = jnp.concatenate(scaled, axis=1)
    fix = rh * rh * total / model
    for span in blocks:
        value = nt(gq[...], wq[span, :]) * rh - full_h[:, span].astype(F32) * fix
        rows_part[:, span] = value.astype(BF16)
    red_rows = scatter_four(ring, rows_part, *four[1], finish_input)
    next(red_rows)
    advance(red_wo, 2)
    advance(red_hout, 2)
    pass_on = pass_along(sections, hout, passed_ref, pass_send, pass_recv)
    next(pass_on)
    for k, span in enumerate(blocks):
        value = tn(full_h[:, span], scaled_q).astype(BF16)
        part_q[k * per_block : (k + 1) * per_block] = value.reshape(per_block, share, value.shape[1])
    red_wq = scatter_line(line, part_q, *lines[2], finish_wq)
    next(red_wq)
    advance(red_keys, 2)
    summed = sums[...]
    kv = kv_raw[...]
    key, slope = kv[:, :HEAD_DIM], summed[:, :HEAD_DIM]
    inverse = lax.rsqrt(jnp.sum(key * key, axis=1, keepdims=True) + EPS)
    along = jnp.sum(key * slope, axis=1, keepdims=True)
    slope = inverse * slope - key * (inverse * inverse * inverse * along)
    both = jnp.concatenate([slope, summed[:, HEAD_DIM:]], axis=1).astype(BF16)
    total = jnp.sum(both.astype(F32) * kv, axis=1, keepdims=True)
    fix = rs * rs * total / model
    for span in blocks:
        value = nt(both, kvw[span, :]) * rs - full_s[:, span].astype(F32) * fix
        source_part[:, span] = value.astype(BF16)
    red_source = scatter_four(ring, source_part, *four[2], finish_memory)
    next(red_source)
    advance(red_wo, 4)
    advance(red_wq, 2)
    advance(red_rows, 2)
    scaled_kv = (both.astype(F32) * rs).astype(BF16)
    for k, span in enumerate(blocks):
        value = tn(full_s[:, span], scaled_kv).astype(BF16)
        part_kv[k * per_block : (k + 1) * per_block] = value.reshape(per_block, share, value.shape[1])
    red_kv = scatter_line(line, part_kv, *lines[3], finish_kv)
    next(red_kv)
    advance(red_wo, 4)
    advance(red_kv, 2)
    advance(red_wq, 4)
    advance(red_kv, 4)
    advance(red_wo, 4)
    advance(red_rows, 2)
    advance(red_wq, 4)
    advance(red_kv, 4)
    advance(red_source, 2)
    advance(red_wq, 4)
    advance(red_kv, 4)
    advance(red_wo, 2)
    advance(red_kv, 2)
    local_refs = (passed_ref, gin_ref, gmem_ref, gwq_ref, gwo_ref, gself_ref, gcache_ref)
    outs = (passed_out, gin_out, gmem_out, gwq_out, gwo_out, gself_out, gcache_out)
    stores = [pltpu.make_async_copy(a, b, store.at[k]) for k, (a, b) in enumerate(zip(local_refs, outs))]
    stores[1].start()
    stores[4].start()
    piece = gself_ref.shape[0]
    copies = []
    for k in range(1, section):
        first = pl.multiple_of(sections.at(k) * piece, 8)
        copy = remote(
            mine.at[pl.ds(first, piece), :], got.at[sections.me], ex_send.at[k], ex_recv.at[k], sections.device(k)
        )
        copy.start()
        copies.append(copy)
    first = pl.multiple_of(sections.me * piece, 8)
    local = pltpu.make_async_copy(mine.at[pl.ds(first, piece), :], got.at[sections.me], ex_local)
    local.start()
    advance(red_wq, 2)
    stores[3].start()
    run_together(red_source, pass_on, red_rows, red_hout, gather_s, gather_h, gather_c, keys)
    stores[0].start()
    stores[2].start()
    run_together(red_keys, red_wo, red_wq, red_kv)
    for copy in copies:
        copy.wait_recv()
    local.wait()
    gself_ref[...] = got[0]
    total = got[1]
    for k in range(2, section):
        total = total + got[k]
    gcache_ref[...] = total
    stores[5].start()
    stores[6].start()
    for copy in copies:
        copy.wait_send()
    for copy in stores:
        copy.wait()


def pass_along(ring, in_ref, out_ref, send, recv):
    copy = remote(in_ref, out_ref, send, recv, ring.device(1))
    copy.start()
    yield
    copy.wait()


def whole_step(tp, seq, section, docs, hidden, memory, cot, wq, wo, self_w, cache_w):
    rows, width = hidden.shape
    model, cols = wq.shape
    heads = cols // HEAD_DIM
    kv = self_w.shape[1] * self_w.shape[2]
    chips = seq // 2
    share = model // seq
    piece = share // section
    vmem = pltpu.VMEM
    dma = pltpu.SemaphoreType.DMA
    outs = [((rows, width), BF16)] * 3 + [((share, cols), F32)] * 2 + [((piece, kv), F32)] * 2
    scratch = [vmem(*out) for out in outs] + [
        dma((7,)), vmem(self_w.shape, BF16),
        vmem((rows, model), BF16), vmem((rows, model), BF16), vmem((rows, model), BF16),
        vmem((model, cols), BF16), vmem((cols, model), BF16), vmem((model, kv), BF16),
        vmem((rows, cols), F32), vmem((rows, kv), F32),
        vmem((seq, rows + DOC_ROWS, kv), BF16),
        vmem((heads * rows, HEAD_DIM), BF16), vmem((heads * rows, HEAD_DIM), BF16),
        vmem((chips, heads * rows, 2 * rows), BF16),
        vmem((heads * rows, 2 * rows), BF16), vmem((heads * rows, 128), F32),
        vmem((heads * rows, 2 * HEAD_DIM), F32), vmem((heads * rows, HEAD_DIM), F32),
        vmem((rows, cols), BF16), vmem((rows, cols), BF16), vmem((rows, width), BF16),
        vmem((rows, model), BF16), vmem((rows, model), BF16), vmem((rows, model), BF16),
        vmem((seq, rows, kv), BF16),
        vmem((seq, share, cols), BF16), vmem((seq, share, cols), BF16), vmem((seq, share, kv), BF16),
        vmem((rows, kv), F32), vmem((share, kv), F32), vmem((section, piece, kv), F32),
        dma((6,)), dma((3, 6)), dma((3, 6)), dma, dma, dma((section,)), dma((section,)), dma,
    ]
    scratch += gather_line_scratch(chips)
    for _ in range(3):
        scratch += scatter_four_scratch(rows, width)
    for shape in ((share, cols), (rows, kv), (share, cols), (share, kv)):
        scratch += scatter_line_scratch(chips, *shape)
    return pl.pallas_call(
        functools.partial(step_kernel, tp, seq, section),
        out_shape=tuple(jax.ShapeDtypeStruct(*out) for out in outs),
        in_specs=[SMEM_SPEC] + [ANY_SPEC] * 7,
        out_specs=[ANY_SPEC] * 7,
        scratch_shapes=scratch,
        compiler_params=pltpu.CompilerParams(
            collective_id=1, has_side_effects=True, vmem_limit_bytes=VMEM_LIMIT
        ),
        name="step",
    )(docs, hidden, memory, cot, wq, wo, self_w, cache_w)


def finish_kernel(passed, gin, gmem, gwq, gwo, gself, gcache, *refs):
    outs, bufs, pair_a, pair_b, load, store = refs[:7], refs[7:14], refs[14], refs[15], refs[16], refs[17]
    sources = (passed, gin, gmem, gwq, gwo, gself, gcache)
    order = (5, 6, 0, 1, 2, 3, 4)
    loads = [pltpu.make_async_copy(a, b, load.at[k]) for k, (a, b) in enumerate(zip(sources, bufs))]
    last = bufs[:5] + (pair_a, pair_b)
    stores = [pltpu.make_async_copy(b, a, store.at[k]) for k, (a, b) in enumerate(zip(outs, last))]
    for k in order:
        loads[k].start()
    for k in order:
        loads[k].wait()
        if k >= 5:
            half = bufs[k].shape[1] // 2
            last[k][:, 0, :] = bufs[k][:, :half]
            last[k][:, 1, :] = bufs[k][:, half:]
        stores[k].start()
    for copy in stores:
        copy.wait()


def finish(results):
    shapes = [jax.ShapeDtypeStruct(x.shape, x.dtype) for x in results[:5]]
    for x in results[5:]:
        shapes.append(jax.ShapeDtypeStruct((x.shape[0], 2, x.shape[1] // 2), F32))
    return pl.pallas_call(
        finish_kernel,
        out_shape=tuple(shapes),
        in_specs=[ANY_SPEC] * 7,
        out_specs=[ANY_SPEC] * 7,
        scratch_shapes=[pltpu.VMEM(x.shape, x.dtype) for x in results]
        + [pltpu.VMEM(x.shape, x.dtype) for x in shapes[5:]]
        + [pltpu.SemaphoreType.DMA((7,)), pltpu.SemaphoreType.DMA((7,))],
        name="finish",
    )(*results)


def on_device(
    tp, seq, section, h_in, memory, cotangent, block_docs, w_query, w_out, self_weight, cache_weight
):
    results = whole_step(
        tp, seq, section, block_docs, h_in[0], memory[0], cotangent[0], w_query[0], w_out[0], self_weight, cache_weight
    )
    passed, gin, gmem, gwq, gwo, gself, gcache = finish(results)
    return (passed[None], gin[None], gmem[None], gwq[None], gwo.T[None], gself, gcache)


def solution(mesh):
    sizes = mesh.shape
    return jax.shard_map(
        functools.partial(on_device, sizes["tp"], sizes["seq"], sizes["section"]),
        mesh=mesh,
        in_specs=(
            P("section", "seq", "tp"),
            P("section", "seq", "tp"),
            P("section", "seq", "tp"),
            P("section", "seq"),
            P("section", None, "tp"),
            P("section", "tp", None),
            P(None, None, "tp"),
            P(None, None, "tp"),
        ),
        out_specs=(
            P("section", "seq", "tp"),
            P("section", "seq", "tp"),
            P("section", "seq", "tp"),
            P("section", "seq", "tp"),
            P("section", "tp", "seq"),
            P(("seq", "section"), None, "tp"),
            P(("seq", "section"), None, "tp"),
        ),
        check_vma=False,
    )
```

```python
import functools
import math

import jax
import jax.numpy as jnp
from jax import lax
from jax.experimental import pallas as pl
from jax.experimental.pallas import tpu as pltpu
from jax.sharding import PartitionSpec as P

MESH = pl.DeviceIdType.MESH
HEAD_DIM = 128
BLK = 128
WIN = 1024
SCALE = 40.0
EPS = 1e-06
EXP2_SCALE = SCALE * math.log2(math.e)
F32 = jnp.float32
BF16 = jnp.bfloat16
DOC_ROWS = 16
VMEM_SPEC = pl.BlockSpec(memory_space=pltpu.VMEM)
ANY_SPEC = pl.BlockSpec(memory_space=pl.ANY)
SMEM_SPEC = pl.BlockSpec(memory_space=pltpu.SMEM)
VMEM_LIMIT = 60 * 1024 * 1024


def nt(left, right):
    return lax.dot_general(left, right, (((1,), (1,)), ((), ())), preferred_element_type=F32)


def nn(left, right):
    return lax.dot_general(left, right, (((1,), (0,)), ((), ())), preferred_element_type=F32)


def tn(left, right):
    return lax.dot_general(left, right, (((0,), (0,)), ((), ())), preferred_element_type=F32)


def remote(src, dst, send_sem, recv_sem, device):
    return pltpu.make_async_remote_copy(
        src_ref=src,
        dst_ref=dst,
        send_sem=send_sem,
        recv_sem=recv_sem,
        device_id=device,
        device_id_type=MESH,
    )


def greet(devices):
    barrier = pltpu.get_barrier_semaphore()
    for device in devices:
        pl.semaphore_signal(barrier, inc=1, device_id=device, device_id_type=MESH)
    pl.semaphore_wait(barrier, len(devices))


def run_together(*streams):
    live = list(streams)
    while live:
        for stream in list(live):
            try:
                next(stream)
            except StopIteration:
                live.remove(stream)


class Ring:
    def __init__(self, axis, count):
        self.axis = axis
        self.me = lax.axis_index(axis)
        self.count = count

    def at(self, step):
        return lax.rem(self.me + step + self.count, self.count)

    def device(self, step):
        return {self.axis: self.at(step)}


class Line:
    def __init__(self, count):
        self.me = lax.axis_index("seq")
        self.chips = count // 2
        self.chip = self.me // 2
        self.core = self.me - self.chip * 2
        self.other = 1 - self.core

    def chip_at(self, step):
        return lax.rem(self.chip + step + self.chips, self.chips)

    def index(self, step):
        return self.chip_at(step) * 2 + self.core

    def device(self, step):
        return {"seq": self.index(step)}

    def partner(self):
        return {"seq": self.chip * 2 + self.other}


def gather_four(ring, full, send, recv):
    rows = full.shape[0]
    width = full.shape[1] // ring.count
    lo, hi = pl.ds(0, rows // 2), pl.ds(rows // 2, rows // 2)

    def block(half, step):
        return full.at[half, pl.ds(pl.multiple_of(ring.at(step) * width, 128), width)]

    def move(piece, slot, step):
        copy = remote(piece, piece, send.at[slot], recv.at[slot], ring.device(step))
        copy.start()
        return copy

    right_lo, left_hi = move(block(lo, 0), 0, 1), move(block(hi, 0), 1, -1)
    right_hi, left_lo = move(block(hi, 0), 2, 1), move(block(lo, 0), 3, -1)
    yield
    right_lo.wait_recv()
    relay_right = move(block(lo, -1), 4, 1)
    left_hi.wait_recv()
    relay_left = move(block(hi, 1), 5, -1)
    yield
    for copy in (right_hi, left_lo, relay_right, relay_left):
        copy.wait_recv()
    yield
    for copy in (right_lo, left_hi, right_hi, left_lo, relay_right, relay_left):
        copy.wait_send()


def gather_line(line, full, send, recv, to_core, from_core):
    rows = full.shape[1]
    cut = (rows // 2 + 15) // 16 * 16
    halves = {1: pl.ds(0, cut), -1: pl.ds(cut, rows - cut)}
    copies, hops, passed = [], {}, []

    def move(piece, s, r, device):
        copy = remote(piece, piece, s, r, device)
        copy.start()
        copies.append(copy)
        return copy

    last = line.chips // 2
    own = full.at[line.me]
    for way, d in ((0, 1), (1, -1)):
        hops[way] = move(own, send.at[way, 0], recv.at[way, 0], line.device(d))
    passed.append(move(own, to_core.at[0], from_core.at[0], line.partner()))
    yield
    slot = 1
    for hop in range(1, last + 1):
        earlier, passed = passed, []
        for way, d in ((0, 1), (1, -1)):
            hops[way].wait_recv()
            block = line.index(-d * hop)
            piece = full.at[block]
            if hop < last:
                ahead = piece if hop < last - 1 else full.at[block, halves[d], :]
                hops[way] = move(ahead, send.at[way, hop], recv.at[way, hop], line.device(d))
            else:
                piece = full.at[block, halves[d], :]
            passed.append(move(piece, to_core.at[slot], from_core.at[slot], line.partner()))
            slot += 1
        for copy in earlier:
            copy.wait_recv()
        yield
    for copy in passed:
        copy.wait_recv()
    yield
    for copy in copies:
        copy.wait_send()


def gather_line_scratch(chips):
    last = chips // 2
    return [
        pltpu.SemaphoreType.DMA((2, last)),
        pltpu.SemaphoreType.DMA((2, last)),
        pltpu.SemaphoreType.DMA((2 * last + 1,)),
        pltpu.SemaphoreType.DMA((2 * last + 1,)),
    ]


def scatter_four(ring, in_ref, buf, stage, send, recv, finish):
    rows = in_ref.shape[0]
    width = in_ref.shape[1] // ring.count
    lo, hi = pl.ds(0, rows // 2), pl.ds(rows // 2, rows // 2)

    def block(half, step):
        return in_ref.at[half, pl.ds(pl.multiple_of(ring.at(step) * width, 128), width)]

    def move(src, slot, step):
        copy = remote(src, buf.at[slot], send.at[slot], recv.at[slot], ring.device(step))
        copy.start()
        return copy

    copies = [
        move(block(lo, 2), 0, 1),
        move(block(hi, 2), 1, -1),
        move(block(hi, 1), 2, 1),
        move(block(lo, -1), 3, -1),
    ]
    yield
    copies[0].wait_recv()
    stage[0] = (buf[0].astype(F32) + block(lo, 1)[...].astype(F32)).astype(BF16)
    copies.append(move(stage.at[0], 4, 1))
    yield
    copies[1].wait_recv()
    stage[1] = (buf[1].astype(F32) + block(hi, -1)[...].astype(F32)).astype(BF16)
    copies.append(move(stage.at[1], 5, -1))
    yield
    copies[2].wait_recv()
    copies[5].wait_recv()
    finish(hi, block(hi, 0)[...].astype(F32) + buf[2].astype(F32) + buf[5].astype(F32))
    yield
    copies[3].wait_recv()
    copies[4].wait_recv()
    finish(lo, block(lo, 0)[...].astype(F32) + buf[3].astype(F32) + buf[4].astype(F32))
    yield
    for copy in copies:
        copy.wait_send()


def scatter_four_scratch(rows, width):
    return [
        pltpu.VMEM((6, rows // 2, width), BF16),
        pltpu.VMEM((2, rows // 2, width), BF16),
        pltpu.SemaphoreType.DMA((6,)),
        pltpu.SemaphoreType.DMA((6,)),
    ]


def scatter_line(line, in_ref, other, buf, stage, send, recv, to_core, from_core, finish, paced=None):
    rows = in_ref.shape[1]
    last = line.chips // 2
    halves = (pl.ds(0, rows // 2), pl.ds(rows // 2, rows // 2))
    groups = [[last]] + [[k, -k] for k in range(last - 1, 0, -1)] + [[0]]
    pieces, copies, ready, sent = {}, [], set(), {}

    def offer(group):
        for step in group:
            slot = len(pieces)
            chip = line.chip_at(step)
            copy = remote(
                in_ref.at[chip * 2 + line.other], other.at[chip], to_core.at[slot], from_core.at[slot], line.partner()
            )
            copy.start()
            copies.append(copy)
            pieces[step] = copy

    def own(step, half):
        if abs(step) == last:
            step = last
        if step not in ready:
            pieces[step].wait_recv()
            ready.add(step)
        chip = line.chip_at(step)
        return in_ref[chip * 2 + line.core, half, :].astype(F32) + other[chip, half, :].astype(F32)

    def ahead(k, which):
        for way, d in ((0, 1), (1, -1)):
            part = which if way == 0 else 1 - which
            half = halves[part]
            value = own(d * k, half)
            if (way, k + 1, part) in sent:
                sent[way, k + 1, part].wait_recv()
                value = value + buf[way, k, half, :].astype(F32)
            stage[way, k - 1, half, :] = value.astype(BF16)
            copy = remote(
                stage.at[way, k - 1, half, :],
                buf.at[way, k - 1, half, :],
                send.at[way, k - 1, part],
                recv.at[way, k - 1, part],
                line.device(d),
            )
            copy.start()
            sent[way, k, part] = copy
            copies.append(copy)
            yield

    plan = [[(last, 0)]] + [[(k, 1), (k, 0)] for k in range(last - 1, 0, -1)]
    if paced is not None:
        paced.extend(functools.partial(offer, group) for group in groups)
        yield
        for steps in plan:
            for step in steps:
                for _ in ahead(*step):
                    pass
                yield
    else:
        for group in groups:
            offer(group)
        yield
        for steps in plan:
            for step in steps:
                yield from ahead(*step)
    for part in (1, 0):
        half = halves[part]
        value = own(0, half)
        for way in (0, 1):
            sent[way, 1, part].wait_recv()
            value = value + buf[way, 0, half, :].astype(F32)
        finish(half, value)
        yield
    for copy in copies:
        copy.wait_send()


def scatter_line_scratch(chips, rows, width):
    last = chips // 2
    return [
        pltpu.VMEM((chips, rows, width), BF16),
        pltpu.VMEM((2, last, rows, width), BF16),
        pltpu.VMEM((2, last, rows, width), BF16),
        pltpu.SemaphoreType.DMA((2, last, 2)),
        pltpu.SemaphoreType.DMA((2, last, 2)),
        pltpu.SemaphoreType.DMA((chips,)),
        pltpu.SemaphoreType.DMA((chips,)),
    ]


def step_kernel(
    tp, seq, section,
    docs_ref, h_ref, mem_ref, cot_ref, wq_any, wo_any, self_any, cache_any,
    passed_out, gin_out, gmem_out, gwq_out, gwo_out, gself_out, gcache_out,
    passed_ref, gin_ref, gmem_ref, gwq_ref, gwo_ref, gself_ref, gcache_ref, store,
    kv_pair, full_h, full_s, full_c, wq, wo, kvw,
    q_raw, kv_raw, all_kv, q_unit, dout, weights, scores, delta_all, acc, dq, attn, gq, hout,
    proj, rows_part, source_part, dkv, part_q, part_o, part_kv, sums, mine, got,
    load, gather_send, gather_recv, pass_send, pass_recv, ex_send, ex_recv, ex_local,
    *scratch,
):
    line_gather, scratch = scratch[:4], scratch[4:]
    four = [scratch[4 * k : 4 * k + 4] for k in range(3)]
    scratch = scratch[12:]
    lines = [scratch[7 * k : 7 * k + 7] for k in range(4)]
    ring, line, sections = Ring("tp", tp), Line(seq), Ring("section", section)
    me = line.me
    is_self = sections.me == 0
    rows, width = h_ref.shape
    model = width * tp
    heads = wq.shape[1] // HEAD_DIM

    def cols(step):
        return pl.ds(pl.multiple_of(ring.at(step) * width, 128), width)

    own_h = pltpu.make_async_copy(h_ref, full_h.at[:, cols(0)], load.at[0])
    own_c = pltpu.make_async_copy(cot_ref, full_c.at[:, cols(0)], load.at[1])
    source_self = pltpu.make_async_copy(h_ref, full_s.at[:, cols(0)], load.at[2])
    source_cross = pltpu.make_async_copy(mem_ref, full_s.at[:, cols(0)], load.at[2])

    kvw_self = pltpu.make_async_copy(self_any, kv_pair, load.at[3])
    kvw_cross = pltpu.make_async_copy(cache_any, kv_pair, load.at[3])

    @pl.when(is_self)
    def _():
        source_self.start()
        kvw_self.start()

    @pl.when(jnp.logical_not(is_self))
    def _():
        source_cross.start()
        kvw_cross.start()

    own_h.start()
    own_c.start()
    load_wq = pltpu.make_async_copy(wq_any, wq, load.at[4])
    load_wo = pltpu.make_async_copy(wo_any, wo, load.at[5])
    load_wq.start()
    load_wo.start()
    greet(
        [ring.device(1), ring.device(-1), line.device(1), line.device(-1), line.partner()]
        + [sections.device(k) for k in range(1, section)]
    )
    gather_s, gather_h, gather_c = [
        gather_four(ring, full, gather_send.at[k], gather_recv.at[k])
        for k, full in enumerate((full_s, full_h, full_c))
    ]
    keys = gather_line(line, all_kv, *line_gather)
    blocks = [pl.ds(k * width, width) for k in range(tp)]

    def factor(full):
        total = jnp.zeros((rows, 128), F32)
        for span in blocks:
            wide = full[:, span].astype(F32)
            wide = wide * wide
            for first in range(0, width, 128):
                total += wide[:, first : first + 128]
        return lax.rsqrt(jnp.sum(total, axis=1, keepdims=True) / model + EPS)

    def head_rows(head):
        return pl.ds(head * rows, rows)

    def head_cols(head):
        return pl.ds(head * HEAD_DIM, HEAD_DIM)

    source_self.wait()
    next(gather_s)
    own_h.wait()
    own_c.wait()
    acc[...] = jnp.zeros_like(acc)
    dq[...] = jnp.zeros_like(dq)
    low_chip = jnp.where(is_self, jnp.maximum(line.chip - WIN // (2 * rows), 0), 0)
    zero_chunk = jnp.zeros((2 * rows, 2 * HEAD_DIM), BF16).reshape(2, rows, 2 * HEAD_DIM)

    @pl.loop(0, low_chip)
    def _(j):
        dkv[pl.ds(2 * j, 2)] = zero_chunk

    @pl.loop(line.chip + 1, line.chips)
    def _(j):
        dkv[pl.ds(2 * j, 2)] = zero_chunk

    kvw_self.wait()
    pairs = 256

    @pl.loop(0, model // pairs)
    def _(k):
        span = pl.ds(k * pairs, pairs)
        kvw[span, :] = kv_pair[span].reshape(pairs, kvw.shape[1])

    next(gather_s)
    next(gather_h)
    next(gather_s)
    rs = factor(full_s)
    kv = nn(full_s[:, blocks[0]], kvw[blocks[0], :])
    for span in blocks[1:]:
        kv += nn(full_s[:, span], kvw[span, :])
    kv = kv * rs
    kv_raw[...] = kv
    key, value = kv[:, :HEAD_DIM], kv[:, HEAD_DIM:]
    unit = key * lax.rsqrt(jnp.sum(key * key, axis=1, keepdims=True) + EPS)
    all_kv[me, 0:rows, 0:HEAD_DIM] = unit.astype(BF16)
    all_kv[me, 0:rows, HEAD_DIM:] = value.astype(BF16)
    doc_lane = lax.broadcasted_iota(jnp.int32, (DOC_ROWS, 2 * BLK), 1)
    docs = jnp.where(doc_lane < BLK, docs_ref[0, 0], docs_ref[0, 1])
    all_kv[me, rows:, :] = docs.astype(F32).astype(BF16)
    next(keys)
    next(gather_h)
    next(gather_c)
    load_wq.wait()
    next(keys)
    next(keys)
    next(gather_h)
    rh = factor(full_h)
    q = nn(full_h[:, blocks[0]], wq[blocks[0], :])
    for span in blocks[1:]:
        q += nn(full_h[:, span], wq[span, :])
    q_raw[...] = q * rh
    for head in range(heads):
        part = q_raw[:, head_cols(head)]
        unit = part * lax.rsqrt(jnp.sum(part * part, axis=1, keepdims=True) + EPS)
        q_unit[head_rows(head), :] = unit.astype(BF16)
    row = lax.broadcasted_iota(jnp.int32, (rows, 1), 0)
    lane = lax.broadcasted_iota(jnp.int32, (1, rows), 1)
    query_doc = jnp.where(row < BLK, docs_ref[0, 0], docs_ref[0, 1]).astype(F32)
    query_pos = me * rows + row
    upper = jnp.where(is_self, query_pos, query_pos // BLK * BLK + BLK - 1)
    lower = jnp.where(is_self, query_pos - WIN, -1)
    ones = jnp.ones((2 * rows, HEAD_DIM), BF16)

    def for_chips(hop, body):
        count = 1 if hop % (line.chips // 2) == 0 else 2

        @pl.loop(0, count)
        def _(turn):
            chip = line.chip_at(hop * (1 - 2 * turn))

            @pl.when((chip >= low_chip) & (chip <= line.chip))
            def _():
                body(chip)

    def forward(chip):
        sides = [2 * chip, 2 * chip + 1]
        value = jnp.concatenate([all_kv[j, 0:rows, HEAD_DIM:] for j in sides], axis=0)
        value = jnp.concatenate([value, ones], axis=1)
        seen = []
        for j in sides:
            key_doc = all_kv[j, rows:, :].astype(F32)[0:1, :]
            key_pos = j * rows + lane
            seen.append((key_doc == query_doc) & (key_pos <= upper) & (key_pos > lower))
        for head in range(heads):
            parts = []
            for side, j in enumerate(sides):
                score = nt(q_unit[head_rows(head), :], all_kv[j, 0:rows, 0:HEAD_DIM])
                weight = jnp.where(seen[side], jnp.exp2(score * EXP2_SCALE), 0.0).astype(BF16)
                weights[chip, head_rows(head), side * rows : (side + 1) * rows] = weight
                parts.append(weight)
            acc[head_rows(head), :] += nn(jnp.concatenate(parts, axis=1), value)

    next(keys)
    for_chips(0, forward)
    next(gather_c)
    for_chips(1, forward)
    for_chips(2, forward)
    next(keys)
    for_chips(3, forward)
    next(keys)
    for_chips(4, forward)
    for head in range(heads):
        total = acc[head_rows(head), :]
        attn[:, head_cols(head)] = (total[:, :HEAD_DIM] * (1.0 / total[:, HEAD_DIM:])).astype(BF16)
    load_wo.wait()
    attn_now = attn[...]
    for span in blocks:
        proj[:, span] = nn(attn_now, wo[:, span]).astype(BF16)

    def finish_rows(half, value):
        hout[half, :] = (full_h[half, cols(0)].astype(F32) + value).astype(BF16)

    def finish_input(half, value):
        gin_ref[half, :] = (full_c[half, cols(0)].astype(F32) + value).astype(BF16)

    def finish_memory(half, value):
        gmem_ref[half, :] = value.astype(BF16)

    def finish_keys(half, value):
        sums[half, :] = value

    def finish_wq(half, value):
        gwq_ref[half, :] = value

    def finish_wo(half, value):
        gwo_ref[half, :] = value

    def finish_kv(half, value):
        mine[half, :] = value

    red_hout = scatter_four(ring, proj, *four[0], finish_rows)
    next(red_hout)
    next(gather_c)
    grad = nt(full_c[:, blocks[0]], wo[:, blocks[0]])
    for span in blocks[1:]:
        grad += nt(full_c[:, span], wo[:, span])
    deltas = []
    for head in range(heads):
        inverse = 1.0 / acc[head_rows(head), HEAD_DIM:]
        part = grad[:, head * HEAD_DIM : (head + 1) * HEAD_DIM].astype(BF16).astype(F32)
        delta = jnp.sum(part * attn[:, head_cols(head)].astype(F32), axis=1, keepdims=True)
        dout[head_rows(head), :] = (part * inverse).astype(BF16)
        deltas.append(delta * inverse[:, 0:1])

    def advance(stream, times):
        for _ in range(times):
            next(stream, None)

    delta_all[...] = jnp.concatenate([jnp.broadcast_to(d, (rows, 128)) for d in deltas], axis=0)

    def backward(chip):
        sides = [2 * chip, 2 * chip + 1]
        key = jnp.concatenate([all_kv[j, 0:rows, 0:HEAD_DIM] for j in sides], axis=0)
        for head in range(heads):
            part = dout[head_rows(head), :]
            delta = delta_all[head_rows(head), 0:1]
            for side, j in enumerate(sides):
                span = pl.ds(side * rows, rows)
                grad_prob = nt(part, all_kv[j, 0:rows, HEAD_DIM:])
                weight = weights[chip, head_rows(head), span].astype(F32)
                scores[head_rows(head), span] = (weight * (grad_prob - delta)).astype(BF16)
        dq[...] += nn(scores[...], key)
        grad_key = (SCALE * tn(q_unit[...], scores[...])).T
        grad_value = tn(dout[...], weights[chip]).T
        for side, j in enumerate(sides):
            part = slice(side * rows, (side + 1) * rows)
            dkv[j, :, 0:HEAD_DIM] = grad_key[part].astype(BF16)
            dkv[j, :, HEAD_DIM:] = grad_value[part].astype(BF16)

    share = part_o.shape[1]
    per_block = width // share

    def weight_blocks(part, full, right, which):
        for k in which:
            value = tn(full[:, blocks[k]], right).astype(BF16)
            part[k * per_block : (k + 1) * per_block] = value.reshape(per_block, share, value.shape[1])

    offers = []
    red_keys = scatter_line(line, dkv, *lines[1], finish_keys, paced=offers)
    next(red_keys)
    red_wo = scatter_line(line, part_o, *lines[0], finish_wo)
    far = line.chips // 2
    for_chips(far, backward)
    offers[0]()
    for_chips(far - 1, backward)
    offers[1]()
    next(red_keys)
    for_chips(far - 2, backward)
    offers[2]()
    next(red_keys)
    advance(red_hout, 2)
    for_chips(far - 3, backward)
    offers[3]()
    next(red_keys)
    for_chips(0, backward)
    offers[4]()

    total = jnp.zeros((rows, 1), F32)
    scaled = []
    for head in range(heads):
        part = q_raw[:, head_cols(head)]
        slope = SCALE * dq[head_rows(head), :]
        inverse = lax.rsqrt(jnp.sum(part * part, axis=1, keepdims=True) + EPS)
        along = jnp.sum(part * slope, axis=1, keepdims=True)
        value = (inverse * slope - part * (inverse * inverse * inverse * along)).astype(BF16)
        gq[:, head_cols(head)] = value
        total += jnp.sum(value.astype(F32) * part, axis=1, keepdims=True)
        scaled.append((value.astype(F32) * rh).astype(BF16))
    scaled_q = jnp.concatenate(scaled, axis=1)
    next(red_keys)
    fix = rh * rh * total / model
    for span in blocks:
        value = nt(gq[...], wq[span, :]) * rh - full_h[:, span].astype(F32) * fix
        rows_part[:, span] = value.astype(BF16)
    red_rows = scatter_four(ring, rows_part, *four[1], finish_input)
    next(red_rows)
    next(red_keys)
    weight_blocks(part_o, full_c, attn[...], range(tp))
    next(red_wo)
    next(red_keys)
    next(red_keys)
    advance(red_hout, 2)
    pass_on = pass_along(sections, hout, passed_ref, pass_send, pass_recv)
    next(pass_on)
    weight_blocks(part_q, full_h, scaled_q, range(tp))
    advance(red_wo, 2)
    red_wq = scatter_line(line, part_q, *lines[2], finish_wq)
    next(red_wq)
    advance(red_keys, 2)
    summed = sums[...]
    kv = kv_raw[...]
    key, slope = kv[:, :HEAD_DIM], summed[:, :HEAD_DIM]
    inverse = lax.rsqrt(jnp.sum(key * key, axis=1, keepdims=True) + EPS)
    along = jnp.sum(key * slope, axis=1, keepdims=True)
    slope = inverse * slope - key * (inverse * inverse * inverse * along)
    both = jnp.concatenate([slope, summed[:, HEAD_DIM:]], axis=1).astype(BF16)
    total = jnp.sum(both.astype(F32) * kv, axis=1, keepdims=True)
    fix = rs * rs * total / model
    for span in blocks:
        value = nt(both, kvw[span, :]) * rs - full_s[:, span].astype(F32) * fix
        source_part[:, span] = value.astype(BF16)
    red_source = scatter_four(ring, source_part, *four[2], finish_memory)
    next(red_source)
    advance(red_wo, 4)
    advance(red_wq, 2)
    advance(red_rows, 2)
    scaled_kv = (both.astype(F32) * rs).astype(BF16)
    weight_blocks(part_kv, full_s, scaled_kv, range(tp))
    red_kv = scatter_line(line, part_kv, *lines[3], finish_kv)
    next(red_kv)
    advance(red_wo, 4)
    advance(red_kv, 2)
    advance(red_wq, 4)
    advance(red_kv, 4)
    advance(red_wo, 4)
    advance(red_source, 2)
    advance(red_kv, 4)
    advance(red_wq, 4)
    advance(red_kv, 4)
    advance(red_wq, 4)
    advance(red_kv, 2)
    local_refs = (passed_ref, gin_ref, gmem_ref, gwq_ref, gwo_ref, gself_ref, gcache_ref)
    outs = (passed_out, gin_out, gmem_out, gwq_out, gwo_out, gself_out, gcache_out)
    stores = [pltpu.make_async_copy(a, b, store.at[k]) for k, (a, b) in enumerate(zip(local_refs, outs))]
    piece = gself_ref.shape[0]
    copies = []
    for k in range(1, section):
        first = pl.multiple_of(sections.at(k) * piece, 8)
        copy = remote(
            mine.at[pl.ds(first, piece), :], got.at[sections.me], ex_send.at[k], ex_recv.at[k], sections.device(k)
        )
        copy.start()
        copies.append(copy)
    first = pl.multiple_of(sections.me * piece, 8)
    local = pltpu.make_async_copy(mine.at[pl.ds(first, piece), :], got.at[sections.me], ex_local)
    local.start()
    advance(red_wo, 2)
    stores[4].start()
    advance(red_rows, 2)
    stores[1].start()
    advance(red_wq, 2)
    stores[3].start()
    run_together(red_source, pass_on, red_rows, red_hout, gather_s, gather_h, gather_c, keys)
    stores[0].start()
    stores[2].start()
    run_together(red_keys, red_wo, red_wq, red_kv)
    for copy in copies:
        copy.wait_recv()
    local.wait()
    gself_ref[...] = got[0]
    total = got[1]
    for k in range(2, section):
        total = total + got[k]
    gcache_ref[...] = total
    stores[5].start()
    stores[6].start()
    for copy in copies:
        copy.wait_send()
    for copy in stores:
        copy.wait()


def pass_along(ring, in_ref, out_ref, send, recv):
    copy = remote(in_ref, out_ref, send, recv, ring.device(1))
    copy.start()
    yield
    copy.wait()


def whole_step(tp, seq, section, docs, hidden, memory, cot, wq, wo, self_w, cache_w):
    rows, width = hidden.shape
    model, cols = wq.shape
    heads = cols // HEAD_DIM
    kv = self_w.shape[1] * self_w.shape[2]
    chips = seq // 2
    share = model // seq
    piece = share // section
    vmem = pltpu.VMEM
    dma = pltpu.SemaphoreType.DMA
    outs = [((rows, width), BF16)] * 3 + [((share, cols), F32)] * 2 + [((piece, kv), F32)] * 2
    scratch = [vmem(*out) for out in outs] + [
        dma((7,)), vmem(self_w.shape, BF16),
        vmem((rows, model), BF16), vmem((rows, model), BF16), vmem((rows, model), BF16),
        vmem((model, cols), BF16), vmem((cols, model), BF16), vmem((model, kv), BF16),
        vmem((rows, cols), F32), vmem((rows, kv), F32),
        vmem((seq, rows + DOC_ROWS, kv), BF16),
        vmem((heads * rows, HEAD_DIM), BF16), vmem((heads * rows, HEAD_DIM), BF16),
        vmem((chips, heads * rows, 2 * rows), BF16),
        vmem((heads * rows, 2 * rows), BF16), vmem((heads * rows, 128), F32),
        vmem((heads * rows, 2 * HEAD_DIM), F32), vmem((heads * rows, HEAD_DIM), F32),
        vmem((rows, cols), BF16), vmem((rows, cols), BF16), vmem((rows, width), BF16),
        vmem((rows, model), BF16), vmem((rows, model), BF16), vmem((rows, model), BF16),
        vmem((seq, rows, kv), BF16),
        vmem((seq, share, cols), BF16), vmem((seq, share, cols), BF16), vmem((seq, share, kv), BF16),
        vmem((rows, kv), F32), vmem((share, kv), F32), vmem((section, piece, kv), F32),
        dma((6,)), dma((3, 6)), dma((3, 6)), dma, dma, dma((section,)), dma((section,)), dma,
    ]
    scratch += gather_line_scratch(chips)
    for _ in range(3):
        scratch += scatter_four_scratch(rows, width)
    for shape in ((share, cols), (rows, kv), (share, cols), (share, kv)):
        scratch += scatter_line_scratch(chips, *shape)
    return pl.pallas_call(
        functools.partial(step_kernel, tp, seq, section),
        out_shape=tuple(jax.ShapeDtypeStruct(*out) for out in outs),
        in_specs=[SMEM_SPEC] + [ANY_SPEC] * 7,
        out_specs=[ANY_SPEC] * 7,
        scratch_shapes=scratch,
        compiler_params=pltpu.CompilerParams(
            collective_id=1, has_side_effects=True, vmem_limit_bytes=VMEM_LIMIT
        ),
        name="step",
    )(docs, hidden, memory, cot, wq, wo, self_w, cache_w)


def finish_kernel(passed, gin, gmem, gwq, gwo, gself, gcache, *refs):
    outs, bufs, pair_a, pair_b, load, store = refs[:7], refs[7:14], refs[14], refs[15], refs[16], refs[17]
    sources = (passed, gin, gmem, gwq, gwo, gself, gcache)
    order = (5, 6, 0, 1, 2, 3, 4)
    loads = [pltpu.make_async_copy(a, b, load.at[k]) for k, (a, b) in enumerate(zip(sources, bufs))]
    last = bufs[:5] + (pair_a, pair_b)
    stores = [pltpu.make_async_copy(b, a, store.at[k]) for k, (a, b) in enumerate(zip(outs, last))]
    for k in order:
        loads[k].start()
    for k in order:
        loads[k].wait()
        if k >= 5:
            half = bufs[k].shape[1] // 2
            last[k][:, 0, :] = bufs[k][:, :half]
            last[k][:, 1, :] = bufs[k][:, half:]
        stores[k].start()
    for copy in stores:
        copy.wait()


def finish(results):
    shapes = [jax.ShapeDtypeStruct(x.shape, x.dtype) for x in results[:5]]
    for x in results[5:]:
        shapes.append(jax.ShapeDtypeStruct((x.shape[0], 2, x.shape[1] // 2), F32))
    return pl.pallas_call(
        finish_kernel,
        out_shape=tuple(shapes),
        in_specs=[ANY_SPEC] * 7,
        out_specs=[ANY_SPEC] * 7,
        scratch_shapes=[pltpu.VMEM(x.shape, x.dtype) for x in results]
        + [pltpu.VMEM(x.shape, x.dtype) for x in shapes[5:]]
        + [pltpu.SemaphoreType.DMA((7,)), pltpu.SemaphoreType.DMA((7,))],
        name="finish",
    )(*results)


def on_device(
    tp, seq, section, h_in, memory, cotangent, block_docs, w_query, w_out, self_weight, cache_weight
):
    results = whole_step(
        tp, seq, section, block_docs, h_in[0], memory[0], cotangent[0], w_query[0], w_out[0], self_weight, cache_weight
    )
    passed, gin, gmem, gwq, gwo, gself, gcache = finish(results)
    return (passed[None], gin[None], gmem[None], gwq[None], gwo.T[None], gself, gcache)


def solution(mesh):
    sizes = mesh.shape
    return jax.shard_map(
        functools.partial(on_device, sizes["tp"], sizes["seq"], sizes["section"]),
        mesh=mesh,
        in_specs=(
            P("section", "seq", "tp"),
            P("section", "seq", "tp"),
            P("section", "seq", "tp"),
            P("section", "seq"),
            P("section", None, "tp"),
            P("section", "tp", None),
            P(None, None, "tp"),
            P(None, None, "tp"),
        ),
        out_specs=(
            P("section", "seq", "tp"),
            P("section", "seq", "tp"),
            P("section", "seq", "tp"),
            P("section", "seq", "tp"),
            P("section", "tp", "seq"),
            P(("seq", "section"), None, "tp"),
            P(("seq", "section"), None, "tp"),
        ),
        check_vma=False,
    )
```
